128 devices in a mesh: row: 8 (over x, core), col: 16 (over z, y).
Axes of the slice: x: 4, y: 4, z: 4, core: 2. Of those that a mesh axis runs over, the one named last changes fastest.
Arguments:
- send_cells: int32 [128, 128, 512], P(('row', 'col')), may hold values from 0 to 65535, as said below
- send_species: int32 [128, 128, 512], P(('row', 'col')), may hold values from 0 to 5
- send_mix: bfloat16 [128, 6, 128, 512], P(('row', 'col')), may hold values from 0 to 0.5
- send_counts: int32 [128, 128], P(('row', 'col')), may hold values from 64 to 512, as said below
- chi: float32 [6, 6], replicated, may hold values from 0 to 8
Outputs:
- forces: float32 [128, 3, 128, 512], P(('row', 'col'))
The draws below stay inside these ranges and needn't reach their ends.
Inputs may be any that keep to these rules, and one draw needn't show every extreme that they name: `send_cells`: local cell (x * 16 + y) * 256 + z in the destination brick; domain s (flat index) holds particles with z from s * 2 to (s + 1) * 2 - 1 only. `send_counts`: slots at or beyond the count are unused. At most 512 particles go from one domain to one brick; in every draw some domain fills a slot list, and one brick receives 512 from every domain.
All inputs are finite; a program needn't handle non-finite values.
Results may differ from the reference program's by a relative error of at most 0.0023.
Values may be sent and summed in bfloat16 or wider, within the bound.
No kernel may reach another device: no remote copies, remote signals or barrier semaphores. Data moves between devices by JAX's collectives and lax.ppermute only.
A program may use at most 256 MiB of HBM per device.

```python
import jax
import jax.numpy as jnp
from jax import lax

SPECIES = 6
BX = 16
BY = 16
NZ = 256
SLOTS = 512
DOMAINS = 128
NX = 128
NY = 256
N_COL = 16


def draw_send_counts(key, part):
    key_heavy, key_light, key_full = jax.random.split(jax.random.fold_in(key, 11), 3)
    source = jnp.arange(DOMAINS, dtype=jnp.int32)[:, None]
    heavy = jnp.abs(2 * source - DOMAINS + 1) < DOMAINS // 2
    heavy_counts = jax.random.randint(key_heavy, (DOMAINS, DOMAINS), SLOTS // 2, SLOTS + 1)
    light_counts = jax.random.randint(key_light, (DOMAINS, DOMAINS), SLOTS // 8, SLOTS // 2 + 1)
    counts = jnp.where(heavy, heavy_counts, light_counts)
    full_brick = jax.random.randint(key_full, (), 0, DOMAINS)
    counts = jnp.where(jnp.arange(DOMAINS, dtype=jnp.int32)[None, :] == full_brick, SLOTS, counts)
    return counts.astype(jnp.int32)


def draw_send_cells(key, part):
    key_x, key_y, key_z = jax.random.split(jax.random.fold_in(key, 23), 3)
    shape = (DOMAINS, DOMAINS, SLOTS)
    cell_x = jax.random.randint(key_x, shape, 0, BX)
    cell_y = jax.random.randint(key_y, shape, 0, BY)
    offset = jax.random.randint(key_z, shape, 0, NZ // DOMAINS)
    source = jnp.arange(DOMAINS, dtype=jnp.int32)[:, None, None]
    cell_z = source * (NZ // DOMAINS) + offset
    return ((cell_x * BY + cell_y) * NZ + cell_z).astype(jnp.int32)


def set_ends(entries, stream_key, low, high):
    shape = entries.shape
    spot = [jax.random.randint(jax.random.fold_in(stream_key, axis), (), 0, shape[axis]) for axis in range(len(shape))]
    entries = entries.at[tuple(spot)].set(low)
    longest = shape.index(max(shape))
    spot[longest] = (spot[longest] + 1) % shape[longest]
    return entries.at[tuple(spot)].set(high)


def level_of(rng, extent, cuts, smallest, largest):
    factor_of, own = 1.0, jax.random.fold_in(rng, 6)
    for position, shards_of in cuts:
        heights = jnp.exp(jax.random.uniform(jax.random.fold_in(own, position), (shards_of,), jnp.float32, smallest / len(cuts), largest / len(cuts)))
        factor_of = factor_of * jnp.repeat(heights, extent[position] // shards_of).reshape([-1 if axis == position else 1 for axis in range(len(extent))])
    return factor_of


def setup_inputs(seed: int = 0) -> dict:
    key_of = jax.random.split(jax.random.key(seed), 6)
    return {
        "send_cells": draw_send_cells(jax.random.fold_in(key_of[5], 71), 0),
        "send_species": set_ends(jax.random.randint(key_of[1], (DOMAINS, DOMAINS, SLOTS), 0, SPECIES), jax.random.fold_in(key_of[1], 1), 0, SPECIES - 1).astype(jnp.int32),
        "send_mix": jnp.clip(0.5 * jax.random.uniform(key_of[2], (DOMAINS, SPECIES, DOMAINS, SLOTS), jnp.float32) ** level_of(key_of[2], (DOMAINS, SPECIES, DOMAINS, SLOTS), ((0, 128),), -0.2, 0.2), 0.0, 0.5).astype(jnp.bfloat16),
        "send_counts": draw_send_counts(jax.random.fold_in(key_of[5], 71), 0),
        "chi": jnp.clip(jax.random.uniform(key_of[4], (SPECIES, SPECIES), jnp.float32, 0.0, 8.0), 0.0, 8.0),
    }


raw_taps = (0.1353352832366127, 0.6065306597126334, 1.0, 0.6065306597126334, 0.1353352832366127)
tap_total = sum(raw_taps)
taps = tuple(t / tap_total for t in raw_taps)
rho_ref = 2.0
inv_kappa = 1.0


def smooth(padded):
    width_x = padded.shape[1] - 4
    width_y = padded.shape[2] - 4
    along_x = taps[0] * padded[:, 0:width_x]
    for t in range(1, 5):
        along_x = along_x + taps[t] * padded[:, t:t + width_x]
    along_y = taps[0] * along_x[:, :, 0:width_y]
    for t in range(1, 5):
        along_y = along_y + taps[t] * along_x[:, :, t:t + width_y]
    along_z = taps[0] * jnp.roll(along_y, 2, axis=3)
    for t in range(1, 5):
        along_z = along_z + taps[t] * jnp.roll(along_y, 2 - t, axis=3)
    return along_z


def potential_of(filtered, chi):
    count = chi.shape[0]
    chis = 0.5 * (chi + chi.T) * (1.0 - jnp.eye(count, dtype=jnp.float32))
    mixing = jnp.einsum("kl,lxyz->kxyz", chis, filtered, precision=lax.Precision.HIGHEST) / rho_ref
    total = jnp.sum(filtered, axis=0) / rho_ref
    return mixing + inv_kappa * (total[None] - 1.0)


def reference(send_cells, send_species, send_mix, send_counts, chi):
    slot_ids = jnp.arange(SLOTS, dtype=jnp.int32)
    valid = slot_ids[None, None, :] < send_counts[:, :, None]
    onehot = (send_species[:, None, :, :] == jnp.arange(SPECIES, dtype=jnp.int32)[None, :, None, None]).astype(jnp.float32)
    weights = jnp.where(valid[:, None], onehot + send_mix.astype(jnp.float32), 0.0).astype(jnp.bfloat16)
    dest = jnp.arange(DOMAINS, dtype=jnp.int32)[None, :, None]
    brick_r = dest // N_COL
    brick_q = dest % N_COL
    cell_x = send_cells // (BY * NZ)
    cell_y = (send_cells // NZ) % BY
    cell_z = send_cells % NZ
    place = ((brick_r * BX + cell_x) * NY + brick_q * BY + cell_y) * NZ + cell_z
    place = place.reshape(-1).astype(jnp.int32)
    flat_w = jnp.transpose(weights.astype(jnp.float32), (1, 0, 2, 3)).reshape(SPECIES, -1)
    density = jnp.zeros((SPECIES, NX * NY * NZ), jnp.float32).at[:, place].add(flat_w)
    density = density.reshape(SPECIES, NX, NY, NZ)
    padded = jnp.pad(density, ((0, 0), (2, 2), (2, 2), (0, 0)), mode="wrap")
    filtered = smooth(padded)
    potential = potential_of(filtered, chi)
    extended = jnp.pad(potential, ((0, 0), (1, 1), (1, 1), (0, 0)), mode="wrap")
    grad_x = 0.5 * (extended[:, 2:, 1:-1] - extended[:, :-2, 1:-1])
    grad_y = 0.5 * (extended[:, 1:-1, 2:] - extended[:, 1:-1, :-2])
    grad_z = 0.5 * (jnp.roll(potential, -1, axis=3) - jnp.roll(potential, 1, axis=3))
    results = []
    for grad in (grad_x, grad_y, grad_z):
        picked = grad.reshape(SPECIES, -1)[:, place]
        results.append((-jnp.sum(flat_w * picked, axis=0)).reshape(DOMAINS, DOMAINS, SLOTS))
    return jnp.stack(results, axis=1)
```

```python
import functools

import jax
import jax.numpy as jnp
from jax import lax
from jax.experimental import pallas as pl
from jax.experimental.pallas import tpu as pltpu
from jax.sharding import PartitionSpec as P

SPECIES = 6
ROWS = 8
COLS = 16
HALVES = 16
LANES = 128
SLOTS = 512

raw_taps = (0.1353352832366127, 0.6065306597126334, 1.0)
tap_total = raw_taps[2] + 2.0 * (raw_taps[0] + raw_taps[1])
T2, T1, T0 = (t / tap_total for t in raw_taps)

f32 = jnp.float32
bf16 = jnp.bfloat16


def onehot_of(plane_row):
    ids = lax.broadcasted_iota(jnp.int32, (256, SLOTS), 0)
    return jnp.where(ids == plane_row, 1.0, 0.0).astype(bf16)


def deposit_kernel(counts, mix_matrix, cells, species, mix, own, low, high, mixed, w_s, v_s, d_s):
    r = pl.program_id(0)
    rows = lax.broadcasted_iota(jnp.int32, (COLS, LANES), 0)
    limit = jnp.zeros((COLS, LANES), jnp.int32)
    for i in range(COLS):
        limit = jnp.where(rows == i, counts[r * COLS + i], limit)
    lane = lax.broadcasted_iota(jnp.int32, (COLS, LANES), 1)
    zero = jnp.zeros((COLS, LANES), f32)
    for t in range(4):
        part = pl.ds(t * LANES, LANES)
        valid = (lane + t * LANES) < limit
        kind = species[:, part]
        upper = (cells[:, part] & 1) == 1
        ws = []
        for k in range(SPECIES):
            w = jnp.where(kind == k, 1.0, 0.0) + mix[k, :, part].astype(f32)
            w = jnp.where(valid, w, 0.0).astype(bf16).astype(f32)
            ws.append(w)
            w_s[t, k * COLS:(k + 1) * COLS] = jnp.where(upper, 0.0, w)
            w_s[t, (8 + k) * COLS:(9 + k) * COLS] = jnp.where(upper, w, 0.0)
        for k in (6, 7):
            w_s[t, k * COLS:(k + 1) * COLS] = zero
            w_s[t, (8 + k) * COLS:(9 + k) * COLS] = zero
            v_s[t, k * COLS:(k + 1) * COLS] = zero
        for l in range(SPECIES):
            v = mix_matrix[l, 0] * ws[0]
            for k in range(1, SPECIES):
                v = v + mix_matrix[l, k] * ws[k]
            v_s[t, l * COLS:(l + 1) * COLS] = v

    def one_brick(b, carry):
        table = onehot_of(cells[pl.ds(b, 1), :] >> 8)
        w = jnp.concatenate([w_s[t, pl.ds(b, 16, stride=COLS)] for t in range(4)], axis=1)
        dens = lax.dot_general(
            w.astype(bf16), table, (((1,), (1,)), ((), ())), preferred_element_type=f32
        )
        d_s[0, pl.ds(b, 16, stride=COLS)] = dens[:, :LANES]
        d_s[1, pl.ds(b, 16, stride=COLS)] = dens[:, LANES:]
        for t in range(4):
            mixed[b, :, t * LANES:(t + 1) * LANES] = v_s[t, pl.ds(b, 8, stride=COLS)]
        return carry

    lax.fori_loop(0, COLS, one_brick, 0, unroll=2)
    for z in range(2):
        for k in range(SPECIES):
            for h in range(2):
                value = d_s[h, (z * 8 + k) * COLS:(z * 8 + k + 1) * COLS]
                own[z, k, h] = value
                (low, high)[z][k, h] = value.astype(bf16)


def deposit(counts, mix_matrix, cells, species, mix):
    plane = (SPECIES, HALVES, COLS, LANES)
    return pl.pallas_call(
        deposit_kernel,
        name="deposit",
        grid_spec=pltpu.PrefetchScalarGridSpec(
            num_scalar_prefetch=2,
            grid=(ROWS,),
            in_specs=[
                pl.BlockSpec((COLS, SLOTS), lambda r, *_: (r, 0)),
                pl.BlockSpec((COLS, SLOTS), lambda r, *_: (r, 0)),
                pl.BlockSpec((SPECIES, COLS, SLOTS), lambda r, *_: (0, r, 0)),
            ],
            out_specs=[
                pl.BlockSpec((2, SPECIES, 2, COLS, LANES), lambda r, *_: (0, 0, r, 0, 0)),
                pl.BlockSpec((SPECIES, 2, COLS, LANES), lambda r, *_: (0, r, 0, 0)),
                pl.BlockSpec((SPECIES, 2, COLS, LANES), lambda r, *_: (0, r, 0, 0)),
                pl.BlockSpec((COLS, 8, SLOTS), lambda r, *_: (r, 0, 0)),
            ],
            scratch_shapes=[
                pltpu.VMEM((4, 16 * COLS, LANES), f32),
                pltpu.VMEM((4, 8 * COLS, LANES), f32),
                pltpu.VMEM((2, 16 * COLS, LANES), f32),
            ],
        ),
        out_shape=[
            jax.ShapeDtypeStruct((2,) + plane, f32),
            jax.ShapeDtypeStruct(plane, bf16),
            jax.ShapeDtypeStruct(plane, bf16),
            jax.ShapeDtypeStruct((ROWS * COLS, 8, SLOTS), f32),
        ],
        compiler_params=pltpu.CompilerParams(dimension_semantics=("arbitrary",)),
    )(counts, mix_matrix, cells, species, mix)


def shift_y(v, step, col):
    a = pltpu.roll(v, (-step) % LANES, 1)
    if step > 0:
        b = pltpu.roll(pltpu.roll(v, COLS - 1, 0), 16 - step, 1)
        return jnp.where(col < 16 - step, a, b)
    b = pltpu.roll(pltpu.roll(v, 1, 0), (-16 - step) % LANES, 1)
    return jnp.where(col >= -step, a, b)


def shift_x(here, beyond, step, lane):
    amount = (-16 * step) % LANES
    a = pltpu.roll(here, amount, 1)
    b = pltpu.roll(beyond, amount, 1)
    if step > 0:
        return jnp.where(lane < LANES - 16 * step, a, b)
    return jnp.where(lane >= -16 * step, a, b)


def force_kernel(cells, own, far_low, near_low0, near_low1, near_high0, near_high1, far_high, mixed,
                 forces, y_s, s_s, g_s):
    lane = lax.broadcasted_iota(jnp.int32, (COLS, LANES), 1)
    col = lane & 15

    def one_species(k, carry):
        def along_zy(h, c):
            l2 = far_low[k, h].astype(f32)
            a = near_low0[k, h].astype(f32)
            b = near_low1[k, h].astype(f32)
            o0 = own[0, k, h]
            o1 = own[1, k, h]
            r0 = near_high0[k, h].astype(f32)
            r1 = near_high1[k, h].astype(f32)
            r2 = far_high[k, h].astype(f32)
            um = T2 * (l2 + o1) + T1 * (a + o0) + T0 * b
            u0 = T2 * (a + r0) + T1 * (b + o1) + T0 * o0
            u1 = T2 * (b + r1) + T1 * (o0 + r0) + T0 * o1
            up = T2 * (o0 + r2) + T1 * (o1 + r1) + T0 * r0
            for i, v in enumerate((u0, u1, 0.5 * (u1 - um), 0.5 * (up - u0))):
                y_s[i, h] = (
                    T2 * (shift_y(v, -2, col) + shift_y(v, 2, col))
                    + T1 * (shift_y(v, -1, col) + shift_y(v, 1, col))
                    + T0 * v
                )
            return c

        lax.fori_loop(0, HALVES, along_zy, 0)

        def along_x(h, c):
            before = lax.rem(h + HALVES - 1, HALVES)
            after = lax.rem(h + 1, HALVES)
            for i in range(4):
                m, v, n = y_s[i, before], y_s[i, h], y_s[i, after]
                out = (
                    T2 * (shift_x(v, m, -2, lane) + shift_x(v, n, 2, lane))
                    + T1 * (shift_x(v, m, -1, lane) + shift_x(v, n, 1, lane))
                    + T0 * v
                )
                if i < 2:
                    s_s[i, h] = out
                    gy = 0.5 * (shift_y(out, 1, col) - shift_y(out, -1, col))
                    g_s[h, pl.ds(pl.multiple_of(((2 + i) * 8 + k) * COLS, COLS), COLS)] = gy
                else:
                    g_s[h, pl.ds(pl.multiple_of(((2 + i) * 8 + k) * COLS, COLS), COLS)] = out
            return c

        lax.fori_loop(0, HALVES, along_x, 0)

        def slope_x(h, c):
            before = lax.rem(h + HALVES - 1, HALVES)
            after = lax.rem(h + 1, HALVES)
            for i in range(2):
                m, v, n = s_s[i, before], s_s[i, h], s_s[i, after]
                gx = 0.5 * (shift_x(v, n, 1, lane) - shift_x(v, m, -1, lane))
                g_s[h, pl.ds(pl.multiple_of((i * 8 + k) * COLS, COLS), COLS)] = gx
            return c

        lax.fori_loop(0, HALVES, slope_x, 0)
        return carry

    lax.fori_loop(0, SPECIES, one_species, 0)
    zero = jnp.zeros((COLS, LANES), f32)
    for h in range(HALVES):
        for j in range(6):
            for k in (6, 7):
                g_s[h, (j * 8 + k) * COLS:(j * 8 + k + 1) * COLS] = zero

    def one_brick(d, carry):
        r = lax.div(d, COLS)
        q = lax.rem(d, COLS)
        row = cells[pl.ds(d, 1), :]
        table = onehot_of(row >> 8)
        g = jnp.concatenate(
            [g_s[2 * r + h, pl.ds(q, 48, stride=COLS)] for h in range(2)], axis=1
        )
        top = g.astype(bf16)
        rest = (g - top.astype(f32)).astype(bf16)
        got = jnp.dot(jnp.concatenate([top, rest], axis=0), table, preferred_element_type=f32)
        got = got[:48] + got[48:]
        upper = (row & 1) == 1
        v = mixed[d]
        for a in range(3):
            value = jnp.where(upper, got[(2 * a + 1) * 8:(2 * a + 2) * 8], got[2 * a * 8:(2 * a + 1) * 8])
            forces[a, pl.ds(d, 1), :] = jnp.sum(value * v, axis=0, keepdims=True)
        return carry

    lax.fori_loop(0, ROWS * COLS, one_brick, 0, unroll=2)


def pick(*args):
    return pl.pallas_call(
        force_kernel,
        name="force",
        out_shape=jax.ShapeDtypeStruct((3, ROWS * COLS, SLOTS), f32),
        in_specs=[pl.BlockSpec(memory_space=pltpu.VMEM)] * len(args),
        out_specs=pl.BlockSpec(memory_space=pltpu.VMEM),
        scratch_shapes=[
            pltpu.VMEM((4, HALVES, COLS, LANES), f32),
            pltpu.VMEM((2, HALVES, COLS, LANES), f32),
            pltpu.VMEM((HALVES, 48 * COLS, LANES), f32),
        ],
    )(*args)


def body(send_cells, send_species, send_mix, send_counts, chi):
    axes = ("row", "col")
    count = lax.axis_size("row") * lax.axis_size("col")
    up = [(i, (i + 1) % count) for i in range(count)]
    down = [(j, i) for i, j in up]
    chis = 0.5 * (chi + chi.T) * (1.0 - jnp.eye(SPECIES, dtype=f32))
    mix_matrix = -0.5 * (chis + 1.0)
    cells = send_cells[0]
    own, low, high, mixed = deposit(send_counts[0], mix_matrix, cells, send_species[0], send_mix[0])
    near_low1 = lax.ppermute(high, axes, up)
    near_high0 = lax.ppermute(low, axes, down)
    near_low0 = lax.ppermute(low, axes, up)
    near_high1 = lax.ppermute(high, axes, down)
    far_low = lax.ppermute(near_low1, axes, up)
    far_high = lax.ppermute(near_high0, axes, down)
    forces = pick(cells, own, far_low, near_low0, near_low1, near_high0, near_high1, far_high, mixed)
    return forces[None]


def solution(mesh):
    return jax.shard_map(
        body,
        mesh=mesh,
        in_specs=(
            P(("row", "col"), None, None),
            P(("row", "col"), None, None),
            P(("row", "col"), None, None, None),
            P(("row", "col"), None),
            P(),
        ),
        out_specs=P(("row", "col"), None, None, None),
        check_vma=False,
    )
```

```python
import jax
import jax.numpy as jnp
import numpy as np
from jax import lax
from jax.experimental import pallas as pl
from jax.experimental.pallas import tpu as pltpu
from jax.sharding import PartitionSpec as P

SPECIES = 6
ROWS = 8
COLS = 16
HALVES = 16
LANES = 128
SLOTS = 512

raw_taps = (0.1353352832366127, 0.6065306597126334, 1.0)
tap_total = raw_taps[2] + 2.0 * (raw_taps[0] + raw_taps[1])
T2, T1, T0 = (t / tap_total for t in raw_taps)

f32 = jnp.float32
bf16 = jnp.bfloat16


def onehot_of(plane_row):
    ids = lax.broadcasted_iota(jnp.int32, (16, SLOTS), 0)
    inner = jnp.where((plane_row & 15) == ids, 1.0, 0.0).astype(bf16)
    outer = (plane_row >> 4).astype(f32).astype(bf16)
    none = jnp.zeros((16, SLOTS), bf16)
    return jnp.concatenate(
        [jnp.where(outer == jnp.full((16, SLOTS), i, bf16), inner, none) for i in range(16)], axis=0
    )


def weights_of(limit, t, cells, species, mix):
    part = pl.ds(t * LANES, LANES)
    lane = lax.broadcasted_iota(jnp.int32, (COLS, LANES), 1)
    valid = (lane + t * LANES) < limit
    kind = species[:, part]
    found = []
    for k in range(SPECIES):
        w = jnp.where(kind == k, 1.0, 0.0) + mix[k, :, part].astype(f32)
        found.append(jnp.where(valid, w, 0.0).astype(bf16).astype(f32))
    return found


def limits_of(counts, first):
    rows = lax.broadcasted_iota(jnp.int32, (COLS, LANES), 0)
    limit = jnp.zeros((COLS, LANES), jnp.int32)
    for i in range(COLS):
        limit = jnp.where(rows == i, counts[first + i], limit)
    return limit


def deposit_kernel(counts, cells, species, mix, own, low, high, w_s, d_s):
    r = pl.program_id(0)
    limit = limits_of(counts, r * COLS)
    zero = jnp.zeros((COLS, LANES), f32)
    for t in range(4):
        upper = (cells[:, pl.ds(t * LANES, LANES)] & 1) == 1
        for k, w in enumerate(weights_of(limit, t, cells, species, mix)):
            w_s[t, k * COLS:(k + 1) * COLS] = jnp.where(upper, 0.0, w)
            w_s[t, (8 + k) * COLS:(9 + k) * COLS] = jnp.where(upper, w, 0.0)
        for k in (6, 7):
            w_s[t, k * COLS:(k + 1) * COLS] = zero
            w_s[t, (8 + k) * COLS:(9 + k) * COLS] = zero

    for b in range(COLS):
        table = onehot_of(jnp.broadcast_to(cells[b:b + 1, :] >> 8, (16, SLOTS)))
        w = jnp.concatenate([w_s[t, pl.ds(b, 16, stride=COLS)] for t in range(4)], axis=1)
        dens = lax.dot_general(
            w.astype(bf16), table, (((1,), (1,)), ((), ())), preferred_element_type=f32
        )
        d_s[0, pl.ds(b, 16, stride=COLS)] = dens[:, :LANES]
        d_s[1, pl.ds(b, 16, stride=COLS)] = dens[:, LANES:]

    for z in range(2):
        for k in range(SPECIES):
            for h in range(2):
                value = d_s[h, (z * 8 + k) * COLS:(z * 8 + k + 1) * COLS]
                own[z, k, h] = value
                (low, high)[z][k, h] = value.astype(bf16)


def deposit(counts, cells, species, mix):
    plane = (SPECIES, HALVES, COLS, LANES)
    return pl.pallas_call(
        deposit_kernel,
        name="deposit",
        grid_spec=pltpu.PrefetchScalarGridSpec(
            num_scalar_prefetch=1,
            grid=(ROWS,),
            in_specs=[
                pl.BlockSpec((COLS, SLOTS), lambda r, *_: (r, 0)),
                pl.BlockSpec((COLS, SLOTS), lambda r, *_: (r, 0)),
                pl.BlockSpec((SPECIES, COLS, SLOTS), lambda r, *_: (0, r, 0)),
            ],
            out_specs=[
                pl.BlockSpec((2, SPECIES, 2, COLS, LANES), lambda r, *_: (0, 0, r, 0, 0)),
                pl.BlockSpec((SPECIES, 2, COLS, LANES), lambda r, *_: (0, r, 0, 0)),
                pl.BlockSpec((SPECIES, 2, COLS, LANES), lambda r, *_: (0, r, 0, 0)),
            ],
            scratch_shapes=[
                pltpu.VMEM((4, 16 * COLS, LANES), f32),
                pltpu.VMEM((2, 16 * COLS, LANES), f32),
            ],
        ),
        out_shape=[
            jax.ShapeDtypeStruct((2,) + plane, f32),
            jax.ShapeDtypeStruct(plane, bf16),
            jax.ShapeDtypeStruct(plane, bf16),
        ],
        cost_estimate=pl.CostEstimate(flops=4 * 10**9, bytes_accessed=5 * 10**6, transcendentals=0),
    )(counts, cells, species, mix)


def mixing_kernel(counts, mix_matrix, cells, species, mix, mixed, v_s):
    r = pl.program_id(0)
    limit = limits_of(counts, r * COLS)
    zero = jnp.zeros((COLS, LANES), f32)
    for t in range(4):
        ws = weights_of(limit, t, cells, species, mix)
        for l in range(SPECIES):
            v = mix_matrix[l, 0] * ws[0]
            for k in range(1, SPECIES):
                v = v + mix_matrix[l, k] * ws[k]
            v_s[t, l * COLS:(l + 1) * COLS] = v
        for k in (6, 7):
            v_s[t, k * COLS:(k + 1) * COLS] = zero
    for b in range(COLS):
        for t in range(4):
            mixed[b, :, t * LANES:(t + 1) * LANES] = v_s[t, pl.ds(b, 8, stride=COLS)]


def mixing(counts, mix_matrix, cells, species, mix):
    return pl.pallas_call(
        mixing_kernel,
        name="mixing",
        grid_spec=pltpu.PrefetchScalarGridSpec(
            num_scalar_prefetch=2,
            grid=(ROWS,),
            in_specs=[
                pl.BlockSpec((COLS, SLOTS), lambda r, *_: (r, 0)),
                pl.BlockSpec((COLS, SLOTS), lambda r, *_: (r, 0)),
                pl.BlockSpec((SPECIES, COLS, SLOTS), lambda r, *_: (0, r, 0)),
            ],
            out_specs=pl.BlockSpec((COLS, 8, SLOTS), lambda r, *_: (r, 0, 0)),
            scratch_shapes=[pltpu.VMEM((4, 8 * COLS, LANES), f32)],
        ),
        out_shape=jax.ShapeDtypeStruct((ROWS * COLS, 8, SLOTS), f32),
        cost_estimate=pl.CostEstimate(flops=10**9, bytes_accessed=4 * 10**6, transcendentals=0),
    )(counts, mix_matrix, cells, species, mix)


def scaled_taps():
    smooth_scale, slope_scale = 1.6396387, 1.5596421
    smooth_taps = {0: T0, 1: T1, -1: T1, 2: T2, -2: T2}
    slope_taps = {1: 0.5 * (T0 - T2), 2: 0.5 * T1, 3: 0.5 * T2}
    slope_taps.update({-j: -v for j, v in slope_taps.items()})
    return (
        {j: smooth_scale * v for j, v in smooth_taps.items()},
        {j: slope_scale * v for j, v in slope_taps.items()},
        smooth_scale,
        slope_scale,
    )


SMOOTH, SLOPE, SMOOTH_SCALE, SLOPE_SCALE = scaled_taps()


def tap_matrices():
    lane = np.arange(LANES)
    x, y = lane // 16, lane % 16
    results = []
    for main, other, extent in ((y, x, 16), (x, y, 8)):
        source = np.concatenate([main, np.where(main < extent // 2, main + extent, main - extent)])
        same = np.concatenate([other, other])[:, None] == other[None, :]
        gap = source[:, None] - main[None, :]
        for taps in (SMOOTH, SLOPE):
            matrix = np.zeros((2 * LANES, LANES), np.float32)
            for j, value in taps.items():
                matrix += np.where(same & (gap == j), np.float32(value), np.float32(0))
            results.append(matrix)
    return jnp.asarray(np.concatenate(results, axis=1)).astype(bf16)


def split(v):
    top = v.astype(bf16)
    return top, (v - top.astype(f32)).astype(bf16)


def force_kernel(cells, taps, own, far_low, near_low0, near_low1, near_high0, near_high1, far_high, mixed_far,
                 forces, x_s, y_s, w_s, g_s, mixed, sem):
    k = pl.program_id(0)
    lane = lax.broadcasted_iota(jnp.int32, (COLS, LANES), 1)
    col = lane & 15
    fetch = pltpu.make_async_copy(mixed_far, mixed, sem)

    @pl.when(k == 0)
    def _():
        fetch.start()
        zero = jnp.zeros((HALVES, COLS, LANES), f32)
        for j in range(6):
            for i in (6, 7):
                g_s[:, (j * 8 + i) * COLS:(j * 8 + i + 1) * COLS] = zero

    cu = 1.0 / (SMOOTH_SCALE * SLOPE_SCALE)
    cz = 0.5 / (SMOOTH_SCALE * SMOOTH_SCALE)
    for h in range(HALVES):
        l2 = far_low[0, h].astype(f32)
        a = near_low0[0, h].astype(f32)
        b = near_low1[0, h].astype(f32)
        o0 = own[0, 0, h]
        o1 = own[1, 0, h]
        r0 = near_high0[0, h].astype(f32)
        r1 = near_high1[0, h].astype(f32)
        r2 = far_high[0, h].astype(f32)
        um = T2 * (l2 + o1) + T1 * (a + o0) + T0 * b
        u0 = T2 * (a + r0) + T1 * (b + o1) + T0 * o0
        u1 = T2 * (b + r1) + T1 * (o0 + r0) + T0 * o1
        up = T2 * (o0 + r2) + T1 * (o1 + r1) + T0 * r0
        for i, v in enumerate((cu * u0, cu * u1, cz * (u1 - um), cz * (up - u0))):
            around = jnp.where(col < 8, pltpu.roll(v, COLS - 1, 0), pltpu.roll(v, 1, 0))
            for part, value in ((0, v), (1, around)):
                for level, piece in enumerate(split(value)):
                    x_s[level, i, h * COLS:(h + 1) * COLS, part * LANES:(part + 1) * LANES] = piece
    for i in range(4):
        width = 2 * LANES if i < 2 else LANES
        table = taps[:, :width]
        out = jnp.dot(x_s[0, i], table, preferred_element_type=f32) + jnp.dot(
            x_s[1, i], table, preferred_element_type=f32
        )
        if i < 2:
            y_s[i] = out[:, :LANES]
            y_s[2 + i] = out[:, LANES:]
        else:
            y_s[2 + i] = out
    for p in range(6):
        for h in range(HALVES):
            before = (h + HALVES - 1) % HALVES
            after = (h + 1) % HALVES
            v = y_s[p, h * COLS:(h + 1) * COLS]
            around = jnp.where(
                lane < 64,
                y_s[p, after * COLS:(after + 1) * COLS],
                y_s[p, before * COLS:(before + 1) * COLS],
            )
            for part, value in ((0, v), (1, around)):
                for level, piece in enumerate(split(value)):
                    w_s[level, p, h * COLS:(h + 1) * COLS, part * LANES:(part + 1) * LANES] = piece
        table = taps[:, 3 * LANES:] if p < 2 else taps[:, 2 * LANES:3 * LANES]
        out = jnp.dot(w_s[0, p], table, preferred_element_type=f32) + jnp.dot(
            w_s[1, p], table, preferred_element_type=f32
        )
        for h in range(HALVES):
            g_s[h, pl.ds(pl.multiple_of((p * 8 + k) * COLS, COLS), COLS)] = out[h * COLS:(h + 1) * COLS]

    def one_brick(d):
        r = lax.div(d, COLS)
        q = lax.rem(d, COLS)
        row = cells[pl.ds(d, 1), :]
        table = onehot_of(jnp.broadcast_to(row >> 8, (16, SLOTS)))
        g = jnp.concatenate(
            [g_s[2 * r + h, pl.ds(q, 48, stride=COLS)] for h in range(2)], axis=1
        )
        got = jnp.dot(jnp.concatenate(split(g), axis=0), table, preferred_element_type=f32)
        got = got[:48] + got[48:]
        upper = (row & 1) == 1
        v = mixed[d]
        for a in range(3):
            value = jnp.where(upper, got[(2 * a + 1) * 8:(2 * a + 2) * 8], got[2 * a * 8:(2 * a + 1) * 8])
            forces[a, pl.ds(d, 1), :] = jnp.sum(value * v, axis=0, keepdims=True)

    @pl.when(k == SPECIES - 1)
    def _():
        fetch.wait()

        def some_bricks(i, carry):
            for j in range(8):
                one_brick(i * 8 + j)
            return carry

        lax.fori_loop(0, ROWS * COLS // 8, some_bricks, 0)


def pick(cells, taps, own, *others):
    plane = pl.BlockSpec((1, HALVES, COLS, LANES), lambda k: (k, 0, 0, 0))
    return pl.pallas_call(
        force_kernel,
        name="force",
        grid=(SPECIES,),
        out_shape=jax.ShapeDtypeStruct((3, ROWS * COLS, SLOTS), f32),
        in_specs=[
            pl.BlockSpec((ROWS * COLS, SLOTS), lambda k: (0, 0)),
            pl.BlockSpec((2 * LANES, 4 * LANES), lambda k: (0, 0)),
            pl.BlockSpec((2, 1, HALVES, COLS, LANES), lambda k: (0, k, 0, 0, 0)),
        ]
        + [plane] * 6
        + [pl.BlockSpec(memory_space=pl.ANY)],
        out_specs=pl.BlockSpec((3, ROWS * COLS, SLOTS), lambda k: (0, 0, 0)),
        scratch_shapes=[
            pltpu.VMEM((2, 4, HALVES * COLS, 2 * LANES), bf16),
            pltpu.VMEM((6, HALVES * COLS, LANES), f32),
            pltpu.VMEM((2, 6, HALVES * COLS, 2 * LANES), bf16),
            pltpu.VMEM((HALVES, 48 * COLS, LANES), f32),
            pltpu.VMEM((ROWS * COLS, 8, SLOTS), f32),
            pltpu.SemaphoreType.DMA,
        ],
    )(cells, taps, own, *others)


def body(send_cells, send_species, send_mix, send_counts, chi):
    axes = ("row", "col")
    count = lax.axis_size("row") * lax.axis_size("col")
    up = [(i, (i + 1) % count) for i in range(count)]
    down = [(j, i) for i, j in up]
    chis = 0.5 * (chi + chi.T) * (1.0 - jnp.eye(SPECIES, dtype=f32))
    mix_matrix = -0.5 * (chis + 1.0)
    cells, species, mix, counts = send_cells[0], send_species[0], send_mix[0], send_counts[0]
    own, low, high = deposit(counts, cells, species, mix)
    near_low1 = lax.ppermute(high, axes, up)
    near_high0 = lax.ppermute(low, axes, down)
    near_low0 = lax.ppermute(low, axes, up)
    near_high1 = lax.ppermute(high, axes, down)
    far_low = lax.ppermute(near_low1, axes, up)
    far_high = lax.ppermute(near_high0, axes, down)
    mixed = mixing(counts, mix_matrix, cells, species, mix)
    forces = pick(
        cells, tap_matrices(), own, far_low, near_low0, near_low1, near_high0, near_high1, far_high, mixed
    )
    return forces[None]


def solution(mesh):
    return jax.shard_map(
        body,
        mesh=mesh,
        in_specs=(
            P(("row", "col"), None, None),
            P(("row", "col"), None, None),
            P(("row", "col"), None, None, None),
            P(("row", "col"), None),
            P(),
        ),
        out_specs=P(("row", "col"), None, None, None),
        check_vma=False,
    )
```

```python
import jax
import jax.numpy as jnp
import numpy as np
from jax import lax
from jax.experimental import pallas as pl
from jax.experimental.pallas import tpu as pltpu
from jax.sharding import PartitionSpec as P

SPECIES = 6
ROWS = 8
COLS = 16
HALVES = 16
LANES = 128
SLOTS = 512
CHUNKS = 3
PER = SPECIES // CHUNKS
GROUP = 8
MIB = 1 << 20

raw_taps = (0.1353352832366127, 0.6065306597126334, 1.0)
tap_total = raw_taps[2] + 2.0 * (raw_taps[0] + raw_taps[1])
T2, T1, T0 = (t / tap_total for t in raw_taps)

f32 = jnp.float32
bf16 = jnp.bfloat16


def onehot_of(row, count):
    wide = jnp.broadcast_to(row, (16, SLOTS))
    ids = lax.broadcasted_iota(jnp.int32, (16, SLOTS), 0)
    inner = jnp.where((wide & 15) == ids, 1.0, 0.0).astype(bf16)
    outer = (wide >> 4).astype(f32).astype(bf16)
    none = jnp.zeros((16, SLOTS), bf16)
    return jnp.concatenate(
        [jnp.where(outer == jnp.full((16, SLOTS), i, bf16), inner, none) for i in range(count)], axis=0
    )


def weights_of(limit, t, rows, species, mix):
    part = pl.ds(t * LANES, LANES)
    lane = lax.broadcasted_iota(jnp.int32, (COLS, LANES), 1)
    valid = (lane + t * LANES) < limit
    kind = species[rows, part]
    found = []
    for k in range(SPECIES):
        w = jnp.where(kind == k, 1.0, 0.0) + mix[k, rows, part].astype(f32)
        found.append(jnp.where(valid, w, 0.0).astype(bf16).astype(f32))
    return found


def limits_of(counts, first):
    rows = lax.broadcasted_iota(jnp.int32, (COLS, LANES), 0)
    limit = jnp.zeros((COLS, LANES), jnp.int32)
    for i in range(COLS):
        limit = jnp.where(rows == i, counts[first + i], limit)
    return limit


def deposit_kernel(counts, cells_far, species_far, mix_far, own, sent0, sent1, sent2,
                   cells, species, mix, w_s, d_s, sems):
    sent = (sent0, sent1, sent2)

    def fetches(r):
        rows = pl.ds(pl.multiple_of(r * COLS, COLS), COLS)
        return (
            pltpu.make_async_copy(cells_far.at[rows], cells.at[rows], sems.at[0, r]),
            pltpu.make_async_copy(species_far.at[rows], species.at[rows], sems.at[1, r]),
            pltpu.make_async_copy(mix_far.at[:, rows], mix.at[:, rows], sems.at[2, r]),
        )

    for r in range(ROWS):
        for copy in fetches(r):
            copy.start()
    zero = jnp.zeros((COLS, LANES), f32)
    for t in range(4):
        for k in (6, 7):
            w_s[t, k * COLS:(k + 1) * COLS] = zero
            w_s[t, (8 + k) * COLS:(9 + k) * COLS] = zero

    def one_row(r, carry):
        for copy in fetches(r):
            copy.wait()
        first = pl.multiple_of(r * COLS, COLS)
        rows = pl.ds(first, COLS)
        limit = limits_of(counts, first)
        for t in range(4):
            upper = (cells[rows, pl.ds(t * LANES, LANES)] & 1) == 1
            for k, w in enumerate(weights_of(limit, t, rows, species, mix)):
                w_s[t, k * COLS:(k + 1) * COLS] = jnp.where(upper, 0.0, w)
                w_s[t, (8 + k) * COLS:(9 + k) * COLS] = jnp.where(upper, w, 0.0)
        for b in range(COLS):
            plane = cells[pl.ds(first + b, 1), :] >> 8
            table = onehot_of(plane & 127, 8)
            w = jnp.concatenate([w_s[t, pl.ds(b, 16, stride=COLS)] for t in range(4)], axis=1).astype(bf16)
            second = jnp.broadcast_to(plane >> 7, (16, SLOTS)).astype(f32).astype(bf16) > 0.5
            none = jnp.zeros((16, SLOTS), bf16)
            halves = jnp.concatenate([jnp.where(second, none, w), jnp.where(second, w, none)], axis=0)
            dens = lax.dot_general(halves, table, (((1,), (1,)), ((), ())), preferred_element_type=f32)
            d_s[0, pl.ds(b, 16, stride=COLS)] = dens[:16]
            d_s[1, pl.ds(b, 16, stride=COLS)] = dens[16:]
        for z in range(2):
            for k in range(SPECIES):
                for h in range(2):
                    value = d_s[h, (z * 8 + k) * COLS:(z * 8 + k + 1) * COLS]
                    own[z, k, 2 * r + h] = value
                    sent[k // PER][z, k % PER, 2 * r + h] = value.astype(bf16)
        return carry

    lax.fori_loop(0, ROWS, one_row, 0)


VM = pltpu.MemorySpace.VMEM
SM = pltpu.MemorySpace.SMEM


def deposit(counts, cells, species, mix):
    half = (HALVES, COLS, LANES)
    return pl.pallas_call(
        deposit_kernel,
        name="deposit",
        in_specs=[pl.BlockSpec(memory_space=SM)] + [pl.BlockSpec(memory_space=pl.ANY)] * 3,
        out_specs=[pl.BlockSpec(memory_space=VM)] * 4,
        scratch_shapes=[
            pltpu.VMEM((ROWS * COLS, SLOTS), jnp.int32),
            pltpu.VMEM((ROWS * COLS, SLOTS), jnp.int32),
            pltpu.VMEM((SPECIES, ROWS * COLS, SLOTS), bf16),
            pltpu.VMEM((4, 16 * COLS, LANES), f32),
            pltpu.VMEM((2, 16 * COLS, LANES), f32),
            pltpu.SemaphoreType.DMA((3, ROWS)),
        ],
        out_shape=[jax.ShapeDtypeStruct((2, SPECIES) + half, f32)]
        + [jax.ShapeDtypeStruct((2, PER) + half, bf16)] * CHUNKS,
        compiler_params=pltpu.CompilerParams(vmem_limit_bytes=16 * MIB),
        cost_estimate=pl.CostEstimate(flops=10**9, bytes_accessed=5 * 10**6, transcendentals=0),
    )(counts, cells, species, mix)


def mixing_kernel(counts, mix_matrix, species, mix, mixed):
    def one_row(r, carry):
        first = pl.multiple_of(r * COLS, COLS)
        rows = pl.ds(first, COLS)
        limit = limits_of(counts, first)
        for t in range(4):
            ws = weights_of(limit, t, rows, species, mix)
            for l in range(SPECIES):
                v = mix_matrix[l, 0] * ws[0]
                for k in range(1, SPECIES):
                    v = v + mix_matrix[l, k] * ws[k]
                mixed[l, rows, t * LANES:(t + 1) * LANES] = v
        return carry

    lax.fori_loop(0, ROWS, one_row, 0)


def mixing(counts, mix_matrix, species, mix):
    return pl.pallas_call(
        mixing_kernel,
        name="mixing",
        in_specs=[pl.BlockSpec(memory_space=SM)] * 2 + [pl.BlockSpec(memory_space=VM)] * 2,
        out_specs=pl.BlockSpec(memory_space=VM),
        out_shape=jax.ShapeDtypeStruct((SPECIES, ROWS * COLS, SLOTS), f32),
        compiler_params=pltpu.CompilerParams(vmem_limit_bytes=12 * MIB),
        cost_estimate=pl.CostEstimate(flops=10**9, bytes_accessed=4 * 10**6, transcendentals=0),
    )(counts, mix_matrix, species, mix)


def scaled_taps():
    smooth_scale, slope_scale = 1.6396387, 1.5596421
    smooth_taps = {0: T0, 1: T1, -1: T1, 2: T2, -2: T2}
    slope_taps = {1: 0.5 * (T0 - T2), 2: 0.5 * T1, 3: 0.5 * T2}
    slope_taps.update({-j: -v for j, v in slope_taps.items()})
    return (
        {j: smooth_scale * v for j, v in smooth_taps.items()},
        {j: slope_scale * v for j, v in slope_taps.items()},
        smooth_scale,
        slope_scale,
    )


SMOOTH, SLOPE, SMOOTH_SCALE, SLOPE_SCALE = scaled_taps()


def tap_matrices():
    lane = np.arange(LANES)
    x, y = lane // 16, lane % 16
    results = []
    for main, other, extent in ((y, x, 16), (x, y, 8)):
        source = np.concatenate([main, np.where(main < extent // 2, main + extent, main - extent)])
        same = np.concatenate([other, other])[:, None] == other[None, :]
        gap = source[:, None] - main[None, :]
        for taps in (SMOOTH, SLOPE):
            matrix = np.zeros((2 * LANES, LANES), np.float32)
            for j, value in taps.items():
                matrix += np.where(same & (gap == j), np.float32(value), np.float32(0))
            results.append(matrix)
    return jnp.asarray(np.concatenate(results, axis=1)).astype(bf16)


def split(v):
    top = v.astype(bf16)
    return top, (v - top.astype(f32)).astype(bf16)


def smooth_kernel(taps, own, near_low, near_high, far_low, far_high, ready, x_s, y_s, w_s, g_s):
    k = pl.program_id(0)
    lane = lax.broadcasted_iota(jnp.int32, (COLS, LANES), 1)
    col = lane & 15
    cu = 1.0 / (SMOOTH_SCALE * SLOPE_SCALE)
    cz = 0.5 / (SMOOTH_SCALE * SMOOTH_SCALE)
    for h in range(HALVES):
        l2 = far_low[0, h].astype(f32)
        a = near_low[0, 0, h].astype(f32)
        b = near_low[1, 0, h].astype(f32)
        o0 = own[0, 0, h]
        o1 = own[1, 0, h]
        r0 = near_high[0, 0, h].astype(f32)
        r1 = near_high[1, 0, h].astype(f32)
        r2 = far_high[0, h].astype(f32)
        um = T2 * (l2 + o1) + T1 * (a + o0) + T0 * b
        u0 = T2 * (a + r0) + T1 * (b + o1) + T0 * o0
        u1 = T2 * (b + r1) + T1 * (o0 + r0) + T0 * o1
        up = T2 * (o0 + r2) + T1 * (o1 + r1) + T0 * r0
        for i, v in enumerate((cu * u0, cu * u1, cz * (u1 - um), cz * (up - u0))):
            around = jnp.where(col < 8, pltpu.roll(v, COLS - 1, 0), pltpu.roll(v, 1, 0))
            for part, value in ((0, v), (1, around)):
                for level, piece in enumerate(split(value)):
                    x_s[level, i, h * COLS:(h + 1) * COLS, part * LANES:(part + 1) * LANES] = piece
    for i in range(4):
        width = 2 * LANES if i < 2 else LANES
        table = taps[:, :width]
        out = jnp.dot(x_s[0, i], table, preferred_element_type=f32) + jnp.dot(
            x_s[1, i], table, preferred_element_type=f32
        )
        if i < 2:
            y_s[i] = out[:, :LANES]
            y_s[2 + i] = out[:, LANES:]
        else:
            y_s[2 + i] = out
    for p in range(6):
        for h in range(HALVES):
            before = (h + HALVES - 1) % HALVES
            after = (h + 1) % HALVES
            v = y_s[p, h * COLS:(h + 1) * COLS]
            around = jnp.where(
                lane < 64,
                y_s[p, after * COLS:(after + 1) * COLS],
                y_s[p, before * COLS:(before + 1) * COLS],
            )
            for part, value in ((0, v), (1, around)):
                for level, piece in enumerate(split(value)):
                    w_s[level, p, h * COLS:(h + 1) * COLS, part * LANES:(part + 1) * LANES] = piece
        table = taps[:, 3 * LANES:] if p < 2 else taps[:, 2 * LANES:3 * LANES]
        out = jnp.dot(w_s[0, p], table, preferred_element_type=f32) + jnp.dot(
            w_s[1, p], table, preferred_element_type=f32
        )
        for h in range(HALVES):
            g_s[h, pl.ds(pl.multiple_of((k * 8 + p) * COLS, COLS), COLS)] = out[h * COLS:(h + 1) * COLS]

    @pl.when(k == 0)
    def _():
        zero = jnp.zeros((HALVES, 2 * COLS, LANES), f32)
        for i in range(PER):
            g_s[:, (i * 8 + 6) * COLS:(i * 8 + 8) * COLS] = zero

    @pl.when(k == PER - 1)
    def _():
        def one_row(r, carry):
            for q in range(COLS):
                for h in range(2):
                    top, rest = split(g_s[2 * r + h, pl.ds(q, 16, stride=COLS)])
                    ready[r * COLS + q, :16, h * LANES:(h + 1) * LANES] = top
                    ready[r * COLS + q, 16:, h * LANES:(h + 1) * LANES] = rest
            return carry

        lax.fori_loop(0, ROWS, one_row, 0)


def smooth(chunk, taps, own, near_low, near_high, far_low, far_high):
    half = (HALVES, COLS, LANES)
    two = pl.BlockSpec((2, 1) + half, lambda k: (0, k, 0, 0, 0))
    one = pl.BlockSpec((1,) + half, lambda k: (k, 0, 0, 0))
    return pl.pallas_call(
        smooth_kernel,
        name="smooth",
        grid=(PER,),
        in_specs=[
            pl.BlockSpec((2 * LANES, 4 * LANES), lambda k: (0, 0)),
            pl.BlockSpec((2, 1) + half, lambda k: (0, chunk * PER + k, 0, 0, 0)),
            two,
            two,
            one,
            one,
        ],
        out_specs=pl.BlockSpec((ROWS * COLS, 32, 2 * LANES), lambda k: (0, 0, 0)),
        out_shape=jax.ShapeDtypeStruct((ROWS * COLS, 32, 2 * LANES), bf16),
        scratch_shapes=[
            pltpu.VMEM((2, 4, HALVES * COLS, 2 * LANES), bf16),
            pltpu.VMEM((6, HALVES * COLS, LANES), f32),
            pltpu.VMEM((2, 6, HALVES * COLS, 2 * LANES), bf16),
            pltpu.VMEM((HALVES, PER * 8 * COLS, LANES), f32),
        ],
        compiler_params=pltpu.CompilerParams(vmem_limit_bytes=24 * MIB),
        cost_estimate=pl.CostEstimate(flops=10**9, bytes_accessed=4 * 10**6, transcendentals=0),
    )(taps, own, near_low, near_high, far_low, far_high)


def pick_kernel(cells, ready0, ready1, ready2, mixed, forces, got_s):
    def one_group(g, slot):
        first = pl.multiple_of(g * GROUP, GROUP)
        for b in range(GROUP):
            d = first + b
            table = onehot_of(cells[pl.ds(d, 1), :] >> 8, 16)
            parts = [ready[d] for ready in (ready0, ready1, ready2)]
            rows = jnp.concatenate([p[:16] for p in parts] + [p[16:] for p in parts], axis=0)
            got = jnp.dot(rows, table, preferred_element_type=f32)
            got = got[:48] + got[48:]
            for t in range(4):
                got_s[slot, t, pl.ds(b, 48, stride=GROUP)] = got[:, t * LANES:(t + 1) * LANES]
        for t in range(4):
            lanes = slice(t * LANES, (t + 1) * LANES)
            upper = (cells[pl.ds(first, GROUP), lanes] & 1) == 1
            vs = [mixed[k, pl.ds(first, GROUP), lanes] for k in range(SPECIES)]
            for a in range(3):
                total = None
                for k in range(SPECIES):
                    row = ((k // PER) * 16 + (k % PER) * 8 + 2 * a) * GROUP
                    value = jnp.where(
                        upper, got_s[slot, t, row + GROUP:row + 2 * GROUP], got_s[slot, t, row:row + GROUP]
                    )
                    total = vs[k] * value if total is None else total + vs[k] * value
                forces[a, pl.ds(first, GROUP), lanes] = total

    def two_groups(i, carry):
        one_group(2 * i, 0)
        one_group(2 * i + 1, 1)
        return carry

    lax.fori_loop(0, ROWS * COLS // GROUP // 2, two_groups, 0)


def pick(cells, ready, mixed):
    return pl.pallas_call(
        pick_kernel,
        name="pick",
        in_specs=[pl.BlockSpec(memory_space=VM)] * 5,
        out_specs=pl.BlockSpec(memory_space=VM),
        out_shape=jax.ShapeDtypeStruct((3, ROWS * COLS, SLOTS), f32),
        scratch_shapes=[pltpu.VMEM((2, 4, 48 * GROUP, LANES), f32)],
        compiler_params=pltpu.CompilerParams(vmem_limit_bytes=24 * MIB),
        cost_estimate=pl.CostEstimate(flops=6 * 10**9, bytes_accessed=10**7, transcendentals=0),
    )(cells, *ready, mixed)


def body(send_cells, send_species, send_mix, send_counts, chi):
    axes = ("row", "col")
    count = lax.axis_size("row") * lax.axis_size("col")
    up = [(i, (i + 1) % count) for i in range(count)]
    down = [(j, i) for i, j in up]
    chis = 0.5 * (chi + chi.T) * (1.0 - jnp.eye(SPECIES, dtype=f32))
    mix_matrix = -0.5 * (chis + 1.0)
    cells, species, mix, counts = send_cells[0], send_species[0], send_mix[0], send_counts[0]
    own, *sent = deposit(counts, cells, species, mix)
    taps = tap_matrices()
    ready = []
    for chunk in range(CHUNKS):
        near_low = lax.ppermute(sent[chunk], axes, up)
        near_high = lax.ppermute(sent[chunk], axes, down)
        far_low = lax.ppermute(near_low[1], axes, up)
        far_high = lax.ppermute(near_high[0], axes, down)
        ready.append(smooth(chunk, taps, own, near_low, near_high, far_low, far_high))
    mixed = mixing(counts, mix_matrix, species, mix)
    return pick(cells, ready, mixed)[None]


def solution(mesh):
    return jax.shard_map(
        body,
        mesh=mesh,
        in_specs=(
            P(("row", "col"), None, None),
            P(("row", "col"), None, None),
            P(("row", "col"), None, None, None),
            P(("row", "col"), None),
            P(),
        ),
        out_specs=P(("row", "col"), None, None, None),
        check_vma=False,
    )
```

```python
import functools

import jax
import jax.numpy as jnp
import numpy as np
from jax import lax
from jax.experimental import pallas as pl
from jax.experimental.pallas import tpu as pltpu
from jax.sharding import PartitionSpec as P


SPECIES = 6
ROWS = 8
COLS = 16
HALVES = 16
LANES = 128
SLOTS = 512
SIZES = (4, 2)
STARTS = (0, 4)
GROUP = 8
WIDE = COLS + 1
SLOT = GROUP + 1
MIB = 1 << 20

raw_taps = (0.1353352832366127, 0.6065306597126334, 1.0)
tap_total = raw_taps[2] + 2.0 * (raw_taps[0] + raw_taps[1])
T2, T1, T0 = (t / tap_total for t in raw_taps)

f32 = jnp.float32
bf16 = jnp.bfloat16


def onehot_of(row, count):
    wide = jnp.broadcast_to(row, (16, SLOTS))
    ids = lax.broadcasted_iota(jnp.int32, (16, SLOTS), 0)
    inner = jnp.where((wide & 15) == ids, 1.0, 0.0).astype(bf16)
    outer = (wide >> 4).astype(f32).astype(bf16)
    none = jnp.zeros((16, SLOTS), bf16)
    return jnp.concatenate(
        [jnp.where(outer == jnp.full((16, SLOTS), i, bf16), inner, none) for i in range(count)], axis=0
    )


def weights_of(limit, t, rows, species, mix):
    part = pl.ds(t * LANES, LANES)
    lane = lax.broadcasted_iota(jnp.int32, (COLS, LANES), 1)
    valid = (lane + t * LANES) < limit
    kind = species[rows, part]
    found = []
    for k in range(SPECIES):
        w = jnp.where(kind == k, 1.0, 0.0) + mix[k, rows, part].astype(f32)
        found.append(jnp.where(valid, w, 0.0).astype(bf16).astype(f32))
    return found


def limits_of(counts, first):
    rows = lax.broadcasted_iota(jnp.int32, (COLS, LANES), 0)
    limit = jnp.zeros((COLS, LANES), jnp.int32)
    for i in range(COLS):
        limit = jnp.where(rows == i, counts[first + i], limit)
    return limit


def deposit_kernel(counts, cells_far, species_far, mix_far, own_far, sent0_far, sent1_far,
                   cells, species, mix, own, sent0, sent1, w_s, d_s, sems, out_sems):
    sent = [(sent0, k) for k in range(SIZES[0])] + [(sent1, k) for k in range(SIZES[1])]

    def fetches(r):
        rows = pl.ds(pl.multiple_of(r * COLS, COLS), COLS)
        return (
            pltpu.make_async_copy(cells_far.at[rows], cells.at[rows], sems.at[0, r]),
            pltpu.make_async_copy(species_far.at[rows], species.at[rows], sems.at[1, r]),
            pltpu.make_async_copy(mix_far.at[:, rows], mix.at[:, rows], sems.at[2, r]),
        )

    def results(r):
        part = pl.ds(2 * r, 2)
        return [
            pltpu.make_async_copy(near.at[:, :, part], far.at[:, :, part], out_sems.at[i, r])
            for i, (near, far) in enumerate(((sent0, sent0_far), (sent1, sent1_far), (own, own_far)))
        ]

    for r in range(ROWS):
        for copy in fetches(r):
            copy.start()
    zero = jnp.zeros((COLS, LANES), f32)
    for t in range(4):
        for k in (6, 7):
            w_s[t, k * WIDE:k * WIDE + COLS] = zero
            w_s[t, (8 + k) * WIDE:(8 + k) * WIDE + COLS] = zero

    def one_row(r, carry):
        for copy in fetches(r):
            copy.wait()
        first = pl.multiple_of(r * COLS, COLS)
        rows = pl.ds(first, COLS)
        limit = limits_of(counts, first)
        for t in range(4):
            upper = (cells[rows, pl.ds(t * LANES, LANES)] & 1) == 1
            for k, w in enumerate(weights_of(limit, t, rows, species, mix)):
                w_s[t, k * WIDE:k * WIDE + COLS] = jnp.where(upper, 0.0, w)
                w_s[t, (8 + k) * WIDE:(8 + k) * WIDE + COLS] = jnp.where(upper, w, 0.0)
        for b in range(COLS):
            plane = cells[pl.ds(first + b, 1), :] >> 8
            table = onehot_of(plane & 127, 8)
            w = jnp.concatenate([w_s[t, pl.ds(b, 16, stride=WIDE)] for t in range(4)], axis=1).astype(bf16)
            second = jnp.broadcast_to(plane >> 7, (16, SLOTS)).astype(f32).astype(bf16) > 0.5
            none = jnp.zeros((16, SLOTS), bf16)
            halves = jnp.concatenate([jnp.where(second, none, w), jnp.where(second, w, none)], axis=0)
            dens = lax.dot_general(halves, table, (((1,), (1,)), ((), ())), preferred_element_type=f32)
            d_s[0, pl.ds(b, 16, stride=WIDE)] = dens[:16]
            d_s[1, pl.ds(b, 16, stride=WIDE)] = dens[16:]
        for z in range(2):
            for k in range(SPECIES):
                for h in range(2):
                    value = d_s[h, (z * 8 + k) * WIDE:(z * 8 + k) * WIDE + COLS]
                    own[z, k, 2 * r + h] = value
                    sent[k][0][z, sent[k][1], 2 * r + h] = value.astype(bf16)
        for copy in results(r):
            copy.start()
        return carry

    lax.fori_loop(0, ROWS, one_row, 0)
    for r in range(ROWS):
        for copy in results(r):
            copy.wait()


VM = pltpu.MemorySpace.VMEM
SM = pltpu.MemorySpace.SMEM


def deposit(counts, cells, species, mix):
    half = (HALVES, COLS, LANES)
    return pl.pallas_call(
        deposit_kernel,
        name="deposit",
        in_specs=[pl.BlockSpec(memory_space=SM)] + [pl.BlockSpec(memory_space=pltpu.MemorySpace.HBM)] * 3,
        out_specs=[pl.BlockSpec(memory_space=pltpu.MemorySpace.HBM)] * 3,
        scratch_shapes=[
            pltpu.VMEM((ROWS * COLS, SLOTS), jnp.int32),
            pltpu.VMEM((ROWS * COLS, SLOTS), jnp.int32),
            pltpu.VMEM((SPECIES, ROWS * COLS, SLOTS), bf16),
            pltpu.VMEM((2, SPECIES) + half, f32),
            pltpu.VMEM((2, SIZES[0]) + half, bf16),
            pltpu.VMEM((2, SIZES[1]) + half, bf16),
            pltpu.VMEM((4, 16 * WIDE, LANES), f32),
            pltpu.VMEM((2, 16 * WIDE, LANES), f32),
            pltpu.SemaphoreType.DMA((3, ROWS)),
            pltpu.SemaphoreType.DMA((3, ROWS)),
        ],
        out_shape=[jax.ShapeDtypeStruct((2, SPECIES) + half, f32)]
        + [jax.ShapeDtypeStruct((2, size) + half, bf16) for size in SIZES],
        compiler_params=pltpu.CompilerParams(vmem_limit_bytes=60 * MIB),
        cost_estimate=pl.CostEstimate(flops=10**9, bytes_accessed=5 * 10**6, transcendentals=0),
    )(counts, cells, species, mix)


def mixing_kernel(counts, mix_matrix, species, mix, mixed):
    def one_row(r, carry):
        first = pl.multiple_of(r * COLS, COLS)
        rows = pl.ds(first, COLS)
        limit = limits_of(counts, first)
        for t in range(4):
            ws = weights_of(limit, t, rows, species, mix)
            for l in range(SPECIES):
                v = mix_matrix[l, 0] * ws[0]
                for k in range(1, SPECIES):
                    v = v + mix_matrix[l, k] * ws[k]
                mixed[l, rows, t * LANES:(t + 1) * LANES] = v
        return carry

    lax.fori_loop(0, ROWS, one_row, 0)


def mixing(counts, mix_matrix, species, mix):
    return pl.pallas_call(
        mixing_kernel,
        name="mixing",
        in_specs=[pl.BlockSpec(memory_space=SM)] * 2 + [pl.BlockSpec(memory_space=VM)] * 2,
        out_specs=pl.BlockSpec(memory_space=VM),
        out_shape=jax.ShapeDtypeStruct((SPECIES, ROWS * COLS, SLOTS), f32),
        compiler_params=pltpu.CompilerParams(vmem_limit_bytes=12 * MIB),
        cost_estimate=pl.CostEstimate(flops=10**9, bytes_accessed=4 * 10**6, transcendentals=0),
    )(counts, mix_matrix, species, mix)


def scaled_taps():
    smooth_scale, slope_scale = 1.6396387, 1.5596421
    smooth_taps = {0: T0, 1: T1, -1: T1, 2: T2, -2: T2}
    slope_taps = {1: 0.5 * (T0 - T2), 2: 0.5 * T1, 3: 0.5 * T2}
    slope_taps.update({-j: -v for j, v in slope_taps.items()})
    return (
        {j: smooth_scale * v for j, v in smooth_taps.items()},
        {j: slope_scale * v for j, v in slope_taps.items()},
        smooth_scale,
        slope_scale,
    )


SMOOTH, SLOPE, SMOOTH_SCALE, SLOPE_SCALE = scaled_taps()


def tap_matrices():
    lane = np.arange(LANES)
    x, y = lane // 16, lane % 16
    results = []
    for main, other, extent in ((y, x, 16), (x, y, 8)):
        source = np.concatenate([main, np.where(main < extent // 2, main + extent, main - extent)])
        same = np.concatenate([other, other])[:, None] == other[None, :]
        gap = source[:, None] - main[None, :]
        for taps in (SMOOTH, SLOPE):
            matrix = np.zeros((2 * LANES, LANES), np.float32)
            for j, value in taps.items():
                matrix += np.where(same & (gap == j), np.float32(value), np.float32(0))
            results.append(matrix)
    return jnp.asarray(np.concatenate(results, axis=1)).astype(bf16)


def split(v):
    top = v.astype(bf16)
    return top, (v - top.astype(f32)).astype(bf16)


def smooth_kernel(size, even_ref, taps, own, near_a, near_b, far_a, far_b, ready, x_s, y_s, w_s, g_s):
    k = pl.program_id(0)
    lane = lax.broadcasted_iota(jnp.int32, (COLS, LANES), 1)
    col = lane & 15
    cu = 1.0 / (SMOOTH_SCALE * SLOPE_SCALE)
    cz = 0.5 / (SMOOTH_SCALE * SMOOTH_SCALE)
    even = jnp.full((COLS, LANES), even_ref[0], jnp.int32) == 1
    for h in range(HALVES):
        def sides(a, b):
            a, b = a.astype(f32), b.astype(f32)
            return jnp.where(even, b, a), jnp.where(even, a, b)

        l2, r2 = sides(far_a[0, h], far_b[0, h])
        a, r0 = sides(near_a[0, 0, h], near_b[0, 0, h])
        b, r1 = sides(near_a[1, 0, h], near_b[1, 0, h])
        o0 = own[0, 0, h]
        o1 = own[1, 0, h]
        um = T2 * (l2 + o1) + T1 * (a + o0) + T0 * b
        u0 = T2 * (a + r0) + T1 * (b + o1) + T0 * o0
        u1 = T2 * (b + r1) + T1 * (o0 + r0) + T0 * o1
        up = T2 * (o0 + r2) + T1 * (o1 + r1) + T0 * r0
        for i, v in enumerate((cu * u0, cu * u1, cz * (u1 - um), cz * (up - u0))):
            around = jnp.where(col < 8, pltpu.roll(v, COLS - 1, 0), pltpu.roll(v, 1, 0))
            for part, value in ((0, v), (1, around)):
                for level, piece in enumerate(split(value)):
                    x_s[level, i, h * COLS:(h + 1) * COLS, part * LANES:(part + 1) * LANES] = piece
    for i in range(4):
        width = 2 * LANES if i < 2 else LANES
        table = taps[:, :width]
        out = jnp.dot(x_s[0, i], table, preferred_element_type=f32) + jnp.dot(
            x_s[1, i], table, preferred_element_type=f32
        )
        if i < 2:
            y_s[i] = out[:, :LANES]
            y_s[2 + i] = out[:, LANES:]
        else:
            y_s[2 + i] = out
    for p in range(6):
        for h in range(HALVES):
            before = (h + HALVES - 1) % HALVES
            after = (h + 1) % HALVES
            v = y_s[p, h * COLS:(h + 1) * COLS]
            around = jnp.where(
                lane < 64,
                y_s[p, after * COLS:(after + 1) * COLS],
                y_s[p, before * COLS:(before + 1) * COLS],
            )
            for part, value in ((0, v), (1, around)):
                for level, piece in enumerate(split(value)):
                    w_s[level, p, h * COLS:(h + 1) * COLS, part * LANES:(part + 1) * LANES] = piece
        table = taps[:, 3 * LANES:] if p < 2 else taps[:, 2 * LANES:3 * LANES]
        out = jnp.dot(w_s[0, p], table, preferred_element_type=f32) + jnp.dot(
            w_s[1, p], table, preferred_element_type=f32
        )
        for h in range(HALVES):
            g_s[h, pl.ds((k * 8 + p) * WIDE, COLS)] = out[h * COLS:(h + 1) * COLS]

    @pl.when(k == 0)
    def _():
        zero = jnp.zeros((HALVES, 2 * WIDE, LANES), f32)
        for i in range(size):
            g_s[:, (i * 8 + 6) * WIDE:(i * 8 + 8) * WIDE] = zero

    @pl.when(k == size - 1)
    def _():
        def one_row(r, carry):
            for q in range(COLS):
                for h in range(2):
                    top, rest = split(g_s[2 * r + h, pl.ds(q, 8 * size, stride=WIDE)])
                    ready[r * COLS + q, :8 * size, h * LANES:(h + 1) * LANES] = top
                    ready[r * COLS + q, 8 * size:, h * LANES:(h + 1) * LANES] = rest
            return carry

        lax.fori_loop(0, ROWS, one_row, 0)


def smooth(chunk, even, taps, own, near_a, near_b, far_a, far_b):
    size, start = SIZES[chunk], STARTS[chunk]
    half = (HALVES, COLS, LANES)
    two = pl.BlockSpec((2, 1) + half, lambda k: (0, k, 0, 0, 0))
    one = pl.BlockSpec((1,) + half, lambda k: (k, 0, 0, 0))
    return pl.pallas_call(
        functools.partial(smooth_kernel, size),
        name="smooth",
        grid=(size,),
        in_specs=[
            pl.BlockSpec(memory_space=SM),
            pl.BlockSpec((2 * LANES, 4 * LANES), lambda k: (0, 0)),
            pl.BlockSpec((2, 1) + half, lambda k: (0, start + k, 0, 0, 0)),
            two,
            two,
            one,
            one,
        ],
        out_specs=pl.BlockSpec((ROWS * COLS, 16 * size, 2 * LANES), lambda k: (0, 0, 0)),
        out_shape=jax.ShapeDtypeStruct((ROWS * COLS, 16 * size, 2 * LANES), bf16),
        scratch_shapes=[
            pltpu.VMEM((2, 4, HALVES * COLS, 2 * LANES), bf16),
            pltpu.VMEM((6, HALVES * COLS, LANES), f32),
            pltpu.VMEM((2, 6, HALVES * COLS, 2 * LANES), bf16),
            pltpu.VMEM((HALVES, size * 8 * WIDE, LANES), f32),
        ],
        compiler_params=pltpu.CompilerParams(vmem_limit_bytes=24 * MIB),
        cost_estimate=pl.CostEstimate(flops=10**9, bytes_accessed=4 * 10**6, transcendentals=0),
    )(even, taps, own, near_a, near_b, far_a, far_b)


def pick_kernel(cells, ready0, ready1, mixed, forces, got_s):
    def one_group(g, slot):
        first = pl.multiple_of(g * GROUP, GROUP)
        for b in range(GROUP):
            d = first + b
            table = onehot_of(cells[pl.ds(d, 1), :] >> 8, 16)
            rows = jnp.concatenate(
                [ready0[d, :32], ready1[d, :16], ready0[d, 32:], ready1[d, 16:]], axis=0
            )
            got = jnp.dot(rows, table, preferred_element_type=f32)
            got = got[:48] + got[48:]
            for t in range(4):
                got_s[slot, t, pl.ds(b, 48, stride=SLOT)] = got[:, t * LANES:(t + 1) * LANES]
        for t in range(4):
            lanes = slice(t * LANES, (t + 1) * LANES)
            upper = (cells[pl.ds(first, GROUP), lanes] & 1) == 1
            vs = [mixed[k, pl.ds(first, GROUP), lanes] for k in range(SPECIES)]
            for a in range(3):
                total = None
                for k in range(SPECIES):
                    row = (k * 8 + 2 * a) * SLOT
                    value = jnp.where(
                        upper, got_s[slot, t, row + SLOT:row + SLOT + GROUP], got_s[slot, t, row:row + GROUP]
                    )
                    total = vs[k] * value if total is None else total + vs[k] * value
                forces[a, pl.ds(first, GROUP), lanes] = total

    def four_groups(i, carry):
        for j in range(4):
            one_group(4 * i + j, j)
        return carry

    lax.fori_loop(0, ROWS * COLS // GROUP // 4, four_groups, 0)


def pick(cells, ready, mixed):
    return pl.pallas_call(
        pick_kernel,
        name="pick",
        in_specs=[pl.BlockSpec(memory_space=VM)] * 4,
        out_specs=pl.BlockSpec(memory_space=VM),
        out_shape=jax.ShapeDtypeStruct((3, ROWS * COLS, SLOTS), f32),
        scratch_shapes=[pltpu.VMEM((4, 4, 48 * SLOT, LANES), f32)],
        compiler_params=pltpu.CompilerParams(vmem_limit_bytes=24 * MIB),
        cost_estimate=pl.CostEstimate(flops=6 * 10**9, bytes_accessed=10**7, transcendentals=0),
    )(cells, *ready, mixed)


def body(send_cells, send_species, send_mix, send_counts, chi):
    axes = ("row", "col")
    count = lax.axis_size("row") * lax.axis_size("col")
    swap_a = [(i, i ^ 1) for i in range(count)]
    swap_b = [(i, (i + (1 if i % 2 else -1)) % count) for i in range(count)]
    odd = lax.axis_index("col") % 2
    even = (1 - odd).reshape(1)
    chis = 0.5 * (chi + chi.T) * (1.0 - jnp.eye(SPECIES, dtype=f32))
    mix_matrix = -0.5 * (chis + 1.0)
    cells, species, mix, counts = send_cells[0], send_species[0], send_mix[0], send_counts[0]
    own, *sent = deposit(counts, cells, species, mix)
    taps = tap_matrices()
    ready = []
    for chunk in range(len(SIZES)):
        def swap(value, pairs):
            return lax.ppermute(value, axes, pairs)

        near_a = swap(sent[chunk], swap_a)
        near_b = swap(sent[chunk], swap_b)
        far_a = swap(lax.dynamic_index_in_dim(near_b, 1 - odd, 0, False), swap_a)
        far_b = swap(lax.dynamic_index_in_dim(near_a, odd, 0, False), swap_b)
        ready.append(smooth(chunk, even, taps, own, near_a, near_b, far_a, far_b))
    mixed = mixing(counts, mix_matrix, species, mix)
    return pick(cells, ready, mixed)[None]


def solution(mesh):
    return jax.shard_map(
        body,
        mesh=mesh,
        in_specs=(
            P(("row", "col"), None, None),
            P(("row", "col"), None, None),
            P(("row", "col"), None, None, None),
            P(("row", "col"), None),
            P(),
        ),
        out_specs=P(("row", "col"), None, None, None),
        check_vma=False,
    )
```

```python
import functools

import jax
import jax.numpy as jnp
import numpy as np
from jax import lax
from jax.experimental import pallas as pl
from jax.experimental.pallas import tpu as pltpu
from jax.sharding import PartitionSpec as P


SPECIES = 6
ROWS = 8
COLS = 16
HALVES = 16
LANES = 128
SLOTS = 512
SIZES = (4, 2)
STARTS = (0, 4)
GROUP = 8
WIDE = COLS + 1
SLOT = GROUP + 1
MIB = 1 << 20
LIMIT = 24

raw_taps = (0.1353352832366127, 0.6065306597126334, 1.0)
tap_total = raw_taps[2] + 2.0 * (raw_taps[0] + raw_taps[1])
T2, T1, T0 = (t / tap_total for t in raw_taps)

f32 = jnp.float32
bf16 = jnp.bfloat16


def digits_of(row):
    wide = jnp.broadcast_to(row, (8, SLOTS))
    low = (wide >> 8) & 15
    ids = lax.broadcasted_iota(jnp.int32, (8, SLOTS), 0)
    inner = jnp.concatenate(
        [jnp.where(low == ids, 1.0, 0.0), jnp.where(low == ids + 8, 1.0, 0.0)], axis=0
    ).astype(bf16)
    high = (wide >> 12).astype(f32)
    return inner, jnp.concatenate([high, high], axis=0).astype(bf16)


def table_of(inner, outer, count):
    none = jnp.zeros((16, SLOTS), bf16)
    return jnp.concatenate(
        [jnp.where(outer == jnp.full((16, SLOTS), i, bf16), inner, none) for i in range(count)], axis=0
    )


def weights_of(limit, t, rows, species, mix):
    part = pl.ds(t * LANES, LANES)
    lane = lax.broadcasted_iota(jnp.int32, (COLS, LANES), 1)
    valid = (lane + t * LANES) < limit
    kind = species[rows, part]
    found = []
    for k in range(SPECIES):
        w = jnp.where(kind == k, 1.0, 0.0) + mix[k, rows, part].astype(f32)
        found.append(jnp.where(valid, w, 0.0).astype(bf16).astype(f32))
    return found


def limits_of(counts, first):
    rows = lax.broadcasted_iota(jnp.int32, (COLS, LANES), 0)
    limit = jnp.zeros((COLS, LANES), jnp.int32)
    for i in range(COLS):
        limit = jnp.where(rows == i, counts[first + i], limit)
    return limit


def deposit_kernel(counts_far, cells_far, species_far, mix_far, own_far, sent0_far, sent1_far,
                   counts, cells, species, mix, own, sent0, sent1, w_s, d_s, sems, out_sems, count_sem):
    sent = [(sent0, k) for k in range(SIZES[0])] + [(sent1, k) for k in range(SIZES[1])]

    def fetches(r):
        rows = pl.ds(pl.multiple_of(r * COLS, COLS), COLS)
        return (
            pltpu.make_async_copy(cells_far.at[rows], cells.at[rows], sems.at[0, r]),
            pltpu.make_async_copy(species_far.at[rows], species.at[rows], sems.at[1, r]),
            pltpu.make_async_copy(mix_far.at[:, rows], mix.at[:, rows], sems.at[2, r]),
        )

    def results(r):
        part = pl.ds(2 * r, 2)
        return [
            pltpu.make_async_copy(near.at[:, :, part], far.at[:, :, part], out_sems.at[i, r])
            for i, (near, far) in enumerate(((sent0, sent0_far), (sent1, sent1_far), (own, own_far)))
        ]

    count_copy = pltpu.make_async_copy(counts_far, counts, count_sem)
    count_copy.start()
    for r in range(ROWS):
        for copy in fetches(r):
            copy.start()
    zero = jnp.zeros((COLS, LANES), f32)
    for t in range(4):
        for k in (6, 7):
            w_s[t, k * WIDE:k * WIDE + COLS] = zero
            w_s[t, (8 + k) * WIDE:(8 + k) * WIDE + COLS] = zero

    count_copy.wait()

    def one_row(r, carry):
        for copy in fetches(r):
            copy.wait()
        first = pl.multiple_of(r * COLS, COLS)
        rows = pl.ds(first, COLS)
        limit = limits_of(counts, first)
        for t in range(4):
            upper = (cells[rows, pl.ds(t * LANES, LANES)] & 1) == 1
            for k, w in enumerate(weights_of(limit, t, rows, species, mix)):
                w_s[t, k * WIDE:k * WIDE + COLS] = jnp.where(upper, 0.0, w)
                w_s[t, (8 + k) * WIDE:(8 + k) * WIDE + COLS] = jnp.where(upper, w, 0.0)
        for b in range(COLS):
            inner, outer = digits_of(cells[pl.ds(first + b, 1), :])
            second = outer > 7.5
            table = table_of(inner, jnp.where(second, outer - 8.0, outer), 8)
            w = jnp.concatenate([w_s[t, pl.ds(b, 16, stride=WIDE)] for t in range(4)], axis=1).astype(bf16)
            none = jnp.zeros((16, SLOTS), bf16)
            halves = jnp.concatenate([jnp.where(second, none, w), jnp.where(second, w, none)], axis=0)
            dens = lax.dot_general(halves, table, (((1,), (1,)), ((), ())), preferred_element_type=f32)
            d_s[0, pl.ds(b, 16, stride=WIDE)] = dens[:16]
            d_s[1, pl.ds(b, 16, stride=WIDE)] = dens[16:]
        for z in range(2):
            for k in range(SPECIES):
                for h in range(2):
                    value = d_s[h, (z * 8 + k) * WIDE:(z * 8 + k) * WIDE + COLS]
                    own[z, k, 2 * r + h] = value
                    sent[k][0][z, sent[k][1], 2 * r + h] = value.astype(bf16)
        for copy in results(r):
            copy.start()
        return carry

    lax.fori_loop(0, ROWS, one_row, 0)
    for r in range(ROWS):
        for copy in results(r):
            copy.wait()


VM = pltpu.MemorySpace.VMEM
SM = pltpu.MemorySpace.SMEM
FAR = pltpu.MemorySpace.HBM


def deposit(counts, cells, species, mix):
    half = (HALVES, COLS, LANES)
    return pl.pallas_call(
        deposit_kernel,
        name="deposit",
        in_specs=[pl.BlockSpec(memory_space=FAR)] * 4,
        out_specs=[pl.BlockSpec(memory_space=FAR)] * 3,
        scratch_shapes=[
            pltpu.SMEM((ROWS * COLS,), jnp.int32),
            pltpu.VMEM((ROWS * COLS, SLOTS), jnp.int32),
            pltpu.VMEM((ROWS * COLS, SLOTS), jnp.int32),
            pltpu.VMEM((SPECIES, ROWS * COLS, SLOTS), bf16),
            pltpu.VMEM((2, SPECIES) + half, f32),
            pltpu.VMEM((2, SIZES[0]) + half, bf16),
            pltpu.VMEM((2, SIZES[1]) + half, bf16),
            pltpu.VMEM((4, 16 * WIDE, LANES), f32),
            pltpu.VMEM((2, 16 * WIDE, LANES), f32),
            pltpu.SemaphoreType.DMA((3, ROWS)),
            pltpu.SemaphoreType.DMA((3, ROWS)),
            pltpu.SemaphoreType.DMA,
        ],
        out_shape=[jax.ShapeDtypeStruct((2, SPECIES) + half, f32)]
        + [jax.ShapeDtypeStruct((2, size) + half, bf16) for size in SIZES],
        compiler_params=pltpu.CompilerParams(vmem_limit_bytes=LIMIT * MIB),
        cost_estimate=pl.CostEstimate(flops=10**9, bytes_accessed=5 * 10**6, transcendentals=0),
    )(*(pltpu.with_memory_space_constraint(v, FAR) for v in (counts, cells, species, mix)))


def mixing_kernel(counts, mix_matrix, species, mix, mixed):
    def one_row(r, carry):
        first = pl.multiple_of(r * COLS, COLS)
        rows = pl.ds(first, COLS)
        limit = limits_of(counts, first)
        for t in range(4):
            ws = weights_of(limit, t, rows, species, mix)
            for l in range(SPECIES):
                v = mix_matrix[l, 0] * ws[0]
                for k in range(1, SPECIES):
                    v = v + mix_matrix[l, k] * ws[k]
                mixed[l, rows, t * LANES:(t + 1) * LANES] = v
        return carry

    lax.fori_loop(0, ROWS, one_row, 0)


def mixing(counts, mix_matrix, species, mix):
    return pl.pallas_call(
        mixing_kernel,
        name="mixing",
        in_specs=[pl.BlockSpec(memory_space=SM)] * 2 + [pl.BlockSpec(memory_space=VM)] * 2,
        out_specs=pl.BlockSpec(memory_space=VM),
        out_shape=jax.ShapeDtypeStruct((SPECIES, ROWS * COLS, SLOTS), f32),
        compiler_params=pltpu.CompilerParams(vmem_limit_bytes=12 * MIB),
        cost_estimate=pl.CostEstimate(flops=10**9, bytes_accessed=4 * 10**6, transcendentals=0),
    )(counts, mix_matrix, species, mix)


def scaled_taps():
    smooth_scale, slope_scale = 1.6396387, 1.5596421
    smooth_taps = {0: T0, 1: T1, -1: T1, 2: T2, -2: T2}
    slope_taps = {1: 0.5 * (T0 - T2), 2: 0.5 * T1, 3: 0.5 * T2}
    slope_taps.update({-j: -v for j, v in slope_taps.items()})
    return (
        {j: smooth_scale * v for j, v in smooth_taps.items()},
        {j: slope_scale * v for j, v in slope_taps.items()},
        smooth_scale,
        slope_scale,
    )


SMOOTH, SLOPE, SMOOTH_SCALE, SLOPE_SCALE = scaled_taps()


def tap_matrices():
    lane = np.arange(LANES)
    x, y = lane // 16, lane % 16
    results = []
    for main, other, extent in ((y, x, 16), (x, y, 8)):
        source = np.concatenate([main, np.where(main < extent // 2, main + extent, main - extent)])
        same = np.concatenate([other, other])[:, None] == other[None, :]
        gap = source[:, None] - main[None, :]
        for taps in (SMOOTH, SLOPE):
            matrix = np.zeros((2 * LANES, LANES), np.float32)
            for j, value in taps.items():
                matrix += np.where(same & (gap == j), np.float32(value), np.float32(0))
            results.append(matrix)
    return jnp.asarray(np.concatenate(results, axis=1)).astype(bf16)


def split(v):
    top = v.astype(bf16)
    return top, (v - top.astype(f32)).astype(bf16)


def smooth_kernel(size, even_ref, taps, own, near_a, near_b, far_a, far_b, ready, x_s, y_s, w_s, g_s):
    k = pl.program_id(0)
    lane = lax.broadcasted_iota(jnp.int32, (COLS, LANES), 1)
    col = lane & 15
    lower = lane.astype(f32).astype(bf16) < 64
    cu = 1.0 / (SMOOTH_SCALE * SLOPE_SCALE)
    cz = 0.5 / (SMOOTH_SCALE * SMOOTH_SCALE)
    even = jnp.full((COLS, LANES), even_ref[0], jnp.int32) == 1
    for h in range(HALVES):
        def sides(a, b):
            a, b = a.astype(f32), b.astype(f32)
            return jnp.where(even, b, a), jnp.where(even, a, b)

        l2, r2 = sides(far_a[0, h], far_b[0, h])
        a, r0 = sides(near_a[0, 0, h], near_b[0, 0, h])
        b, r1 = sides(near_a[1, 0, h], near_b[1, 0, h])
        o0 = own[0, 0, h]
        o1 = own[1, 0, h]
        um = T2 * (l2 + o1) + T1 * (a + o0) + T0 * b
        u0 = T2 * (a + r0) + T1 * (b + o1) + T0 * o0
        u1 = T2 * (b + r1) + T1 * (o0 + r0) + T0 * o1
        up = T2 * (o0 + r2) + T1 * (o1 + r1) + T0 * r0
        for i, v in enumerate((cu * u0, cu * u1, cz * (u1 - um), cz * (up - u0))):
            around = jnp.where(col < 8, pltpu.roll(v, COLS - 1, 0), pltpu.roll(v, 1, 0))
            for part, value in ((0, v), (1, around)):
                for level, piece in enumerate(split(value)):
                    x_s[level, i, h * COLS:(h + 1) * COLS, part * LANES:(part + 1) * LANES] = piece
    for i in range(4):
        width = 2 * LANES if i < 2 else LANES
        table = taps[:, :width]
        out = jnp.dot(x_s[0, i], table, preferred_element_type=f32) + jnp.dot(
            x_s[1, i], table, preferred_element_type=f32
        )
        if i < 2:
            y_s[i] = out[:, :LANES]
            y_s[2 + i] = out[:, LANES:]
        else:
            y_s[2 + i] = out
    for p in range(6):
        pieces = [split(y_s[p, h * COLS:(h + 1) * COLS]) for h in range(HALVES)]
        for h in range(HALVES):
            rows = slice(h * COLS, (h + 1) * COLS)
            for level in range(2):
                w_s[level, p, rows, :LANES] = pieces[h][level]
                w_s[level, p, rows, LANES:] = jnp.where(
                    lower, pieces[(h + 1) % HALVES][level], pieces[(h - 1) % HALVES][level]
                )
        table = taps[:, 3 * LANES:] if p < 2 else taps[:, 2 * LANES:3 * LANES]
        out = jnp.dot(w_s[0, p], table, preferred_element_type=f32) + jnp.dot(
            w_s[1, p], table, preferred_element_type=f32
        )
        for h in range(HALVES):
            g_s[h, pl.ds((k * 8 + p) * WIDE, COLS)] = out[h * COLS:(h + 1) * COLS]

    @pl.when(k == 0)
    def _():
        zero = jnp.zeros((HALVES, 2 * WIDE, LANES), f32)
        for i in range(size):
            g_s[:, (i * 8 + 6) * WIDE:(i * 8 + 8) * WIDE] = zero

    @pl.when(k == size - 1)
    def _():
        def one_row(r, carry):
            for q in range(COLS):
                for h in range(2):
                    top, rest = split(g_s[2 * r + h, pl.ds(q, 8 * size, stride=WIDE)])
                    ready[r * COLS + q, :8 * size, h * LANES:(h + 1) * LANES] = top
                    ready[r * COLS + q, 8 * size:, h * LANES:(h + 1) * LANES] = rest
            return carry

        lax.fori_loop(0, ROWS, one_row, 0)


def smooth(chunk, even, taps, own, near_a, near_b, far_a, far_b):
    size, start = SIZES[chunk], STARTS[chunk]
    half = (HALVES, COLS, LANES)
    two = pl.BlockSpec((2, 1) + half, lambda k: (0, k, 0, 0, 0))
    one = pl.BlockSpec((1,) + half, lambda k: (k, 0, 0, 0))
    return pl.pallas_call(
        functools.partial(smooth_kernel, size),
        name="smooth",
        grid=(size,),
        in_specs=[
            pl.BlockSpec(memory_space=SM),
            pl.BlockSpec((2 * LANES, 4 * LANES), lambda k: (0, 0)),
            pl.BlockSpec((2, 1) + half, lambda k: (0, start + k, 0, 0, 0)),
            two,
            two,
            one,
            one,
        ],
        out_specs=pl.BlockSpec((ROWS * COLS, 16 * size, 2 * LANES), lambda k: (0, 0, 0)),
        out_shape=jax.ShapeDtypeStruct((ROWS * COLS, 16 * size, 2 * LANES), bf16),
        scratch_shapes=[
            pltpu.VMEM((2, 4, HALVES * COLS, 2 * LANES), bf16),
            pltpu.VMEM((6, HALVES * COLS, LANES), f32),
            pltpu.VMEM((2, 6, HALVES * COLS, 2 * LANES), bf16),
            pltpu.VMEM((HALVES, size * 8 * WIDE, LANES), f32),
        ],
        compiler_params=pltpu.CompilerParams(vmem_limit_bytes=24 * MIB),
        cost_estimate=pl.CostEstimate(flops=10**9, bytes_accessed=4 * 10**6, transcendentals=0),
    )(even, taps, own, near_a, near_b, far_a, far_b)


def pick_kernel(cells, ready0, ready1, mixed, forces, got_s):
    def one_group(g, slot):
        first = pl.multiple_of(g * GROUP, GROUP)
        for b in range(GROUP):
            d = first + b
            table = table_of(*digits_of(cells[pl.ds(d, 1), :]), 16)
            rows = jnp.concatenate(
                [ready0[d, :32], ready1[d, :16], ready0[d, 32:], ready1[d, 16:]], axis=0
            )
            got = jnp.dot(rows, table, preferred_element_type=f32)
            got = got[:48] + got[48:]
            for t in range(4):
                got_s[slot, t, pl.ds(b, 48, stride=SLOT)] = got[:, t * LANES:(t + 1) * LANES]
        for t in range(4):
            lanes = slice(t * LANES, (t + 1) * LANES)
            upper = (cells[pl.ds(first, GROUP), lanes] & 1) == 1
            vs = [mixed[k, pl.ds(first, GROUP), lanes] for k in range(SPECIES)]
            for a in range(3):
                total = None
                for k in range(SPECIES):
                    row = (k * 8 + 2 * a) * SLOT
                    value = jnp.where(
                        upper, got_s[slot, t, row + SLOT:row + SLOT + GROUP], got_s[slot, t, row:row + GROUP]
                    )
                    total = vs[k] * value if total is None else total + vs[k] * value
                forces[a, pl.ds(first, GROUP), lanes] = total

    def four_groups(i, carry):
        for j in range(4):
            one_group(4 * i + j, j)
        return carry

    lax.fori_loop(0, ROWS * COLS // GROUP // 4, four_groups, 0)


def pick(cells, ready, mixed):
    return pl.pallas_call(
        pick_kernel,
        name="pick",
        in_specs=[pl.BlockSpec(memory_space=VM)] * 4,
        out_specs=pl.BlockSpec(memory_space=VM),
        out_shape=jax.ShapeDtypeStruct((3, ROWS * COLS, SLOTS), f32),
        scratch_shapes=[pltpu.VMEM((4, 4, 48 * SLOT, LANES), f32)],
        compiler_params=pltpu.CompilerParams(vmem_limit_bytes=24 * MIB),
        cost_estimate=pl.CostEstimate(flops=6 * 10**9, bytes_accessed=10**7, transcendentals=0),
    )(cells, *ready, mixed)


def body(send_cells, send_species, send_mix, send_counts, chi):
    axes = ("row", "col")
    count = lax.axis_size("row") * lax.axis_size("col")
    swap_a = [(i, i ^ 1) for i in range(count)]
    swap_b = [(i, (i + (1 if i % 2 else -1)) % count) for i in range(count)]
    odd = lax.axis_index("col") % 2
    even = (1 - odd).reshape(1)
    chis = 0.5 * (chi + chi.T) * (1.0 - jnp.eye(SPECIES, dtype=f32))
    mix_matrix = -0.5 * (chis + 1.0)
    cells, species, mix, counts = send_cells[0], send_species[0], send_mix[0], send_counts[0]
    own, *sent = deposit(counts, cells, species, mix)
    taps = tap_matrices()
    ready = []
    for chunk in range(len(SIZES)):
        def swap(value, pairs):
            return lax.ppermute(value, axes, pairs)

        near_a = swap(sent[chunk], swap_a)
        near_b = swap(sent[chunk], swap_b)
        far_a = swap(lax.dynamic_index_in_dim(near_b, 1 - odd, 0, False), swap_a)
        far_b = swap(lax.dynamic_index_in_dim(near_a, odd, 0, False), swap_b)
        ready.append(smooth(chunk, even, taps, own, near_a, near_b, far_a, far_b))
    mixed = mixing(counts, mix_matrix, species, mix)
    return pick(cells, ready, mixed)[None]


def solution(mesh):
    return jax.shard_map(
        body,
        mesh=mesh,
        in_specs=(
            P(("row", "col"), None, None),
            P(("row", "col"), None, None),
            P(("row", "col"), None, None, None),
            P(("row", "col"), None),
            P(),
        ),
        out_specs=P(("row", "col"), None, None, None),
        check_vma=False,
    )
```

```python
import functools

import jax
import jax.numpy as jnp
import numpy as np
from jax import lax
from jax.experimental import pallas as pl
from jax.experimental.pallas import tpu as pltpu
from jax.sharding import PartitionSpec as P


SPECIES = 6
ROWS = 8
COLS = 16
HALVES = 16
LANES = 128
SLOTS = 512
SIZES = (4, 2)
STARTS = (0, 4)
GROUP = 8
WIDE = COLS + 1
SLOT = GROUP + 1
MIB = 1 << 20
LIMIT = 24

raw_taps = (0.1353352832366127, 0.6065306597126334, 1.0)
tap_total = raw_taps[2] + 2.0 * (raw_taps[0] + raw_taps[1])
T2, T1, T0 = (t / tap_total for t in raw_taps)

f32 = jnp.float32
bf16 = jnp.bfloat16


def digits_of(row):
    wide = jnp.broadcast_to(row, (8, SLOTS))
    low = (wide >> 8) & 15
    ids = lax.broadcasted_iota(jnp.int32, (8, SLOTS), 0)
    inner = jnp.concatenate(
        [jnp.where(low == ids, 1.0, 0.0), jnp.where(low == ids + 8, 1.0, 0.0)], axis=0
    ).astype(bf16)
    high = (wide >> 12).astype(f32)
    return inner, jnp.concatenate([high, high], axis=0).astype(bf16)


def table_of(inner, outer, count):
    none = jnp.zeros((16, SLOTS), bf16)
    return jnp.concatenate(
        [jnp.where(outer == jnp.full((16, SLOTS), i, bf16), inner, none) for i in range(count)], axis=0
    )


def weights_of(limit, t, rows, species, mix):
    part = pl.ds(t * LANES, LANES)
    lane = lax.broadcasted_iota(jnp.int32, (COLS, LANES), 1)
    valid = (lane + t * LANES) < limit
    kind = species[rows, part]
    found = []
    for k in range(SPECIES):
        w = jnp.where(kind == k, 1.0, 0.0) + mix[k, rows, part].astype(f32)
        found.append(jnp.where(valid, w, 0.0).astype(bf16).astype(f32))
    return found


def limits_of(counts, first):
    rows = lax.broadcasted_iota(jnp.int32, (COLS, LANES), 0)
    limit = jnp.zeros((COLS, LANES), jnp.int32)
    for i in range(COLS):
        limit = jnp.where(rows == i, counts[first + i], limit)
    return limit


def deposit_kernel(counts_far, cells_far, species_far, mix_far, own_far, sent0_far, sent1_far,
                   counts, cells, species, mix, own, sent0, sent1, w_s, d_s, sems, out_sems, count_sem):
    sent = [(sent0, k) for k in range(SIZES[0])] + [(sent1, k) for k in range(SIZES[1])]

    def fetches(r):
        rows = pl.ds(pl.multiple_of(r * COLS, COLS), COLS)
        return (
            pltpu.make_async_copy(cells_far.at[rows], cells.at[rows], sems.at[0, r]),
            pltpu.make_async_copy(species_far.at[rows], species.at[rows], sems.at[1, r]),
            pltpu.make_async_copy(mix_far.at[:, rows], mix.at[:, rows], sems.at[2, r]),
        )

    def results(r):
        part = pl.ds(2 * r, 2)
        return [
            pltpu.make_async_copy(near.at[:, :, part], far.at[:, :, part], out_sems.at[i, r])
            for i, (near, far) in enumerate(((sent0, sent0_far), (sent1, sent1_far), (own, own_far)))
        ]

    count_copy = pltpu.make_async_copy(counts_far, counts, count_sem)
    count_copy.start()
    for r in range(ROWS):
        for copy in fetches(r):
            copy.start()
    zero = jnp.zeros((COLS, LANES), f32)
    for t in range(4):
        for k in (6, 7):
            w_s[t, k * WIDE:k * WIDE + COLS] = zero
            w_s[t, (8 + k) * WIDE:(8 + k) * WIDE + COLS] = zero

    count_copy.wait()

    def one_row(r, carry):
        for copy in fetches(r):
            copy.wait()
        first = pl.multiple_of(r * COLS, COLS)
        rows = pl.ds(first, COLS)
        limit = limits_of(counts, first)
        for t in range(4):
            upper = (cells[rows, pl.ds(t * LANES, LANES)] & 1) == 1
            for k, w in enumerate(weights_of(limit, t, rows, species, mix)):
                w_s[t, k * WIDE:k * WIDE + COLS] = jnp.where(upper, 0.0, w)
                w_s[t, (8 + k) * WIDE:(8 + k) * WIDE + COLS] = jnp.where(upper, w, 0.0)
        for b in range(COLS):
            inner, outer = digits_of(cells[pl.ds(first + b, 1), :])
            second = outer > 7.5
            table = table_of(inner, jnp.where(second, outer - 8.0, outer), 8)
            w = jnp.concatenate([w_s[t, pl.ds(b, 16, stride=WIDE)] for t in range(4)], axis=1).astype(bf16)
            none = jnp.zeros((16, SLOTS), bf16)
            halves = jnp.concatenate([jnp.where(second, none, w), jnp.where(second, w, none)], axis=0)
            dens = lax.dot_general(halves, table, (((1,), (1,)), ((), ())), preferred_element_type=f32)
            d_s[0, pl.ds(b, 16, stride=WIDE)] = dens[:16]
            d_s[1, pl.ds(b, 16, stride=WIDE)] = dens[16:]
        for z in range(2):
            for k in range(SPECIES):
                for h in range(2):
                    value = d_s[h, (z * 8 + k) * WIDE:(z * 8 + k) * WIDE + COLS]
                    own[z, k, 2 * r + h] = value
                    sent[k][0][z, sent[k][1], 2 * r + h] = value.astype(bf16)
        for copy in results(r):
            copy.start()
        return carry

    lax.fori_loop(0, ROWS, one_row, 0)
    for r in range(ROWS):
        for copy in results(r):
            copy.wait()


VM = pltpu.MemorySpace.VMEM
SM = pltpu.MemorySpace.SMEM
FAR = pltpu.MemorySpace.HBM


def deposit(counts, cells, species, mix):
    half = (HALVES, COLS, LANES)
    return pl.pallas_call(
        deposit_kernel,
        name="deposit",
        in_specs=[pl.BlockSpec(memory_space=FAR)] * 4,
        out_specs=[pl.BlockSpec(memory_space=FAR)] * 3,
        scratch_shapes=[
            pltpu.SMEM((ROWS * COLS,), jnp.int32),
            pltpu.VMEM((ROWS * COLS, SLOTS), jnp.int32),
            pltpu.VMEM((ROWS * COLS, SLOTS), jnp.int32),
            pltpu.VMEM((SPECIES, ROWS * COLS, SLOTS), bf16),
            pltpu.VMEM((2, SPECIES) + half, f32),
            pltpu.VMEM((2, SIZES[0]) + half, bf16),
            pltpu.VMEM((2, SIZES[1]) + half, bf16),
            pltpu.VMEM((4, 16 * WIDE, LANES), f32),
            pltpu.VMEM((2, 16 * WIDE, LANES), f32),
            pltpu.SemaphoreType.DMA((3, ROWS)),
            pltpu.SemaphoreType.DMA((3, ROWS)),
            pltpu.SemaphoreType.DMA,
        ],
        out_shape=[jax.ShapeDtypeStruct((2, SPECIES) + half, f32)]
        + [jax.ShapeDtypeStruct((2, size) + half, bf16) for size in SIZES],
        compiler_params=pltpu.CompilerParams(vmem_limit_bytes=LIMIT * MIB),
        cost_estimate=pl.CostEstimate(flops=10**9, bytes_accessed=5 * 10**6, transcendentals=0),
    )(*(pltpu.with_memory_space_constraint(v, FAR) for v in (counts, cells, species, mix)))


def mixing_kernel(counts, mix_matrix, species, mix, mixed):
    def one_row(r, carry):
        first = pl.multiple_of(r * COLS, COLS)
        rows = pl.ds(first, COLS)
        limit = limits_of(counts, first)
        for t in range(4):
            ws = weights_of(limit, t, rows, species, mix)
            for l in range(SPECIES):
                v = mix_matrix[l, 0] * ws[0]
                for k in range(1, SPECIES):
                    v = v + mix_matrix[l, k] * ws[k]
                mixed[l, rows, t * LANES:(t + 1) * LANES] = v
        return carry

    lax.fori_loop(0, ROWS, one_row, 0)


def mixing(counts, mix_matrix, species, mix):
    return pl.pallas_call(
        mixing_kernel,
        name="mixing",
        in_specs=[pl.BlockSpec(memory_space=SM)] * 2 + [pl.BlockSpec(memory_space=VM)] * 2,
        out_specs=pl.BlockSpec(memory_space=VM),
        out_shape=jax.ShapeDtypeStruct((SPECIES, ROWS * COLS, SLOTS), f32),
        compiler_params=pltpu.CompilerParams(vmem_limit_bytes=12 * MIB),
        cost_estimate=pl.CostEstimate(flops=10**9, bytes_accessed=4 * 10**6, transcendentals=0),
    )(counts, mix_matrix, species, mix)


def scaled_taps():
    smooth_scale, slope_scale = 1.6396387, 1.5596421
    smooth_taps = {0: T0, 1: T1, -1: T1, 2: T2, -2: T2}
    slope_taps = {1: 0.5 * (T0 - T2), 2: 0.5 * T1, 3: 0.5 * T2}
    slope_taps.update({-j: -v for j, v in slope_taps.items()})
    return (
        {j: smooth_scale * v for j, v in smooth_taps.items()},
        {j: slope_scale * v for j, v in slope_taps.items()},
        smooth_scale,
        slope_scale,
    )


SMOOTH, SLOPE, SMOOTH_SCALE, SLOPE_SCALE = scaled_taps()


def tap_matrices():
    lane = np.arange(LANES)
    x, y = lane // 16, lane % 16
    results = []
    for main, other, extent in ((y, x, 16), (x, y, 8)):
        source = np.concatenate([main, np.where(main < extent // 2, main + extent, main - extent)])
        same = np.concatenate([other, other])[:, None] == other[None, :]
        gap = source[:, None] - main[None, :]
        for taps in (SMOOTH, SLOPE):
            matrix = np.zeros((2 * LANES, LANES), np.float32)
            for j, value in taps.items():
                matrix += np.where(same & (gap == j), np.float32(value), np.float32(0))
            results.append(matrix)
    return jnp.asarray(np.concatenate(results, axis=1)).astype(bf16)


def split(v):
    top = v.astype(bf16)
    return top, (v - top.astype(f32)).astype(bf16)


def smooth_kernel(size, planes, even_ref, taps, own, near_a, near_b, *refs):
    flat, slopes = 0 in planes, 2 in planes
    far_a, far_b = refs[:2] if slopes else (None, None)
    ready, x_s, y_s, w_s, g_s = refs[-5:]
    outs = (0, 1, 2, 3) * flat + (4, 5) * slopes
    rows_of = rows_per_species(planes)
    k = pl.program_id(0)
    lane = lax.broadcasted_iota(jnp.int32, (COLS, LANES), 1)
    col = lane & 15
    lower = lane.astype(f32).astype(bf16) < 64
    cu = 1.0 / (SMOOTH_SCALE * SLOPE_SCALE)
    cz = 0.5 / (SMOOTH_SCALE * SMOOTH_SCALE)
    even = jnp.full((COLS, LANES), even_ref[0], jnp.int32) == 1
    for h in range(HALVES):
        def sides(a, b):
            a, b = a.astype(f32), b.astype(f32)
            return jnp.where(even, b, a), jnp.where(even, a, b)

        a, r0 = sides(near_a[0, 0, h], near_b[0, 0, h])
        b, r1 = sides(near_a[1, 0, h], near_b[1, 0, h])
        o0 = own[0, 0, h]
        o1 = own[1, 0, h]
        u0 = T2 * (a + r0) + T1 * (b + o1) + T0 * o0
        u1 = T2 * (b + r1) + T1 * (o0 + r0) + T0 * o1
        values = {}
        if flat:
            values.update({0: cu * u0, 1: cu * u1})
        if slopes:
            l2, r2 = sides(far_a[0, h], far_b[0, h])
            um = T2 * (l2 + o1) + T1 * (a + o0) + T0 * b
            up = T2 * (o0 + r2) + T1 * (o1 + r1) + T0 * r0
            values.update({2: cz * (u1 - um), 3: cz * (up - u0)})
        for i, plane in enumerate(planes):
            v = values[plane]
            around = jnp.where(col < 8, pltpu.roll(v, COLS - 1, 0), pltpu.roll(v, 1, 0))
            for part, value in ((0, v), (1, around)):
                for level, piece in enumerate(split(value)):
                    x_s[level, i, h * COLS:(h + 1) * COLS, part * LANES:(part + 1) * LANES] = piece
    for i, plane in enumerate(planes):
        table = taps[:, :2 * LANES] if plane < 2 else taps[:, :LANES]
        out = jnp.dot(x_s[0, i], table, preferred_element_type=f32) + jnp.dot(
            x_s[1, i], table, preferred_element_type=f32
        )
        if plane < 2:
            y_s[outs.index(plane)] = out[:, :LANES]
            y_s[outs.index(2 + plane)] = out[:, LANES:]
        else:
            y_s[outs.index(2 + plane)] = out
    for i, p in enumerate(outs):
        pieces = [split(y_s[i, h * COLS:(h + 1) * COLS]) for h in range(HALVES)]
        for h in range(HALVES):
            rows = slice(h * COLS, (h + 1) * COLS)
            for level in range(2):
                w_s[level, i, rows, :LANES] = pieces[h][level]
                w_s[level, i, rows, LANES:] = jnp.where(
                    lower, pieces[(h + 1) % HALVES][level], pieces[(h - 1) % HALVES][level]
                )
        table = taps[:, 3 * LANES:] if p < 2 else taps[:, 2 * LANES:3 * LANES]
        out = jnp.dot(w_s[0, i], table, preferred_element_type=f32) + jnp.dot(
            w_s[1, i], table, preferred_element_type=f32
        )
        for h in range(HALVES):
            g_s[h, pl.ds((k * rows_of + i) * WIDE, COLS)] = out[h * COLS:(h + 1) * COLS]

    if rows_of > len(outs):
        @pl.when(k == 0)
        def _():
            zero = jnp.zeros((HALVES, (rows_of - len(outs)) * WIDE, LANES), f32)
            for i in range(size):
                g_s[:, (i * rows_of + len(outs)) * WIDE:(i + 1) * rows_of * WIDE] = zero

    @pl.when(k == size - 1)
    def _():
        count = rows_of * size

        def one_row(r, carry):
            for q in range(COLS):
                for h in range(2):
                    value = g_s[2 * r + h, pl.ds(q, count, stride=WIDE)]
                    top = value.astype(bf16).astype(f32)
                    ready[r * COLS + q, :, h * LANES:(h + 1) * LANES] = jnp.concatenate(
                        [top, value - top], axis=0
                    ).astype(bf16)
            return carry

        lax.fori_loop(0, ROWS, one_row, 0)


def rows_per_species(planes):
    return {(0, 1): 4, (2, 3): 2, (0, 1, 2, 3): 8}[planes]


def smooth(chunk, planes, even, taps, own, *halos):
    size, start = SIZES[chunk], STARTS[chunk]
    half = (HALVES, COLS, LANES)
    count = rows_per_species(planes) * size
    outs = sum(2 if plane < 2 else 1 for plane in planes)
    two = pl.BlockSpec((2, 1) + half, lambda k: (0, k, 0, 0, 0))
    one = pl.BlockSpec((1,) + half, lambda k: (k, 0, 0, 0))
    return pl.pallas_call(
        functools.partial(smooth_kernel, size, planes),
        name="smooth",
        grid=(size,),
        in_specs=[
            pl.BlockSpec(memory_space=SM),
            pl.BlockSpec((2 * LANES, 4 * LANES), lambda k: (0, 0)),
            pl.BlockSpec((2, 1) + half, lambda k: (0, start + k, 0, 0, 0)),
        ]
        + ([two, two, one, one] if 2 in planes else [two, two]),
        out_specs=pl.BlockSpec((ROWS * COLS, 2 * count, 2 * LANES), lambda k: (0, 0, 0)),
        out_shape=jax.ShapeDtypeStruct((ROWS * COLS, 2 * count, 2 * LANES), bf16),
        scratch_shapes=[
            pltpu.VMEM((2, len(planes), HALVES * COLS, 2 * LANES), bf16),
            pltpu.VMEM((outs, HALVES * COLS, LANES), f32),
            pltpu.VMEM((2, outs, HALVES * COLS, 2 * LANES), bf16),
            pltpu.VMEM((HALVES, count * WIDE, LANES), f32),
        ],
        compiler_params=pltpu.CompilerParams(vmem_limit_bytes=24 * MIB),
        cost_estimate=pl.CostEstimate(flops=10**9, bytes_accessed=4 * 10**6, transcendentals=0),
    )(even, taps, own, *halos)


FLAT = (0, 1)
SLOPES = (2, 3)


def row_of(k, p):
    if k < 4:
        return k * 4 + p if p < 4 else 16 + k * 2 + p - 4
    return 24 + (k - 4) * 8 + p


def pick_kernel(cells, flat0, slopes0, ready1, mixed, forces, got_s):
    def one_group(g, slot):
        first = pl.multiple_of(g * GROUP, GROUP)
        for b in range(GROUP):
            d = first + b
            table = table_of(*digits_of(cells[pl.ds(d, 1), :]), 16)
            rows = jnp.concatenate([flat0[d], slopes0[d], ready1[d]], axis=0)
            got = jnp.dot(rows, table, preferred_element_type=f32)
            got = jnp.concatenate(
                [got[:16] + got[16:32], got[32:40] + got[40:48], got[48:64] + got[64:]], axis=0
            )
            for t in range(4):
                got_s[slot, t, pl.ds(b, 40, stride=SLOT)] = got[:, t * LANES:(t + 1) * LANES]
        for t in range(4):
            lanes = slice(t * LANES, (t + 1) * LANES)
            upper = (cells[pl.ds(first, GROUP), lanes] & 1) == 1
            vs = [mixed[k, pl.ds(first, GROUP), lanes] for k in range(SPECIES)]
            for a in range(3):
                total = None
                for k in range(SPECIES):
                    low, high = (
                        got_s[slot, t, pl.ds(row_of(k, 2 * a + z) * SLOT, GROUP)] for z in range(2)
                    )
                    value = jnp.where(upper, high, low)
                    total = vs[k] * value if total is None else total + vs[k] * value
                forces[a, pl.ds(first, GROUP), lanes] = total

    def four_groups(i, carry):
        for j in range(4):
            one_group(4 * i + j, j)
        return carry

    lax.fori_loop(0, ROWS * COLS // GROUP // 4, four_groups, 0)


def pick(cells, ready, mixed):
    return pl.pallas_call(
        pick_kernel,
        name="pick",
        in_specs=[pl.BlockSpec(memory_space=VM)] * 5,
        out_specs=pl.BlockSpec(memory_space=VM),
        out_shape=jax.ShapeDtypeStruct((3, ROWS * COLS, SLOTS), f32),
        scratch_shapes=[pltpu.VMEM((4, 4, 40 * SLOT, LANES), f32)],
        compiler_params=pltpu.CompilerParams(vmem_limit_bytes=24 * MIB),
        cost_estimate=pl.CostEstimate(flops=6 * 10**9, bytes_accessed=10**7, transcendentals=0),
    )(cells, *ready, mixed)


def body(send_cells, send_species, send_mix, send_counts, chi):
    axes = ("row", "col")
    count = lax.axis_size("row") * lax.axis_size("col")
    swap_a = [(i, i ^ 1) for i in range(count)]
    swap_b = [(i, (i + (1 if i % 2 else -1)) % count) for i in range(count)]
    odd = lax.axis_index("col") % 2
    even = (1 - odd).reshape(1)
    chis = 0.5 * (chi + chi.T) * (1.0 - jnp.eye(SPECIES, dtype=f32))
    mix_matrix = -0.5 * (chis + 1.0)
    cells, species, mix, counts = send_cells[0], send_species[0], send_mix[0], send_counts[0]
    own, *sent = deposit(counts, cells, species, mix)
    taps = tap_matrices()
    ready = []
    for chunk in range(len(SIZES)):
        def swap(value, pairs):
            return lax.ppermute(value, axes, pairs)

        near_a = swap(sent[chunk], swap_a)
        near_b = swap(sent[chunk], swap_b)
        far_a = swap(lax.dynamic_index_in_dim(near_b, 1 - odd, 0, False), swap_a)
        far_b = swap(lax.dynamic_index_in_dim(near_a, odd, 0, False), swap_b)
        if chunk == 0:
            ready.append(smooth(chunk, FLAT, even, taps, own, near_a, near_b))
            ready.append(smooth(chunk, SLOPES, even, taps, own, near_a, near_b, far_a, far_b))
        else:
            ready.append(smooth(chunk, FLAT + SLOPES, even, taps, own, near_a, near_b, far_a, far_b))
    mixed = mixing(counts, mix_matrix, species, mix)
    return pick(cells, ready, mixed)[None]


def solution(mesh):
    return jax.shard_map(
        body,
        mesh=mesh,
        in_specs=(
            P(("row", "col"), None, None),
            P(("row", "col"), None, None),
            P(("row", "col"), None, None, None),
            P(("row", "col"), None),
            P(),
        ),
        out_specs=P(("row", "col"), None, None, None),
        check_vma=False,
    )
```

```python
import functools

import jax
import jax.numpy as jnp
import numpy as np
from jax import lax
from jax.experimental import pallas as pl
from jax.experimental.pallas import tpu as pltpu
from jax.sharding import PartitionSpec as P


SPECIES = 6
ROWS = 8
COLS = 16
HALVES = 16
LANES = 128
SLOTS = 512
GROUP = 8
WIDE = COLS + 1
SLOT = GROUP + 1
MIB = 1 << 20
LIMIT = 24

raw_taps = (0.1353352832366127, 0.6065306597126334, 1.0)
tap_total = raw_taps[2] + 2.0 * (raw_taps[0] + raw_taps[1])
T2, T1, T0 = (t / tap_total for t in raw_taps)

f32 = jnp.float32
bf16 = jnp.bfloat16


def digits_of(row):
    wide = jnp.broadcast_to(row, (8, SLOTS))
    low = (wide >> 8) & 15
    ids = lax.broadcasted_iota(jnp.int32, (8, SLOTS), 0)
    inner = jnp.concatenate(
        [jnp.where(low == ids, 1.0, 0.0), jnp.where(low == ids + 8, 1.0, 0.0)], axis=0
    ).astype(bf16)
    high = (wide >> 12).astype(f32)
    return inner, jnp.concatenate([high, high], axis=0).astype(bf16)


def table_of(inner, outer, count):
    none = jnp.zeros((16, SLOTS), bf16)
    return jnp.concatenate(
        [jnp.where(outer == jnp.full((16, SLOTS), i, bf16), inner, none) for i in range(count)], axis=0
    )


def weights_of(limit, t, rows, species, mix):
    part = pl.ds(t * LANES, LANES)
    lane = lax.broadcasted_iota(jnp.int32, (COLS, LANES), 1)
    valid = (lane + t * LANES) < limit
    kind = species[rows, part]
    found = []
    for k in range(SPECIES):
        w = jnp.where(kind == k, 1.0, 0.0) + mix[k, rows, part].astype(f32)
        found.append(jnp.where(valid, w, 0.0).astype(bf16).astype(f32))
    return found


def limits_of(counts, first):
    rows = lax.broadcasted_iota(jnp.int32, (COLS, LANES), 0)
    limit = jnp.zeros((COLS, LANES), jnp.int32)
    for i in range(COLS):
        limit = jnp.where(rows == i, counts[first + i], limit)
    return limit


def deposit_kernel(counts_far, cells_far, species_far, mix_far, own_far, sent_far,
                   counts, cells, species, mix, own, sent, w_s, d_s, sems, out_sems, count_sem):

    def fetches(r):
        rows = pl.ds(pl.multiple_of(r * COLS, COLS), COLS)
        return (
            pltpu.make_async_copy(cells_far.at[rows], cells.at[rows], sems.at[0, r]),
            pltpu.make_async_copy(species_far.at[rows], species.at[rows], sems.at[1, r]),
            pltpu.make_async_copy(mix_far.at[:, rows], mix.at[:, rows], sems.at[2, r]),
        )

    def results(r):
        part = pl.ds(2 * r, 2)
        return [
            pltpu.make_async_copy(near.at[:, :, part], far.at[:, :, part], out_sems.at[i, r])
            for i, (near, far) in enumerate(((sent, sent_far), (own, own_far)))
        ]

    count_copy = pltpu.make_async_copy(counts_far, counts, count_sem)
    count_copy.start()
    for r in range(ROWS):
        for copy in fetches(r):
            copy.start()
    zero = jnp.zeros((COLS, LANES), f32)
    for t in range(4):
        for k in (6, 7):
            w_s[t, k * WIDE:k * WIDE + COLS] = zero
            w_s[t, (8 + k) * WIDE:(8 + k) * WIDE + COLS] = zero

    count_copy.wait()

    def one_row(r, carry):
        for copy in fetches(r):
            copy.wait()
        first = pl.multiple_of(r * COLS, COLS)
        rows = pl.ds(first, COLS)
        limit = limits_of(counts, first)
        for t in range(4):
            upper = (cells[rows, pl.ds(t * LANES, LANES)] & 1) == 1
            for k, w in enumerate(weights_of(limit, t, rows, species, mix)):
                w_s[t, k * WIDE:k * WIDE + COLS] = jnp.where(upper, 0.0, w)
                w_s[t, (8 + k) * WIDE:(8 + k) * WIDE + COLS] = jnp.where(upper, w, 0.0)
        for b in range(COLS):
            inner, outer = digits_of(cells[pl.ds(first + b, 1), :])
            second = outer > 7.5
            table = table_of(inner, jnp.where(second, outer - 8.0, outer), 8)
            w = jnp.concatenate([w_s[t, pl.ds(b, 16, stride=WIDE)] for t in range(4)], axis=1).astype(bf16)
            none = jnp.zeros((16, SLOTS), bf16)
            halves = jnp.concatenate([jnp.where(second, none, w), jnp.where(second, w, none)], axis=0)
            dens = lax.dot_general(halves, table, (((1,), (1,)), ((), ())), preferred_element_type=f32)
            d_s[0, pl.ds(b, 16, stride=WIDE)] = dens[:16]
            d_s[1, pl.ds(b, 16, stride=WIDE)] = dens[16:]
        for z in range(2):
            for k in range(SPECIES):
                for h in range(2):
                    value = d_s[h, (z * 8 + k) * WIDE:(z * 8 + k) * WIDE + COLS]
                    own[z, k, 2 * r + h] = value
                    sent[z, k, 2 * r + h] = value.astype(bf16)
        for copy in results(r):
            copy.start()
        return carry

    lax.fori_loop(0, ROWS, one_row, 0)
    for r in range(ROWS):
        for copy in results(r):
            copy.wait()


VM = pltpu.MemorySpace.VMEM
SM = pltpu.MemorySpace.SMEM
FAR = pltpu.MemorySpace.HBM


def deposit(counts, cells, species, mix):
    half = (HALVES, COLS, LANES)
    return pl.pallas_call(
        deposit_kernel,
        name="deposit",
        in_specs=[pl.BlockSpec(memory_space=FAR)] * 4,
        out_specs=[pl.BlockSpec(memory_space=FAR)] * 2,
        scratch_shapes=[
            pltpu.SMEM((ROWS * COLS,), jnp.int32),
            pltpu.VMEM((ROWS * COLS, SLOTS), jnp.int32),
            pltpu.VMEM((ROWS * COLS, SLOTS), jnp.int32),
            pltpu.VMEM((SPECIES, ROWS * COLS, SLOTS), bf16),
            pltpu.VMEM((2, SPECIES) + half, f32),
            pltpu.VMEM((2, SPECIES) + half, bf16),
            pltpu.VMEM((4, 16 * WIDE, LANES), f32),
            pltpu.VMEM((2, 16 * WIDE, LANES), f32),
            pltpu.SemaphoreType.DMA((3, ROWS)),
            pltpu.SemaphoreType.DMA((2, ROWS)),
            pltpu.SemaphoreType.DMA,
        ],
        out_shape=[jax.ShapeDtypeStruct((2, SPECIES) + half, dtype) for dtype in (f32, bf16)],
        compiler_params=pltpu.CompilerParams(vmem_limit_bytes=LIMIT * MIB),
        cost_estimate=pl.CostEstimate(flops=10**9, bytes_accessed=5 * 10**6, transcendentals=0),
    )(*(pltpu.with_memory_space_constraint(v, FAR) for v in (counts, cells, species, mix)))


def mixing_kernel(counts, mix_matrix, species, mix, mixed):
    def one_row(r, carry):
        first = pl.multiple_of(r * COLS, COLS)
        rows = pl.ds(first, COLS)
        limit = limits_of(counts, first)
        for t in range(4):
            ws = weights_of(limit, t, rows, species, mix)
            for l in range(SPECIES):
                v = mix_matrix[l, 0] * ws[0]
                for k in range(1, SPECIES):
                    v = v + mix_matrix[l, k] * ws[k]
                mixed[l, rows, t * LANES:(t + 1) * LANES] = v
        return carry

    lax.fori_loop(0, ROWS, one_row, 0)


def mixing(counts, mix_matrix, species, mix):
    return pl.pallas_call(
        mixing_kernel,
        name="mixing",
        in_specs=[pl.BlockSpec(memory_space=SM)] * 2 + [pl.BlockSpec(memory_space=VM)] * 2,
        out_specs=pl.BlockSpec(memory_space=VM),
        out_shape=jax.ShapeDtypeStruct((SPECIES, ROWS * COLS, SLOTS), f32),
        compiler_params=pltpu.CompilerParams(vmem_limit_bytes=12 * MIB),
        cost_estimate=pl.CostEstimate(flops=10**9, bytes_accessed=4 * 10**6, transcendentals=0),
    )(counts, mix_matrix, species, mix)


def scaled_taps():
    smooth_scale, slope_scale = 1.6396387, 1.5596421
    smooth_taps = {0: T0, 1: T1, -1: T1, 2: T2, -2: T2}
    slope_taps = {1: 0.5 * (T0 - T2), 2: 0.5 * T1, 3: 0.5 * T2}
    slope_taps.update({-j: -v for j, v in slope_taps.items()})
    return (
        {j: smooth_scale * v for j, v in smooth_taps.items()},
        {j: slope_scale * v for j, v in slope_taps.items()},
        smooth_scale,
        slope_scale,
    )


SMOOTH, SLOPE, SMOOTH_SCALE, SLOPE_SCALE = scaled_taps()


def tap_matrices():
    lane = np.arange(LANES)
    x, y = lane // 16, lane % 16
    results = []
    for main, other, extent in ((y, x, 16), (x, y, 8)):
        source = np.concatenate([main, np.where(main < extent // 2, main + extent, main - extent)])
        same = np.concatenate([other, other])[:, None] == other[None, :]
        gap = source[:, None] - main[None, :]
        for taps in (SMOOTH, SLOPE):
            matrix = np.zeros((2 * LANES, LANES), np.float32)
            for j, value in taps.items():
                matrix += np.where(same & (gap == j), np.float32(value), np.float32(0))
            results.append(matrix)
    return jnp.asarray(np.concatenate(results, axis=1)).astype(bf16)


def split(v):
    top = v.astype(bf16)
    return top, (v - top.astype(f32)).astype(bf16)


def smooth_kernel(planes, even_ref, taps, own, near_a, near_b, *refs):
    flat, slopes = 0 in planes, 2 in planes
    far_a, far_b = refs[:2] if slopes else (None, None)
    ready, x_s, y_s, w_s, g_s = refs[-5:]
    outs = (0, 1, 2, 3) * flat + (4, 5) * slopes
    rows_of, count = ROWS_OF[planes]
    k = pl.program_id(0)
    lane = lax.broadcasted_iota(jnp.int32, (COLS, LANES), 1)
    col = lane & 15
    lower = lane.astype(f32).astype(bf16) < 64
    cu = 1.0 / (SMOOTH_SCALE * SLOPE_SCALE)
    cz = 0.5 / (SMOOTH_SCALE * SMOOTH_SCALE)
    even = jnp.full((COLS, LANES), even_ref[0], jnp.int32) == 1
    for h in range(HALVES):
        def sides(a, b):
            a, b = a.astype(f32), b.astype(f32)
            return jnp.where(even, b, a), jnp.where(even, a, b)

        a, r0 = sides(near_a[0, 0, h], near_b[0, 0, h])
        b, r1 = sides(near_a[1, 0, h], near_b[1, 0, h])
        o0 = own[0, 0, h]
        o1 = own[1, 0, h]
        u0 = T2 * (a + r0) + T1 * (b + o1) + T0 * o0
        u1 = T2 * (b + r1) + T1 * (o0 + r0) + T0 * o1
        values = {}
        if flat:
            values.update({0: cu * u0, 1: cu * u1})
        if slopes:
            l2, r2 = sides(far_a[0, h], far_b[0, h])
            um = T2 * (l2 + o1) + T1 * (a + o0) + T0 * b
            up = T2 * (o0 + r2) + T1 * (o1 + r1) + T0 * r0
            values.update({2: cz * (u1 - um), 3: cz * (up - u0)})
        for i, plane in enumerate(planes):
            v = values[plane]
            around = jnp.where(col < 8, pltpu.roll(v, COLS - 1, 0), pltpu.roll(v, 1, 0))
            for part, value in ((0, v), (1, around)):
                for level, piece in enumerate(split(value)):
                    x_s[level, i, h * COLS:(h + 1) * COLS, part * LANES:(part + 1) * LANES] = piece
    for i, plane in enumerate(planes):
        table = taps[:, :2 * LANES] if plane < 2 else taps[:, :LANES]
        out = jnp.dot(x_s[0, i], table, preferred_element_type=f32) + jnp.dot(
            x_s[1, i], table, preferred_element_type=f32
        )
        if plane < 2:
            y_s[outs.index(plane)] = out[:, :LANES]
            y_s[outs.index(2 + plane)] = out[:, LANES:]
        else:
            y_s[outs.index(2 + plane)] = out
    for i, p in enumerate(outs):
        pieces = [split(y_s[i, h * COLS:(h + 1) * COLS]) for h in range(HALVES)]
        for h in range(HALVES):
            rows = slice(h * COLS, (h + 1) * COLS)
            for level in range(2):
                w_s[level, i, rows, :LANES] = pieces[h][level]
                w_s[level, i, rows, LANES:] = jnp.where(
                    lower, pieces[(h + 1) % HALVES][level], pieces[(h - 1) % HALVES][level]
                )
        table = taps[:, 3 * LANES:] if p < 2 else taps[:, 2 * LANES:3 * LANES]
        out = jnp.dot(w_s[0, i], table, preferred_element_type=f32) + jnp.dot(
            w_s[1, i], table, preferred_element_type=f32
        )
        for h in range(HALVES):
            g_s[h, pl.ds((k * rows_of + i) * WIDE, COLS)] = out[h * COLS:(h + 1) * COLS]

    if count > rows_of * SPECIES:
        @pl.when(k == 0)
        def _():
            g_s[:, rows_of * SPECIES * WIDE:] = jnp.zeros(
                (HALVES, (count - rows_of * SPECIES) * WIDE, LANES), f32
            )

    @pl.when(k == SPECIES - 1)
    def _():
        def one_row(r, carry):
            for q in range(COLS):
                for h in range(2):
                    value = g_s[2 * r + h, pl.ds(q, count, stride=WIDE)]
                    top = value.astype(bf16).astype(f32)
                    ready[r * COLS + q, :, h * LANES:(h + 1) * LANES] = jnp.concatenate(
                        [top, value - top], axis=0
                    ).astype(bf16)
            return carry

        lax.fori_loop(0, ROWS, one_row, 0)


FLAT = (0, 1)
SLOPES = (2, 3)
ROWS_OF = {FLAT: (4, 24), SLOPES: (2, 16)}


def smooth(planes, even, taps, own, *halos):
    _, count = ROWS_OF[planes]
    half = (HALVES, COLS, LANES)
    outs = sum(2 if plane < 2 else 1 for plane in planes)
    two = pl.BlockSpec((2, 1) + half, lambda k: (0, k, 0, 0, 0))
    one = pl.BlockSpec((1,) + half, lambda k: (k, 0, 0, 0))
    return pl.pallas_call(
        functools.partial(smooth_kernel, planes),
        name="smooth",
        grid=(SPECIES,),
        in_specs=[
            pl.BlockSpec(memory_space=SM),
            pl.BlockSpec((2 * LANES, 4 * LANES), lambda k: (0, 0)),
            pl.BlockSpec((2, 1) + half, lambda k: (0, k, 0, 0, 0)),
        ]
        + ([two, two, one, one] if 2 in planes else [two, two]),
        out_specs=pl.BlockSpec((ROWS * COLS, 2 * count, 2 * LANES), lambda k: (0, 0, 0)),
        out_shape=jax.ShapeDtypeStruct((ROWS * COLS, 2 * count, 2 * LANES), bf16),
        scratch_shapes=[
            pltpu.VMEM((2, len(planes), HALVES * COLS, 2 * LANES), bf16),
            pltpu.VMEM((outs, HALVES * COLS, LANES), f32),
            pltpu.VMEM((2, outs, HALVES * COLS, 2 * LANES), bf16),
            pltpu.VMEM((HALVES, count * WIDE, LANES), f32),
        ],
        compiler_params=pltpu.CompilerParams(vmem_limit_bytes=24 * MIB),
        cost_estimate=pl.CostEstimate(flops=10**9, bytes_accessed=4 * 10**6, transcendentals=0),
    )(even, taps, own, *halos)


def row_of(k, p):
    return k * 4 + p if p < 4 else 24 + k * 2 + p - 4


def pick_kernel(cells, flat, slopes, mixed, forces, got_s):
    def one_group(g, slot):
        first = pl.multiple_of(g * GROUP, GROUP)
        for b in range(GROUP):
            d = first + b
            table = table_of(*digits_of(cells[pl.ds(d, 1), :]), 16)
            rows = jnp.concatenate([flat[d], slopes[d]], axis=0)
            got = jnp.dot(rows, table, preferred_element_type=f32)
            got = jnp.concatenate([got[:24] + got[24:48], got[48:64] + got[64:]], axis=0)
            for t in range(4):
                got_s[slot, t, pl.ds(b, 40, stride=SLOT)] = got[:, t * LANES:(t + 1) * LANES]
        for t in range(4):
            lanes = slice(t * LANES, (t + 1) * LANES)
            upper = (cells[pl.ds(first, GROUP), lanes] & 1) == 1
            vs = [mixed[k, pl.ds(first, GROUP), lanes] for k in range(SPECIES)]
            for a in range(3):
                total = None
                for k in range(SPECIES):
                    low, high = (
                        got_s[slot, t, pl.ds(row_of(k, 2 * a + z) * SLOT, GROUP)] for z in range(2)
                    )
                    value = jnp.where(upper, high, low)
                    total = vs[k] * value if total is None else total + vs[k] * value
                forces[a, pl.ds(first, GROUP), lanes] = total

    def four_groups(i, carry):
        for j in range(4):
            one_group(4 * i + j, j)
        return carry

    lax.fori_loop(0, ROWS * COLS // GROUP // 4, four_groups, 0)


def pick(cells, ready, mixed):
    return pl.pallas_call(
        pick_kernel,
        name="pick",
        in_specs=[pl.BlockSpec(memory_space=VM)] * 4,
        out_specs=pl.BlockSpec(memory_space=VM),
        out_shape=jax.ShapeDtypeStruct((3, ROWS * COLS, SLOTS), f32),
        scratch_shapes=[pltpu.VMEM((4, 4, 40 * SLOT, LANES), f32)],
        compiler_params=pltpu.CompilerParams(vmem_limit_bytes=24 * MIB),
        cost_estimate=pl.CostEstimate(flops=6 * 10**9, bytes_accessed=10**7, transcendentals=0),
    )(cells, *ready, mixed)


def body(send_cells, send_species, send_mix, send_counts, chi):
    axes = ("row", "col")
    count = lax.axis_size("row") * lax.axis_size("col")
    swap_a = [(i, i ^ 1) for i in range(count)]
    swap_b = [(i, (i + (1 if i % 2 else -1)) % count) for i in range(count)]
    odd = lax.axis_index("col") % 2
    even = (1 - odd).reshape(1)
    chis = 0.5 * (chi + chi.T) * (1.0 - jnp.eye(SPECIES, dtype=f32))
    mix_matrix = -0.5 * (chis + 1.0)
    cells, species, mix, counts = send_cells[0], send_species[0], send_mix[0], send_counts[0]
    own, sent = deposit(counts, cells, species, mix)
    taps = tap_matrices()

    def swap(value, pairs):
        return lax.ppermute(value, axes, pairs)

    near_a = swap(sent, swap_a)
    near_b = swap(sent, swap_b)
    far_a = swap(lax.dynamic_index_in_dim(near_b, 1 - odd, 0, False), swap_a)
    far_b = swap(lax.dynamic_index_in_dim(near_a, odd, 0, False), swap_b)
    flat = smooth(FLAT, even, taps, own, near_a, near_b)
    slopes = smooth(SLOPES, even, taps, own, near_a, near_b, far_a, far_b)
    mixed = mixing(counts, mix_matrix, species, mix)
    return pick(cells, (flat, slopes), mixed)[None]


def solution(mesh):
    return jax.shard_map(
        body,
        mesh=mesh,
        in_specs=(
            P(("row", "col"), None, None),
            P(("row", "col"), None, None),
            P(("row", "col"), None, None, None),
            P(("row", "col"), None),
            P(),
        ),
        out_specs=P(("row", "col"), None, None, None),
        check_vma=False,
    )
```

```python
import functools

import jax
import jax.numpy as jnp
import numpy as np
from jax import lax
from jax.experimental import pallas as pl
from jax.experimental.pallas import tpu as pltpu
from jax.sharding import PartitionSpec as P


SPECIES = 6
ROWS = 8
COLS = 16
HALVES = 16
LANES = 128
SLOTS = 512
GROUP = 8
WIDE = COLS + 1
SLOT = GROUP + 1
MIB = 1 << 20
LIMIT = 60

raw_taps = (0.1353352832366127, 0.6065306597126334, 1.0)
tap_total = raw_taps[2] + 2.0 * (raw_taps[0] + raw_taps[1])
T2, T1, T0 = (t / tap_total for t in raw_taps)

f32 = jnp.float32
bf16 = jnp.bfloat16


def digits_of(row):
    wide = jnp.broadcast_to(row, (8, SLOTS))
    low = (wide >> 8) & 15
    ids = lax.broadcasted_iota(jnp.int32, (8, SLOTS), 0)
    inner = jnp.concatenate(
        [jnp.where(low == ids, 1.0, 0.0), jnp.where(low == ids + 8, 1.0, 0.0)], axis=0
    ).astype(bf16)
    high = (wide >> 12).astype(f32)
    return inner, jnp.concatenate([high, high], axis=0).astype(bf16)


def table_of(inner, outer, count):
    none = jnp.zeros((16, SLOTS), bf16)
    return jnp.concatenate(
        [jnp.where(outer == jnp.full((16, SLOTS), i, bf16), inner, none) for i in range(count)], axis=0
    )


def weights_of(limit, t, rows, species, mix):
    part = pl.ds(t * LANES, LANES)
    lane = lax.broadcasted_iota(jnp.int32, (COLS, LANES), 1)
    valid = (lane + t * LANES) < limit
    kind = species[rows, part]
    found = []
    for k in range(SPECIES):
        w = jnp.where(kind == k, 1.0, 0.0) + mix[k, rows, part].astype(f32)
        found.append(jnp.where(valid, w, 0.0).astype(bf16).astype(f32))
    return found


def limits_of(counts, first):
    rows = lax.broadcasted_iota(jnp.int32, (COLS, LANES), 0)
    limit = jnp.zeros((COLS, LANES), jnp.int32)
    for i in range(COLS):
        limit = jnp.where(rows == i, counts[first + i], limit)
    return limit


def deposit_kernel(counts_far, cells_far, species_far, mix_far, own_far, first_far, second_far,
                   counts, cells, species, mix, own, first_s, second_s, w_s, d_s, sems, out_sems, count_sem):
    even = jnp.full((COLS, LANES), lax.axis_index("col") % 2, jnp.int32) == 0

    def fetches(r):
        rows = pl.ds(pl.multiple_of(r * COLS, COLS), COLS)
        return (
            pltpu.make_async_copy(cells_far.at[rows], cells.at[rows], sems.at[0, r]),
            pltpu.make_async_copy(species_far.at[rows], species.at[rows], sems.at[1, r]),
            pltpu.make_async_copy(mix_far.at[:, rows], mix.at[:, rows], sems.at[2, r]),
        )

    def results(r):
        part = pl.ds(2 * r, 2)
        return [
            pltpu.make_async_copy(near.at[:, part] if i < 2 else near.at[:, :, part],
                                  far.at[:, part] if i < 2 else far.at[:, :, part], out_sems.at[i, r])
            for i, (near, far) in enumerate(((first_s, first_far), (second_s, second_far), (own, own_far)))
        ]

    count_copy = pltpu.make_async_copy(counts_far, counts, count_sem)
    count_copy.start()
    for r in range(ROWS):
        for copy in fetches(r):
            copy.start()
    zero = jnp.zeros((COLS, LANES), f32)
    for t in range(4):
        for k in (6, 7):
            w_s[t, k * WIDE:k * WIDE + COLS] = zero
            w_s[t, (8 + k) * WIDE:(8 + k) * WIDE + COLS] = zero

    count_copy.wait()

    def one_row(r, carry):
        for copy in fetches(r):
            copy.wait()
        first = pl.multiple_of(r * COLS, COLS)
        rows = pl.ds(first, COLS)
        limit = limits_of(counts, first)
        for t in range(4):
            upper = (cells[rows, pl.ds(t * LANES, LANES)] & 1) == 1
            for k, w in enumerate(weights_of(limit, t, rows, species, mix)):
                w_s[t, k * WIDE:k * WIDE + COLS] = jnp.where(upper, 0.0, w)
                w_s[t, (8 + k) * WIDE:(8 + k) * WIDE + COLS] = jnp.where(upper, w, 0.0)
        for b in range(COLS):
            inner, outer = digits_of(cells[pl.ds(first + b, 1), :])
            second = outer > 7.5
            table = table_of(inner, jnp.where(second, outer - 8.0, outer), 8)
            w = jnp.concatenate([w_s[t, pl.ds(b, 16, stride=WIDE)] for t in range(4)], axis=1).astype(bf16)
            none = jnp.zeros((16, SLOTS), bf16)
            halves = jnp.concatenate([jnp.where(second, none, w), jnp.where(second, w, none)], axis=0)
            dens = lax.dot_general(halves, table, (((1,), (1,)), ((), ())), preferred_element_type=f32)
            d_s[0, pl.ds(b, 16, stride=WIDE)] = dens[:16]
            d_s[1, pl.ds(b, 16, stride=WIDE)] = dens[16:]
        for k in range(SPECIES):
            for h in range(2):
                low, high = (d_s[h, (z * 8 + k) * WIDE:(z * 8 + k) * WIDE + COLS] for z in range(2))
                own[0, k, 2 * r + h] = low
                own[1, k, 2 * r + h] = high
                first_s[k, 2 * r + h] = jnp.where(even, high, low).astype(bf16)
                second_s[k, 2 * r + h] = jnp.where(even, low, high).astype(bf16)
        for copy in results(r):
            copy.start()
        return carry

    lax.fori_loop(0, ROWS, one_row, 0)
    for r in range(ROWS):
        for copy in results(r):
            copy.wait()


VM = pltpu.MemorySpace.VMEM
SM = pltpu.MemorySpace.SMEM
FAR = pltpu.MemorySpace.HBM


def deposit(counts, cells, species, mix):
    half = (HALVES, COLS, LANES)
    return pl.pallas_call(
        deposit_kernel,
        name="deposit",
        in_specs=[pl.BlockSpec(memory_space=FAR)] * 4,
        out_specs=[pl.BlockSpec(memory_space=FAR)] * 3,
        scratch_shapes=[
            pltpu.SMEM((ROWS * COLS,), jnp.int32),
            pltpu.VMEM((ROWS * COLS, SLOTS), jnp.int32),
            pltpu.VMEM((ROWS * COLS, SLOTS), jnp.int32),
            pltpu.VMEM((SPECIES, ROWS * COLS, SLOTS), bf16),
            pltpu.VMEM((2, SPECIES) + half, f32),
            pltpu.VMEM((SPECIES,) + half, bf16),
            pltpu.VMEM((SPECIES,) + half, bf16),
            pltpu.VMEM((4, 16 * WIDE, LANES), f32),
            pltpu.VMEM((2, 16 * WIDE, LANES), f32),
            pltpu.SemaphoreType.DMA((3, ROWS)),
            pltpu.SemaphoreType.DMA((3, ROWS)),
            pltpu.SemaphoreType.DMA,
        ],
        out_shape=[jax.ShapeDtypeStruct((2, SPECIES) + half, f32)]
        + [jax.ShapeDtypeStruct((SPECIES,) + half, bf16)] * 2,
        compiler_params=pltpu.CompilerParams(vmem_limit_bytes=LIMIT * MIB),
        cost_estimate=pl.CostEstimate(flops=10**9, bytes_accessed=5 * 10**6, transcendentals=0),
    )(*(pltpu.with_memory_space_constraint(v, FAR) for v in (counts, cells, species, mix)))


def mixing_kernel(counts, mix_matrix, species, mix, mixed):
    def one_row(r, carry):
        first = pl.multiple_of(r * COLS, COLS)
        rows = pl.ds(first, COLS)
        limit = limits_of(counts, first)
        for t in range(4):
            ws = weights_of(limit, t, rows, species, mix)
            for l in range(SPECIES):
                v = mix_matrix[l, 0] * ws[0]
                for k in range(1, SPECIES):
                    v = v + mix_matrix[l, k] * ws[k]
                mixed[l, rows, t * LANES:(t + 1) * LANES] = v
        return carry

    lax.fori_loop(0, ROWS, one_row, 0)


def mixing(counts, mix_matrix, species, mix):
    return pl.pallas_call(
        mixing_kernel,
        name="mixing",
        in_specs=[pl.BlockSpec(memory_space=SM)] * 2 + [pl.BlockSpec(memory_space=VM)] * 2,
        out_specs=pl.BlockSpec(memory_space=VM),
        out_shape=jax.ShapeDtypeStruct((SPECIES, ROWS * COLS, SLOTS), f32),
        compiler_params=pltpu.CompilerParams(vmem_limit_bytes=12 * MIB),
        cost_estimate=pl.CostEstimate(flops=10**9, bytes_accessed=4 * 10**6, transcendentals=0),
    )(counts, mix_matrix, species, mix)


def scaled_taps():
    smooth_scale, slope_scale = 1.6396387, 1.5596421
    smooth_taps = {0: T0, 1: T1, -1: T1, 2: T2, -2: T2}
    slope_taps = {1: 0.5 * (T0 - T2), 2: 0.5 * T1, 3: 0.5 * T2}
    slope_taps.update({-j: -v for j, v in slope_taps.items()})
    return (
        {j: smooth_scale * v for j, v in smooth_taps.items()},
        {j: slope_scale * v for j, v in slope_taps.items()},
        smooth_scale,
        slope_scale,
    )


SMOOTH, SLOPE, SMOOTH_SCALE, SLOPE_SCALE = scaled_taps()


def tap_matrices():
    lane = np.arange(LANES)
    x, y = lane // 16, lane % 16
    results = []
    for main, other, extent in ((y, x, 16), (x, y, 8)):
        source = np.concatenate([main, np.where(main < extent // 2, main + extent, main - extent)])
        same = np.concatenate([other, other])[:, None] == other[None, :]
        gap = source[:, None] - main[None, :]
        for taps in (SMOOTH, SLOPE):
            matrix = np.zeros((2 * LANES, LANES), np.float32)
            for j, value in taps.items():
                matrix += np.where(same & (gap == j), np.float32(value), np.float32(0))
            results.append(matrix)
    return jnp.asarray(np.concatenate(results, axis=1)).astype(bf16)


def split(v):
    top = v.astype(bf16)
    return top, (v - top.astype(f32)).astype(bf16)


def smooth_kernel(planes, even_ref, taps, *refs):
    flat = planes == FLAT
    if flat:
        own, first_a, first_b, second_a, second_b, ready, partial, x_s, y_s, w_s, g_s = refs
    else:
        partial, far_a, far_b, ready, x_s, y_s, w_s, g_s = refs
    outs = (0, 1, 2, 3) if flat else (4, 5)
    rows_of, count = ROWS_OF[planes]
    k = pl.program_id(0)
    lane = lax.broadcasted_iota(jnp.int32, (COLS, LANES), 1)
    col = lane & 15
    lower = lane.astype(f32).astype(bf16) < 64
    cu = 1.0 / (SMOOTH_SCALE * SLOPE_SCALE)
    cz = 0.5 / (SMOOTH_SCALE * SMOOTH_SCALE)
    even = jnp.full((COLS, LANES), even_ref[0], jnp.int32) == 1
    for h in range(HALVES):
        def sides(a, b):
            a, b = a.astype(f32), b.astype(f32)
            return jnp.where(even, b, a), jnp.where(even, a, b)

        if flat:
            b, r0 = sides(first_a[0, h], first_b[0, h])
            a, r1 = sides(second_a[0, h], second_b[0, h])
            o0 = own[0, 0, h]
            o1 = own[1, 0, h]
            u0 = T2 * (a + r0) + T1 * (b + o1) + T0 * o0
            u1 = T2 * (b + r1) + T1 * (o0 + r0) + T0 * o1
            partial[0, 0, h] = cz * (u1 - (T2 * o1 + T1 * (a + o0) + T0 * b))
            partial[1, 0, h] = cz * ((T2 * o0 + T1 * (o1 + r1) + T0 * r0) - u0)
            values = (cu * u0, cu * u1)
        else:
            l2, r2 = sides(far_a[0, h], far_b[0, h])
            values = (partial[0, 0, h] - (cz * T2) * l2, partial[1, 0, h] + (cz * T2) * r2)
        for i, v in enumerate(values):
            around = jnp.where(col < 8, pltpu.roll(v, COLS - 1, 0), pltpu.roll(v, 1, 0))
            for part, value in ((0, v), (1, around)):
                for level, piece in enumerate(split(value)):
                    x_s[level, i, h * COLS:(h + 1) * COLS, part * LANES:(part + 1) * LANES] = piece
    for i, plane in enumerate(planes):
        table = taps[:, :2 * LANES] if plane < 2 else taps[:, :LANES]
        out = jnp.dot(x_s[0, i], table, preferred_element_type=f32) + jnp.dot(
            x_s[1, i], table, preferred_element_type=f32
        )
        if plane < 2:
            y_s[outs.index(plane)] = out[:, :LANES]
            y_s[outs.index(2 + plane)] = out[:, LANES:]
        else:
            y_s[outs.index(2 + plane)] = out
    for i, p in enumerate(outs):
        pieces = [split(y_s[i, h * COLS:(h + 1) * COLS]) for h in range(HALVES)]
        for h in range(HALVES):
            rows = slice(h * COLS, (h + 1) * COLS)
            for level in range(2):
                w_s[level, i, rows, :LANES] = pieces[h][level]
                w_s[level, i, rows, LANES:] = jnp.where(
                    lower, pieces[(h + 1) % HALVES][level], pieces[(h - 1) % HALVES][level]
                )
        table = taps[:, 3 * LANES:] if p < 2 else taps[:, 2 * LANES:3 * LANES]
        out = jnp.dot(w_s[0, i], table, preferred_element_type=f32) + jnp.dot(
            w_s[1, i], table, preferred_element_type=f32
        )
        for h in range(HALVES):
            g_s[h, pl.ds((k * rows_of + i) * WIDE, COLS)] = out[h * COLS:(h + 1) * COLS]

    if count > rows_of * SPECIES:
        @pl.when(k == 0)
        def _():
            g_s[:, rows_of * SPECIES * WIDE:] = jnp.zeros(
                (HALVES, (count - rows_of * SPECIES) * WIDE, LANES), f32
            )

    @pl.when(k == SPECIES - 1)
    def _():
        def one_row(r, carry):
            for q in range(COLS):
                for h in range(2):
                    value = g_s[2 * r + h, pl.ds(q, count, stride=WIDE)]
                    top = value.astype(bf16).astype(f32)
                    ready[r * COLS + q, :, h * LANES:(h + 1) * LANES] = jnp.concatenate(
                        [top, value - top], axis=0
                    ).astype(bf16)
            return carry

        lax.fori_loop(0, ROWS, one_row, 0)


FLAT = (0, 1)
SLOPES = (2, 3)
ROWS_OF = {FLAT: (4, 24), SLOPES: (2, 16)}


def smooth(planes, even, taps, *planes_in):
    _, count = ROWS_OF[planes]
    half = (HALVES, COLS, LANES)
    outs = 4 if planes == FLAT else 2
    two = pl.BlockSpec((2, 1) + half, lambda k: (0, k, 0, 0, 0))
    one = pl.BlockSpec((1,) + half, lambda k: (k, 0, 0, 0))
    ready_spec = pl.BlockSpec((ROWS * COLS, 2 * count, 2 * LANES), lambda k: (0, 0, 0))
    ready_shape = jax.ShapeDtypeStruct((ROWS * COLS, 2 * count, 2 * LANES), bf16)
    partial_shape = jax.ShapeDtypeStruct((2, SPECIES) + half, f32)
    return pl.pallas_call(
        functools.partial(smooth_kernel, planes),
        name="smooth",
        grid=(SPECIES,),
        in_specs=[
            pl.BlockSpec(memory_space=SM),
            pl.BlockSpec((2 * LANES, 4 * LANES), lambda k: (0, 0)),
        ]
        + ([two, one, one, one, one] if planes == FLAT else [two, one, one]),
        out_specs=[ready_spec, two] if planes == FLAT else ready_spec,
        out_shape=[ready_shape, partial_shape] if planes == FLAT else ready_shape,
        scratch_shapes=[
            pltpu.VMEM((2, len(planes), HALVES * COLS, 2 * LANES), bf16),
            pltpu.VMEM((outs, HALVES * COLS, LANES), f32),
            pltpu.VMEM((2, outs, HALVES * COLS, 2 * LANES), bf16),
            pltpu.VMEM((HALVES, count * WIDE, LANES), f32),
        ],
        compiler_params=pltpu.CompilerParams(vmem_limit_bytes=24 * MIB),
        cost_estimate=pl.CostEstimate(flops=10**9, bytes_accessed=4 * 10**6, transcendentals=0),
    )(even, taps, *planes_in)


def row_of(k, p):
    return k * 4 + p if p < 4 else 24 + k * 2 + p - 4


def pick_kernel(cells, flat, slopes, mixed, forces, got_s):
    def one_group(g, slot):
        first = pl.multiple_of(g * GROUP, GROUP)
        for b in range(GROUP):
            d = first + b
            table = table_of(*digits_of(cells[pl.ds(d, 1), :]), 16)
            rows = jnp.concatenate([flat[d], slopes[d]], axis=0)
            got = jnp.dot(rows, table, preferred_element_type=f32)
            got = jnp.concatenate([got[:24] + got[24:48], got[48:64] + got[64:]], axis=0)
            for t in range(4):
                got_s[slot, t, pl.ds(b, 40, stride=SLOT)] = got[:, t * LANES:(t + 1) * LANES]
        for t in range(4):
            lanes = slice(t * LANES, (t + 1) * LANES)
            upper = (cells[pl.ds(first, GROUP), lanes] & 1) == 1
            vs = [mixed[k, pl.ds(first, GROUP), lanes] for k in range(SPECIES)]
            for a in range(3):
                total = None
                for k in range(SPECIES):
                    low, high = (
                        got_s[slot, t, pl.ds(row_of(k, 2 * a + z) * SLOT, GROUP)] for z in range(2)
                    )
                    value = jnp.where(upper, high, low)
                    total = vs[k] * value if total is None else total + vs[k] * value
                forces[a, pl.ds(first, GROUP), lanes] = total

    def four_groups(i, carry):
        for j in range(4):
            one_group(4 * i + j, j)
        return carry

    lax.fori_loop(0, ROWS * COLS // GROUP // 4, four_groups, 0)


def pick(cells, ready, mixed):
    return pl.pallas_call(
        pick_kernel,
        name="pick",
        in_specs=[pl.BlockSpec(memory_space=VM)] * 4,
        out_specs=pl.BlockSpec(memory_space=VM),
        out_shape=jax.ShapeDtypeStruct((3, ROWS * COLS, SLOTS), f32),
        scratch_shapes=[pltpu.VMEM((4, 4, 40 * SLOT, LANES), f32)],
        compiler_params=pltpu.CompilerParams(vmem_limit_bytes=24 * MIB),
        cost_estimate=pl.CostEstimate(flops=6 * 10**9, bytes_accessed=10**7, transcendentals=0),
    )(cells, *ready, mixed)


def body(send_cells, send_species, send_mix, send_counts, chi):
    axes = ("row", "col")
    count = lax.axis_size("row") * lax.axis_size("col")
    swap_a = [(i, i ^ 1) for i in range(count)]
    swap_b = [(i, (i + (1 if i % 2 else -1)) % count) for i in range(count)]
    odd = lax.axis_index("col") % 2
    even = (1 - odd).reshape(1)
    chis = 0.5 * (chi + chi.T) * (1.0 - jnp.eye(SPECIES, dtype=f32))
    mix_matrix = -0.5 * (chis + 1.0)
    cells, species, mix, counts = send_cells[0], send_species[0], send_mix[0], send_counts[0]
    own, first, second = deposit(counts, cells, species, mix)
    own = pltpu.with_memory_space_constraint(own, FAR)
    taps = tap_matrices()

    def swap(value, pairs):
        return lax.ppermute(value, axes, pairs)

    first_a = swap(first, swap_a)
    first_b = swap(second, swap_b)
    second_a = swap(second, swap_a)
    second_b = swap(first, swap_b)
    far_b = swap(first_a, swap_b)
    far_a = swap(first_b, swap_a)
    flat, partial = smooth(FLAT, even, taps, own, first_a, first_b, second_a, second_b)
    slopes = smooth(SLOPES, even, taps, partial, far_a, far_b)
    mixed = mixing(counts, mix_matrix, species, mix)
    return pick(cells, (flat, slopes), mixed)[None]


def solution(mesh):
    return jax.shard_map(
        body,
        mesh=mesh,
        in_specs=(
            P(("row", "col"), None, None),
            P(("row", "col"), None, None),
            P(("row", "col"), None, None, None),
            P(("row", "col"), None),
            P(),
        ),
        out_specs=P(("row", "col"), None, None, None),
        check_vma=False,
    )
```

```python
import functools

import jax
import jax.numpy as jnp
import numpy as np
from jax import lax
from jax.experimental import pallas as pl
from jax.experimental.pallas import tpu as pltpu
from jax.sharding import PartitionSpec as P


SPECIES = 6
ROWS = 8
COLS = 16
HALVES = 16
LANES = 128
SLOTS = 512
GROUP = 8
WIDE = COLS + 1
SLOT = GROUP + 1
MIB = 1 << 20
LIMIT = 60

raw_taps = (0.1353352832366127, 0.6065306597126334, 1.0)
tap_total = raw_taps[2] + 2.0 * (raw_taps[0] + raw_taps[1])
T2, T1, T0 = (t / tap_total for t in raw_taps)

f32 = jnp.float32
bf16 = jnp.bfloat16


def digits_of(row):
    wide = jnp.broadcast_to(row, (8, SLOTS))
    low = (wide >> 8) & 15
    ids = lax.broadcasted_iota(jnp.int32, (8, SLOTS), 0)
    inner = jnp.concatenate(
        [jnp.where(low == ids, 1.0, 0.0), jnp.where(low == ids + 8, 1.0, 0.0)], axis=0
    ).astype(bf16)
    high = (wide >> 12).astype(f32)
    return inner, jnp.concatenate([high, high], axis=0).astype(bf16)


def table_of(inner, outer, count):
    none = jnp.zeros((16, SLOTS), bf16)
    return jnp.concatenate(
        [jnp.where(outer == jnp.full((16, SLOTS), i, bf16), inner, none) for i in range(count)], axis=0
    )


def weights_of(limit, t, rows, species, mix):
    part = pl.ds(t * LANES, LANES)
    lane = lax.broadcasted_iota(jnp.int32, (COLS, LANES), 1)
    valid = (lane + t * LANES) < limit
    kind = species[rows, part]
    found = []
    for k in range(SPECIES):
        w = jnp.where(kind == k, 1.0, 0.0) + mix[k, rows, part].astype(f32)
        found.append(jnp.where(valid, w, 0.0).astype(bf16).astype(f32))
    return found


def limits_of(counts, first):
    rows = lax.broadcasted_iota(jnp.int32, (COLS, LANES), 0)
    limit = jnp.zeros((COLS, LANES), jnp.int32)
    for i in range(COLS):
        limit = jnp.where(rows == i, counts[first + i], limit)
    return limit


def deposit_kernel(counts_far, cells_far, species_far, mix_far, own_far, first_far, second_far,
                   counts, cells, species, mix, own, first_s, second_s, w_s, d_s, sems, out_sems, count_sem):
    even = jnp.full((COLS, LANES), lax.axis_index("col") % 2, jnp.int32) == 0

    def fetches(r):
        rows = pl.ds(pl.multiple_of(r * COLS, COLS), COLS)
        return (
            pltpu.make_async_copy(cells_far.at[rows], cells.at[rows], sems.at[0, r]),
            pltpu.make_async_copy(species_far.at[rows], species.at[rows], sems.at[1, r]),
            pltpu.make_async_copy(mix_far.at[:, rows], mix.at[:, rows], sems.at[2, r]),
        )

    def results(r):
        part = pl.ds(2 * r, 2)
        return [
            pltpu.make_async_copy(near.at[:, part] if i < 2 else near.at[:, :, part],
                                  far.at[:, part] if i < 2 else far.at[:, :, part], out_sems.at[i, r])
            for i, (near, far) in enumerate(((first_s, first_far), (second_s, second_far), (own, own_far)))
        ]

    count_copy = pltpu.make_async_copy(counts_far, counts, count_sem)
    count_copy.start()
    for r in range(ROWS):
        for copy in fetches(r):
            copy.start()
    zero = jnp.zeros((COLS, LANES), f32)
    for t in range(4):
        for k in (6, 7):
            w_s[t, k * WIDE:k * WIDE + COLS] = zero
            w_s[t, (8 + k) * WIDE:(8 + k) * WIDE + COLS] = zero

    count_copy.wait()

    def one_row(r, carry):
        for copy in fetches(r):
            copy.wait()
        first = pl.multiple_of(r * COLS, COLS)
        rows = pl.ds(first, COLS)
        limit = limits_of(counts, first)
        for t in range(4):
            upper = (cells[rows, pl.ds(t * LANES, LANES)] & 1) == 1
            for k, w in enumerate(weights_of(limit, t, rows, species, mix)):
                w_s[t, k * WIDE:k * WIDE + COLS] = jnp.where(upper, 0.0, w)
                w_s[t, (8 + k) * WIDE:(8 + k) * WIDE + COLS] = jnp.where(upper, w, 0.0)
        for b in range(COLS):
            inner, outer = digits_of(cells[pl.ds(first + b, 1), :])
            second = outer > 7.5
            table = table_of(inner, jnp.where(second, outer - 8.0, outer), 8)
            w = jnp.concatenate([w_s[t, pl.ds(b, 16, stride=WIDE)] for t in range(4)], axis=1).astype(bf16)
            none = jnp.zeros((16, SLOTS), bf16)
            halves = jnp.concatenate([jnp.where(second, none, w), jnp.where(second, w, none)], axis=0)
            dens = lax.dot_general(halves, table, (((1,), (1,)), ((), ())), preferred_element_type=f32)
            d_s[0, pl.ds(b, 16, stride=WIDE)] = dens[:16]
            d_s[1, pl.ds(b, 16, stride=WIDE)] = dens[16:]
        for k in range(SPECIES):
            for h in range(2):
                low, high = (d_s[h, (z * 8 + k) * WIDE:(z * 8 + k) * WIDE + COLS] for z in range(2))
                own[0, k, 2 * r + h] = low
                own[1, k, 2 * r + h] = high
                first_s[k, 2 * r + h] = jnp.where(even, high, low).astype(bf16)
                second_s[k, 2 * r + h] = jnp.where(even, low, high).astype(bf16)
        for copy in results(r):
            copy.start()
        return carry

    lax.fori_loop(0, ROWS, one_row, 0)
    for r in range(ROWS):
        for copy in results(r):
            copy.wait()


VM = pltpu.MemorySpace.VMEM
SM = pltpu.MemorySpace.SMEM
FAR = pltpu.MemorySpace.HBM


def deposit(counts, cells, species, mix):
    half = (HALVES, COLS, LANES)
    return pl.pallas_call(
        deposit_kernel,
        name="deposit",
        in_specs=[pl.BlockSpec(memory_space=FAR)] * 4,
        out_specs=[pl.BlockSpec(memory_space=FAR)] * 3,
        scratch_shapes=[
            pltpu.SMEM((ROWS * COLS,), jnp.int32),
            pltpu.VMEM((ROWS * COLS, SLOTS), jnp.int32),
            pltpu.VMEM((ROWS * COLS, SLOTS), jnp.int32),
            pltpu.VMEM((SPECIES, ROWS * COLS, SLOTS), bf16),
            pltpu.VMEM((2, SPECIES) + half, f32),
            pltpu.VMEM((SPECIES,) + half, bf16),
            pltpu.VMEM((SPECIES,) + half, bf16),
            pltpu.VMEM((4, 16 * WIDE, LANES), f32),
            pltpu.VMEM((2, 16 * WIDE, LANES), f32),
            pltpu.SemaphoreType.DMA((3, ROWS)),
            pltpu.SemaphoreType.DMA((3, ROWS)),
            pltpu.SemaphoreType.DMA,
        ],
        out_shape=[jax.ShapeDtypeStruct((2, SPECIES) + half, f32)]
        + [jax.ShapeDtypeStruct((SPECIES,) + half, bf16)] * 2,
        compiler_params=pltpu.CompilerParams(vmem_limit_bytes=LIMIT * MIB),
        cost_estimate=pl.CostEstimate(flops=10**9, bytes_accessed=5 * 10**6, transcendentals=0),
    )(*(pltpu.with_memory_space_constraint(v, FAR) for v in (counts, cells, species, mix)))


def mixing_kernel(counts, mix_matrix, species, mix, mixed):
    def one_row(r, carry):
        first = pl.multiple_of(r * COLS, COLS)
        rows = pl.ds(first, COLS)
        limit = limits_of(counts, first)
        for t in range(4):
            ws = weights_of(limit, t, rows, species, mix)
            for l in range(SPECIES):
                v = mix_matrix[l, 0] * ws[0]
                for k in range(1, SPECIES):
                    v = v + mix_matrix[l, k] * ws[k]
                mixed[l, rows, t * LANES:(t + 1) * LANES] = v
        return carry

    lax.fori_loop(0, ROWS, one_row, 0)


def mixing(counts, mix_matrix, species, mix):
    return pl.pallas_call(
        mixing_kernel,
        name="mixing",
        in_specs=[pl.BlockSpec(memory_space=SM)] * 2 + [pl.BlockSpec(memory_space=VM)] * 2,
        out_specs=pl.BlockSpec(memory_space=VM),
        out_shape=jax.ShapeDtypeStruct((SPECIES, ROWS * COLS, SLOTS), f32),
        compiler_params=pltpu.CompilerParams(vmem_limit_bytes=12 * MIB),
        cost_estimate=pl.CostEstimate(flops=10**9, bytes_accessed=4 * 10**6, transcendentals=0),
    )(counts, mix_matrix, species, mix)


def scaled_taps():
    smooth_scale, slope_scale = 1.6396387, 1.5596421
    smooth_taps = {0: T0, 1: T1, -1: T1, 2: T2, -2: T2}
    slope_taps = {1: 0.5 * (T0 - T2), 2: 0.5 * T1, 3: 0.5 * T2}
    slope_taps.update({-j: -v for j, v in slope_taps.items()})
    return (
        {j: smooth_scale * v for j, v in smooth_taps.items()},
        {j: slope_scale * v for j, v in slope_taps.items()},
        smooth_scale,
        slope_scale,
    )


SMOOTH, SLOPE, SMOOTH_SCALE, SLOPE_SCALE = scaled_taps()


def tap_matrices():
    lane = np.arange(LANES)
    x, y = lane // 16, lane % 16
    results = []
    for main, other, extent in ((y, x, 16), (x, y, 8)):
        source = np.concatenate([main, np.where(main < extent // 2, main + extent, main - extent)])
        same = np.concatenate([other, other])[:, None] == other[None, :]
        gap = source[:, None] - main[None, :]
        for taps in (SMOOTH, SLOPE):
            matrix = np.zeros((2 * LANES, LANES), np.float32)
            for j, value in taps.items():
                matrix += np.where(same & (gap == j), np.float32(value), np.float32(0))
            results.append(matrix)
    return jnp.asarray(np.concatenate(results, axis=1)).astype(bf16)


def split(v):
    top = v.astype(bf16)
    return top, (v - top.astype(f32)).astype(bf16)


def smooth_kernel(planes, even_ref, taps, *refs):
    flat = planes == FLAT
    if flat:
        own, first_a, first_b, second_a, second_b, ready, partial, x_s, y_s, w_s, g_s = refs
    else:
        partial, far_a, far_b, ready, x_s, y_s, w_s, g_s = refs
    outs = (0, 1, 2, 3) if flat else (4, 5)
    rows_of, count = ROWS_OF[planes]
    k = pl.program_id(0)
    lane = lax.broadcasted_iota(jnp.int32, (COLS, LANES), 1)
    col = lane & 15
    lower = lane.astype(f32).astype(bf16) < 64
    cu = 1.0 / (SMOOTH_SCALE * SLOPE_SCALE)
    cz = 0.5 / (SMOOTH_SCALE * SMOOTH_SCALE)
    even = jnp.full((COLS, LANES), even_ref[0], jnp.int32) == 1
    for h in range(HALVES):
        def sides(a, b):
            a, b = a.astype(f32), b.astype(f32)
            return jnp.where(even, b, a), jnp.where(even, a, b)

        if flat:
            b, r0 = sides(first_a[0, h], first_b[0, h])
            a, r1 = sides(second_a[0, h], second_b[0, h])
            o0 = own[0, 0, h]
            o1 = own[1, 0, h]
            u0 = T2 * (a + r0) + T1 * (b + o1) + T0 * o0
            u1 = T2 * (b + r1) + T1 * (o0 + r0) + T0 * o1
            partial[0, 0, h] = cz * (u1 - (T2 * o1 + T1 * (a + o0) + T0 * b))
            partial[1, 0, h] = cz * ((T2 * o0 + T1 * (o1 + r1) + T0 * r0) - u0)
            values = (cu * u0, cu * u1)
        else:
            l2, r2 = sides(far_a[0, h], far_b[0, h])
            values = (partial[0, 0, h] - (cz * T2) * l2, partial[1, 0, h] + (cz * T2) * r2)
        for i, v in enumerate(values):
            around = jnp.where(col < 8, pltpu.roll(v, COLS - 1, 0), pltpu.roll(v, 1, 0))
            for part, value in ((0, v), (1, around)):
                for level, piece in enumerate(split(value)):
                    x_s[level, i, h * COLS:(h + 1) * COLS, part * LANES:(part + 1) * LANES] = piece
    for i, plane in enumerate(planes):
        table = taps[:, :2 * LANES] if plane < 2 else taps[:, :LANES]
        out = jnp.dot(x_s[0, i], table, preferred_element_type=f32) + jnp.dot(
            x_s[1, i], table, preferred_element_type=f32
        )
        if plane < 2:
            y_s[outs.index(plane)] = out[:, :LANES]
            y_s[outs.index(2 + plane)] = out[:, LANES:]
        else:
            y_s[outs.index(2 + plane)] = out
    for i, p in enumerate(outs):
        pieces = [split(y_s[i, h * COLS:(h + 1) * COLS]) for h in range(HALVES)]
        for h in range(HALVES):
            rows = slice(h * COLS, (h + 1) * COLS)
            for level in range(2):
                w_s[level, i, rows, :LANES] = pieces[h][level]
                w_s[level, i, rows, LANES:] = jnp.where(
                    lower, pieces[(h + 1) % HALVES][level], pieces[(h - 1) % HALVES][level]
                )
        table = taps[:, 3 * LANES:] if p < 2 else taps[:, 2 * LANES:3 * LANES]
        out = jnp.dot(w_s[0, i], table, preferred_element_type=f32) + jnp.dot(
            w_s[1, i], table, preferred_element_type=f32
        )
        for h in range(HALVES):
            g_s[h, pl.ds((k * rows_of + i) * WIDE, COLS)] = out[h * COLS:(h + 1) * COLS]

    if count > rows_of * SPECIES:
        @pl.when(k == 0)
        def _():
            g_s[:, rows_of * SPECIES * WIDE:] = jnp.zeros(
                (HALVES, (count - rows_of * SPECIES) * WIDE, LANES), f32
            )

    @pl.when(k == SPECIES - 1)
    def _():
        def one_row(r, carry):
            for q in range(COLS):
                for h in range(2):
                    value = g_s[2 * r + h, pl.ds(q, count, stride=WIDE)]
                    top = value.astype(bf16).astype(f32)
                    ready[r * COLS + q, :, h * LANES:(h + 1) * LANES] = jnp.concatenate(
                        [top, value - top], axis=0
                    ).astype(bf16)
            return carry

        lax.fori_loop(0, ROWS, one_row, 0)


FLAT = (0, 1)
SLOPES = (2, 3)
ROWS_OF = {FLAT: (4, 24), SLOPES: (2, 16)}


def smooth(planes, even, taps, *planes_in):
    _, count = ROWS_OF[planes]
    half = (HALVES, COLS, LANES)
    outs = 4 if planes == FLAT else 2
    two = pl.BlockSpec((2, 1) + half, lambda k: (0, k, 0, 0, 0))
    one = pl.BlockSpec((1,) + half, lambda k: (k, 0, 0, 0))
    ready_spec = pl.BlockSpec((ROWS * COLS, 2 * count, 2 * LANES), lambda k: (0, 0, 0))
    ready_shape = jax.ShapeDtypeStruct((ROWS * COLS, 2 * count, 2 * LANES), bf16)
    partial_shape = jax.ShapeDtypeStruct((2, SPECIES) + half, f32)
    return pl.pallas_call(
        functools.partial(smooth_kernel, planes),
        name="smooth",
        grid=(SPECIES,),
        in_specs=[
            pl.BlockSpec(memory_space=SM),
            pl.BlockSpec((2 * LANES, 4 * LANES), lambda k: (0, 0)),
        ]
        + ([two, one, one, one, one] if planes == FLAT else [two, one, one]),
        out_specs=[ready_spec, two] if planes == FLAT else ready_spec,
        out_shape=[ready_shape, partial_shape] if planes == FLAT else ready_shape,
        scratch_shapes=[
            pltpu.VMEM((2, len(planes), HALVES * COLS, 2 * LANES), bf16),
            pltpu.VMEM((outs, HALVES * COLS, LANES), f32),
            pltpu.VMEM((2, outs, HALVES * COLS, 2 * LANES), bf16),
            pltpu.VMEM((HALVES, count * WIDE, LANES), f32),
        ],
        compiler_params=pltpu.CompilerParams(vmem_limit_bytes=24 * MIB),
        cost_estimate=pl.CostEstimate(flops=10**9, bytes_accessed=4 * 10**6, transcendentals=0),
    )(even, taps, *planes_in)


def row_of(k, p):
    return k * 4 + p if p < 4 else 24 + k * 2 + p - 4


def pick_kernel(cells, flat, slopes, mixed, forces_far, got_s, forces, sems):
    def result(i):
        rows = pl.ds(pl.multiple_of(i * 4 * GROUP, 4 * GROUP), 4 * GROUP)
        return pltpu.make_async_copy(forces.at[:, rows], forces_far.at[:, rows], sems.at[i])

    def one_group(g, slot):
        first = pl.multiple_of(g * GROUP, GROUP)
        for b in range(GROUP):
            d = first + b
            table = table_of(*digits_of(cells[pl.ds(d, 1), :]), 16)
            rows = jnp.concatenate([flat[d], slopes[d]], axis=0)
            got = jnp.dot(rows, table, preferred_element_type=f32)
            got = jnp.concatenate([got[:24] + got[24:48], got[48:64] + got[64:]], axis=0)
            for t in range(4):
                got_s[slot, t, pl.ds(b, 40, stride=SLOT)] = got[:, t * LANES:(t + 1) * LANES]
        for t in range(4):
            lanes = slice(t * LANES, (t + 1) * LANES)
            upper = (cells[pl.ds(first, GROUP), lanes] & 1) == 1
            vs = [mixed[k, pl.ds(first, GROUP), lanes] for k in range(SPECIES)]
            for a in range(3):
                total = None
                for k in range(SPECIES):
                    low, high = (
                        got_s[slot, t, pl.ds(row_of(k, 2 * a + z) * SLOT, GROUP)] for z in range(2)
                    )
                    value = jnp.where(upper, high, low)
                    total = vs[k] * value if total is None else total + vs[k] * value
                forces[a, pl.ds(first, GROUP), lanes] = total

    def four_groups(i, carry):
        for j in range(4):
            one_group(4 * i + j, j)
        result(i).start()
        return carry

    lax.fori_loop(0, ROWS * COLS // GROUP // 4, four_groups, 0)
    for i in range(ROWS * COLS // GROUP // 4):
        result(i).wait()


def pick(cells, ready, mixed):
    return pl.pallas_call(
        pick_kernel,
        name="pick",
        in_specs=[pl.BlockSpec(memory_space=VM)] * 4,
        out_specs=pl.BlockSpec(memory_space=FAR),
        out_shape=jax.ShapeDtypeStruct((3, ROWS * COLS, SLOTS), f32),
        scratch_shapes=[
            pltpu.VMEM((4, 4, 40 * SLOT, LANES), f32),
            pltpu.VMEM((3, ROWS * COLS, SLOTS), f32),
            pltpu.SemaphoreType.DMA((ROWS * COLS // GROUP // 4,)),
        ],
        compiler_params=pltpu.CompilerParams(vmem_limit_bytes=24 * MIB),
        cost_estimate=pl.CostEstimate(flops=6 * 10**9, bytes_accessed=10**7, transcendentals=0),
    )(cells, *ready, mixed)


def body(send_cells, send_species, send_mix, send_counts, chi):
    axes = ("row", "col")
    count = lax.axis_size("row") * lax.axis_size("col")
    swap_a = [(i, i ^ 1) for i in range(count)]
    swap_b = [(i, (i + (1 if i % 2 else -1)) % count) for i in range(count)]
    odd = lax.axis_index("col") % 2
    even = (1 - odd).reshape(1)
    chis = 0.5 * (chi + chi.T) * (1.0 - jnp.eye(SPECIES, dtype=f32))
    mix_matrix = -0.5 * (chis + 1.0)
    cells, species, mix, counts = send_cells[0], send_species[0], send_mix[0], send_counts[0]
    own, first, second = deposit(counts, cells, species, mix)
    own = pltpu.with_memory_space_constraint(own, FAR)
    taps = tap_matrices()

    def swap(value, pairs):
        return lax.ppermute(value, axes, pairs)

    first_a = swap(first, swap_a)
    first_b = swap(second, swap_b)
    second_a = swap(second, swap_a)
    second_b = swap(first, swap_b)
    far_b = swap(first_a, swap_b)
    far_a = swap(first_b, swap_a)
    flat, partial = smooth(FLAT, even, taps, own, first_a, first_b, second_a, second_b)
    slopes = smooth(SLOPES, even, taps, partial, far_a, far_b)
    mixed = mixing(counts, mix_matrix, species, mix)
    return pick(cells, (flat, slopes), mixed)[None]


def solution(mesh):
    return jax.shard_map(
        body,
        mesh=mesh,
        in_specs=(
            P(("row", "col"), None, None),
            P(("row", "col"), None, None),
            P(("row", "col"), None, None, None),
            P(("row", "col"), None),
            P(),
        ),
        out_specs=P(("row", "col"), None, None, None),
        check_vma=False,
    )
```

```python
import functools

import jax
import jax.numpy as jnp
import numpy as np
from jax import lax
from jax.experimental import pallas as pl
from jax.experimental.pallas import tpu as pltpu
from jax.sharding import PartitionSpec as P


SPECIES = 6
ROWS = 8
COLS = 16
HALVES = 16
LANES = 128
SLOTS = 512
GROUP = 8
WIDE = COLS + 1
SLOT = GROUP + 1
MIB = 1 << 20
LIMIT = 60

raw_taps = (0.1353352832366127, 0.6065306597126334, 1.0)
tap_total = raw_taps[2] + 2.0 * (raw_taps[0] + raw_taps[1])
T2, T1, T0 = (t / tap_total for t in raw_taps)

f32 = jnp.float32
bf16 = jnp.bfloat16


def digits_of(row):
    wide = jnp.broadcast_to(row, (8, SLOTS))
    low = (wide >> 8) & 15
    ids = lax.broadcasted_iota(jnp.int32, (8, SLOTS), 0)
    inner = jnp.concatenate(
        [jnp.where(low == ids, 1.0, 0.0), jnp.where(low == ids + 8, 1.0, 0.0)], axis=0
    ).astype(bf16)
    high = (wide >> 12).astype(f32)
    return inner, jnp.concatenate([high, high], axis=0).astype(bf16)


def table_of(inner, outer, count):
    none = jnp.zeros((16, SLOTS), bf16)
    return jnp.concatenate(
        [jnp.where(outer == jnp.full((16, SLOTS), i, bf16), inner, none) for i in range(count)], axis=0
    )


def weights_of(limit, t, rows, species, mix):
    part = pl.ds(t * LANES, LANES)
    lane = lax.broadcasted_iota(jnp.int32, (COLS, LANES), 1)
    valid = (lane + t * LANES) < limit
    kind = species[rows, part]
    found = []
    for k in range(SPECIES):
        w = jnp.where(kind == k, 1.0, 0.0) + mix[k, rows, part].astype(f32)
        found.append(jnp.where(valid, w, 0.0).astype(bf16).astype(f32))
    return found


def limits_of(counts, first):
    rows = lax.broadcasted_iota(jnp.int32, (COLS, LANES), 0)
    limit = jnp.zeros((COLS, LANES), jnp.int32)
    for i in range(COLS):
        limit = jnp.where(rows == i, counts[first + i], limit)
    return limit


def deposit_kernel(counts_far, cells_far, species_far, mix_far, own_far, sent_far,
                   counts, cells, species, mix, own, sent, w_s, d_s, sems, out_sems, count_sem):

    def fetches(r):
        rows = pl.ds(pl.multiple_of(r * COLS, COLS), COLS)
        return (
            pltpu.make_async_copy(cells_far.at[rows], cells.at[rows], sems.at[0, r]),
            pltpu.make_async_copy(species_far.at[rows], species.at[rows], sems.at[1, r]),
            pltpu.make_async_copy(mix_far.at[:, rows], mix.at[:, rows], sems.at[2, r]),
        )

    def results(r):
        part = pl.ds(2 * r, 2)
        return [
            pltpu.make_async_copy(near.at[:, :, part], far.at[:, :, part], out_sems.at[i, r])
            for i, (near, far) in enumerate(((sent, sent_far), (own, own_far)))
        ]

    count_copy = pltpu.make_async_copy(counts_far, counts, count_sem)
    count_copy.start()
    for r in range(ROWS):
        for copy in fetches(r):
            copy.start()
    zero = jnp.zeros((COLS, LANES), f32)
    for t in range(4):
        for k in (6, 7):
            w_s[t, k * WIDE:k * WIDE + COLS] = zero
            w_s[t, (8 + k) * WIDE:(8 + k) * WIDE + COLS] = zero

    count_copy.wait()

    def one_row(r, carry):
        for copy in fetches(r):
            copy.wait()
        first = pl.multiple_of(r * COLS, COLS)
        rows = pl.ds(first, COLS)
        limit = limits_of(counts, first)
        for t in range(4):
            upper = (cells[rows, pl.ds(t * LANES, LANES)] & 1) == 1
            for k, w in enumerate(weights_of(limit, t, rows, species, mix)):
                w_s[t, k * WIDE:k * WIDE + COLS] = jnp.where(upper, 0.0, w)
                w_s[t, (8 + k) * WIDE:(8 + k) * WIDE + COLS] = jnp.where(upper, w, 0.0)
        for b in range(COLS):
            inner, outer = digits_of(cells[pl.ds(first + b, 1), :])
            second = outer > 7.5
            table = table_of(inner, jnp.where(second, outer - 8.0, outer), 8)
            w = jnp.concatenate([w_s[t, pl.ds(b, 16, stride=WIDE)] for t in range(4)], axis=1).astype(bf16)
            none = jnp.zeros((16, SLOTS), bf16)
            halves = jnp.concatenate([jnp.where(second, none, w), jnp.where(second, w, none)], axis=0)
            dens = lax.dot_general(halves, table, (((1,), (1,)), ((), ())), preferred_element_type=f32)
            d_s[0, pl.ds(b, 16, stride=WIDE)] = dens[:16]
            d_s[1, pl.ds(b, 16, stride=WIDE)] = dens[16:]
        for z in range(2):
            for k in range(SPECIES):
                for h in range(2):
                    value = d_s[h, (z * 8 + k) * WIDE:(z * 8 + k) * WIDE + COLS]
                    own[z, k, 2 * r + h] = value
                    sent[z, k, 2 * r + h] = value.astype(bf16)
        for copy in results(r):
            copy.start()
        return carry

    lax.fori_loop(0, ROWS, one_row, 0)
    for r in range(ROWS):
        for copy in results(r):
            copy.wait()


VM = pltpu.MemorySpace.VMEM
SM = pltpu.MemorySpace.SMEM
FAR = pltpu.MemorySpace.HBM


def deposit(counts, cells, species, mix):
    half = (HALVES, COLS, LANES)
    return pl.pallas_call(
        deposit_kernel,
        name="deposit",
        in_specs=[pl.BlockSpec(memory_space=FAR)] * 4,
        out_specs=[pl.BlockSpec(memory_space=FAR)] * 2,
        scratch_shapes=[
            pltpu.SMEM((ROWS * COLS,), jnp.int32),
            pltpu.VMEM((ROWS * COLS, SLOTS), jnp.int32),
            pltpu.VMEM((ROWS * COLS, SLOTS), jnp.int32),
            pltpu.VMEM((SPECIES, ROWS * COLS, SLOTS), bf16),
            pltpu.VMEM((2, SPECIES) + half, f32),
            pltpu.VMEM((2, SPECIES) + half, bf16),
            pltpu.VMEM((4, 16 * WIDE, LANES), f32),
            pltpu.VMEM((2, 16 * WIDE, LANES), f32),
            pltpu.SemaphoreType.DMA((3, ROWS)),
            pltpu.SemaphoreType.DMA((2, ROWS)),
            pltpu.SemaphoreType.DMA,
        ],
        out_shape=[jax.ShapeDtypeStruct((2, SPECIES) + half, dtype) for dtype in (f32, bf16)],
        compiler_params=pltpu.CompilerParams(vmem_limit_bytes=LIMIT * MIB),
        cost_estimate=pl.CostEstimate(flops=10**9, bytes_accessed=5 * 10**6, transcendentals=0),
    )(*(pltpu.with_memory_space_constraint(v, FAR) for v in (counts, cells, species, mix)))


def mixing_kernel(counts, mix_matrix, species, mix, mixed):
    def one_row(r, carry):
        first = pl.multiple_of(r * COLS, COLS)
        rows = pl.ds(first, COLS)
        limit = limits_of(counts, first)
        for t in range(4):
            ws = weights_of(limit, t, rows, species, mix)
            for l in range(SPECIES):
                v = mix_matrix[l, 0] * ws[0]
                for k in range(1, SPECIES):
                    v = v + mix_matrix[l, k] * ws[k]
                mixed[l, rows, t * LANES:(t + 1) * LANES] = v
        return carry

    lax.fori_loop(0, ROWS, one_row, 0)


def mixing(counts, mix_matrix, species, mix):
    return pl.pallas_call(
        mixing_kernel,
        name="mixing",
        in_specs=[pl.BlockSpec(memory_space=SM)] * 2 + [pl.BlockSpec(memory_space=VM)] * 2,
        out_specs=pl.BlockSpec(memory_space=VM),
        out_shape=jax.ShapeDtypeStruct((SPECIES, ROWS * COLS, SLOTS), f32),
        compiler_params=pltpu.CompilerParams(vmem_limit_bytes=12 * MIB),
        cost_estimate=pl.CostEstimate(flops=10**9, bytes_accessed=4 * 10**6, transcendentals=0),
    )(counts, mix_matrix, species, mix)


def scaled_taps():
    smooth_scale, slope_scale = 1.6396387, 1.5596421
    smooth_taps = {0: T0, 1: T1, -1: T1, 2: T2, -2: T2}
    slope_taps = {1: 0.5 * (T0 - T2), 2: 0.5 * T1, 3: 0.5 * T2}
    slope_taps.update({-j: -v for j, v in slope_taps.items()})
    return (
        {j: smooth_scale * v for j, v in smooth_taps.items()},
        {j: slope_scale * v for j, v in slope_taps.items()},
        smooth_scale,
        slope_scale,
    )


SMOOTH, SLOPE, SMOOTH_SCALE, SLOPE_SCALE = scaled_taps()


def tap_matrices():
    lane = np.arange(LANES)
    x, y = lane // 16, lane % 16
    results = []
    for main, other, extent in ((y, x, 16), (x, y, 8)):
        source = np.concatenate([main, np.where(main < extent // 2, main + extent, main - extent)])
        same = np.concatenate([other, other])[:, None] == other[None, :]
        gap = source[:, None] - main[None, :]
        for taps in (SMOOTH, SLOPE):
            matrix = np.zeros((2 * LANES, LANES), np.float32)
            for j, value in taps.items():
                matrix += np.where(same & (gap == j), np.float32(value), np.float32(0))
            results.append(matrix)
    return jnp.asarray(np.concatenate(results, axis=1)).astype(bf16)


def split(v):
    top = v.astype(bf16)
    return top, (v - top.astype(f32)).astype(bf16)


def smooth_kernel(planes, even_ref, taps, *refs):
    flat = planes == FLAT
    if flat:
        own, near_a, near_b, ready, partial, x_s, y_s, w_s, g_s = refs
    else:
        partial, far_a, far_b, ready, x_s, y_s, w_s, g_s = refs
    outs = (0, 1, 2, 3) if flat else (4, 5)
    rows_of, count = ROWS_OF[planes]
    k = pl.program_id(0)
    lane = lax.broadcasted_iota(jnp.int32, (COLS, LANES), 1)
    col = lane & 15
    lower = lane.astype(f32).astype(bf16) < 64
    cu = 1.0 / (SMOOTH_SCALE * SLOPE_SCALE)
    cz = 0.5 / (SMOOTH_SCALE * SMOOTH_SCALE)
    even = jnp.full((COLS, LANES), even_ref[0], jnp.int32) == 1
    for h in range(HALVES):
        def sides(a, b):
            a, b = a.astype(f32), b.astype(f32)
            return jnp.where(even, b, a), jnp.where(even, a, b)

        if flat:
            a, r0 = sides(near_a[0, 0, h], near_b[0, 0, h])
            b, r1 = sides(near_a[1, 0, h], near_b[1, 0, h])
            o0 = own[0, 0, h]
            o1 = own[1, 0, h]
            u0 = T2 * (a + r0) + T1 * (b + o1) + T0 * o0
            u1 = T2 * (b + r1) + T1 * (o0 + r0) + T0 * o1
            partial[0, 0, h] = cz * (u1 - (T2 * o1 + T1 * (a + o0) + T0 * b))
            partial[1, 0, h] = cz * ((T2 * o0 + T1 * (o1 + r1) + T0 * r0) - u0)
            values = (cu * u0, cu * u1)
        else:
            l2, r2 = sides(far_a[0, h], far_b[0, h])
            values = (partial[0, 0, h] - (cz * T2) * l2, partial[1, 0, h] + (cz * T2) * r2)
        for i, v in enumerate(values):
            around = jnp.where(col < 8, pltpu.roll(v, COLS - 1, 0), pltpu.roll(v, 1, 0))
            for part, value in ((0, v), (1, around)):
                for level, piece in enumerate(split(value)):
                    x_s[level, i, h * COLS:(h + 1) * COLS, part * LANES:(part + 1) * LANES] = piece
    for i, plane in enumerate(planes):
        table = taps[:, :2 * LANES] if plane < 2 else taps[:, :LANES]
        out = jnp.dot(x_s[0, i], table, preferred_element_type=f32) + jnp.dot(
            x_s[1, i], table, preferred_element_type=f32
        )
        if plane < 2:
            y_s[outs.index(plane)] = out[:, :LANES]
            y_s[outs.index(2 + plane)] = out[:, LANES:]
        else:
            y_s[outs.index(2 + plane)] = out
    for i, p in enumerate(outs):
        pieces = [split(y_s[i, h * COLS:(h + 1) * COLS]) for h in range(HALVES)]
        for h in range(HALVES):
            rows = slice(h * COLS, (h + 1) * COLS)
            for level in range(2):
                w_s[level, i, rows, :LANES] = pieces[h][level]
                w_s[level, i, rows, LANES:] = jnp.where(
                    lower, pieces[(h + 1) % HALVES][level], pieces[(h - 1) % HALVES][level]
                )
        table = taps[:, 3 * LANES:] if p < 2 else taps[:, 2 * LANES:3 * LANES]
        out = jnp.dot(w_s[0, i], table, preferred_element_type=f32) + jnp.dot(
            w_s[1, i], table, preferred_element_type=f32
        )
        for h in range(HALVES):
            g_s[h, pl.ds((k * rows_of + i) * WIDE, COLS)] = out[h * COLS:(h + 1) * COLS]

    if count > rows_of * SPECIES:
        @pl.when(k == 0)
        def _():
            g_s[:, rows_of * SPECIES * WIDE:] = jnp.zeros(
                (HALVES, (count - rows_of * SPECIES) * WIDE, LANES), f32
            )

    @pl.when(k == SPECIES - 1)
    def _():
        def one_row(r, carry):
            for q in range(COLS):
                for h in range(2):
                    value = g_s[2 * r + h, pl.ds(q, count, stride=WIDE)]
                    top = value.astype(bf16).astype(f32)
                    ready[r * COLS + q, :, h * LANES:(h + 1) * LANES] = jnp.concatenate(
                        [top, value - top], axis=0
                    ).astype(bf16)
            return carry

        lax.fori_loop(0, ROWS, one_row, 0)


FLAT = (0, 1)
SLOPES = (2, 3)
ROWS_OF = {FLAT: (4, 24), SLOPES: (2, 16)}


def smooth(planes, even, taps, *planes_in):
    _, count = ROWS_OF[planes]
    half = (HALVES, COLS, LANES)
    outs = 4 if planes == FLAT else 2
    two = pl.BlockSpec((2, 1) + half, lambda k: (0, k, 0, 0, 0))
    one = pl.BlockSpec((1,) + half, lambda k: (k, 0, 0, 0))
    ready_spec = pl.BlockSpec((ROWS * COLS, 2 * count, 2 * LANES), lambda k: (0, 0, 0))
    ready_shape = jax.ShapeDtypeStruct((ROWS * COLS, 2 * count, 2 * LANES), bf16)
    partial_shape = jax.ShapeDtypeStruct((2, SPECIES) + half, f32)
    return pl.pallas_call(
        functools.partial(smooth_kernel, planes),
        name="smooth",
        grid=(SPECIES,),
        in_specs=[
            pl.BlockSpec(memory_space=SM),
            pl.BlockSpec((2 * LANES, 4 * LANES), lambda k: (0, 0)),
        ]
        + ([two, two, two] if planes == FLAT else [two, one, one]),
        out_specs=[ready_spec, two] if planes == FLAT else ready_spec,
        out_shape=[ready_shape, partial_shape] if planes == FLAT else ready_shape,
        scratch_shapes=[
            pltpu.VMEM((2, len(planes), HALVES * COLS, 2 * LANES), bf16),
            pltpu.VMEM((outs, HALVES * COLS, LANES), f32),
            pltpu.VMEM((2, outs, HALVES * COLS, 2 * LANES), bf16),
            pltpu.VMEM((HALVES, count * WIDE, LANES), f32),
        ],
        compiler_params=pltpu.CompilerParams(vmem_limit_bytes=24 * MIB),
        cost_estimate=pl.CostEstimate(flops=10**9, bytes_accessed=4 * 10**6, transcendentals=0),
    )(even, taps, *planes_in)


def row_of(k, p):
    return k * 4 + p if p < 4 else 24 + k * 2 + p - 4


def pick_kernel(cells, flat, slopes, mixed, forces, got_s):
    def one_group(g, slot):
        first = pl.multiple_of(g * GROUP, GROUP)
        for b in range(GROUP):
            d = first + b
            table = table_of(*digits_of(cells[pl.ds(d, 1), :]), 16)
            rows = jnp.concatenate([flat[d], slopes[d]], axis=0)
            got = jnp.dot(rows, table, preferred_element_type=f32)
            got = jnp.concatenate([got[:24] + got[24:48], got[48:64] + got[64:]], axis=0)
            for t in range(4):
                got_s[slot, t, pl.ds(b, 40, stride=SLOT)] = got[:, t * LANES:(t + 1) * LANES]
        for t in range(4):
            lanes = slice(t * LANES, (t + 1) * LANES)
            upper = (cells[pl.ds(first, GROUP), lanes] & 1) == 1
            vs = [mixed[k, pl.ds(first, GROUP), lanes] for k in range(SPECIES)]
            for a in range(3):
                total = None
                for k in range(SPECIES):
                    low, high = (
                        got_s[slot, t, pl.ds(row_of(k, 2 * a + z) * SLOT, GROUP)] for z in range(2)
                    )
                    value = jnp.where(upper, high, low)
                    total = vs[k] * value if total is None else total + vs[k] * value
                forces[a, pl.ds(first, GROUP), lanes] = total

    def four_groups(i, carry):
        for j in range(4):
            one_group(4 * i + j, j)
        return carry

    lax.fori_loop(0, ROWS * COLS // GROUP // 4, four_groups, 0)


def pick(cells, ready, mixed):
    return pl.pallas_call(
        pick_kernel,
        name="pick",
        in_specs=[pl.BlockSpec(memory_space=VM)] * 4,
        out_specs=pl.BlockSpec(memory_space=VM),
        out_shape=jax.ShapeDtypeStruct((3, ROWS * COLS, SLOTS), f32),
        scratch_shapes=[pltpu.VMEM((4, 4, 40 * SLOT, LANES), f32)],
        compiler_params=pltpu.CompilerParams(vmem_limit_bytes=24 * MIB),
        cost_estimate=pl.CostEstimate(flops=6 * 10**9, bytes_accessed=10**7, transcendentals=0),
    )(cells, *ready, mixed)


def body(send_cells, send_species, send_mix, send_counts, chi):
    axes = ("row", "col")
    count = lax.axis_size("row") * lax.axis_size("col")
    swap_a = [(i, i ^ 1) for i in range(count)]
    swap_b = [(i, (i + (1 if i % 2 else -1)) % count) for i in range(count)]
    odd = lax.axis_index("col") % 2
    even = (1 - odd).reshape(1)
    chis = 0.5 * (chi + chi.T) * (1.0 - jnp.eye(SPECIES, dtype=f32))
    mix_matrix = -0.5 * (chis + 1.0)
    cells, species, mix, counts = send_cells[0], send_species[0], send_mix[0], send_counts[0]
    own, sent = deposit(counts, cells, species, mix)
    own = pltpu.with_memory_space_constraint(own, FAR)
    taps = tap_matrices()

    def swap(value, pairs):
        return lax.ppermute(value, axes, pairs)

    near_a = swap(sent, swap_a)
    near_b = swap(sent, swap_b)
    far_a = swap(lax.dynamic_index_in_dim(near_b, 1 - odd, 0, False), swap_a)
    far_b = swap(lax.dynamic_index_in_dim(near_a, odd, 0, False), swap_b)
    flat, partial = smooth(FLAT, even, taps, own, near_a, near_b)
    slopes = smooth(SLOPES, even, taps, partial, far_a, far_b)
    mixed = mixing(counts, mix_matrix, species, mix)
    return pick(cells, (flat, slopes), mixed)[None]


def solution(mesh):
    return jax.shard_map(
        body,
        mesh=mesh,
        in_specs=(
            P(("row", "col"), None, None),
            P(("row", "col"), None, None),
            P(("row", "col"), None, None, None),
            P(("row", "col"), None),
            P(),
        ),
        out_specs=P(("row", "col"), None, None, None),
        check_vma=False,
    )
```

```python
import functools

import jax
import jax.numpy as jnp
import numpy as np
from jax import lax
from jax.experimental import pallas as pl
from jax.experimental.pallas import tpu as pltpu
from jax.sharding import PartitionSpec as P


SPECIES = 6
ROWS = 8
COLS = 16
HALVES = 16
LANES = 128
SLOTS = 512
GROUP = 8
WIDE = COLS + 1
SLOT = GROUP + 1
MIB = 1 << 20
LIMIT = 60

raw_taps = (0.1353352832366127, 0.6065306597126334, 1.0)
tap_total = raw_taps[2] + 2.0 * (raw_taps[0] + raw_taps[1])
T2, T1, T0 = (t / tap_total for t in raw_taps)

f32 = jnp.float32
bf16 = jnp.bfloat16


def digits_of(row):
    wide = jnp.broadcast_to(row, (8, SLOTS))
    low = (wide >> 8) & 15
    ids = lax.broadcasted_iota(jnp.int32, (8, SLOTS), 0)
    inner = jnp.concatenate(
        [jnp.where(low == ids, 1.0, 0.0), jnp.where(low == ids + 8, 1.0, 0.0)], axis=0
    ).astype(bf16)
    high = (wide >> 12).astype(f32)
    return inner, jnp.concatenate([high, high], axis=0).astype(bf16)


def table_of(inner, outer, count):
    none = jnp.zeros((16, SLOTS), bf16)
    return jnp.concatenate(
        [jnp.where(outer == jnp.full((16, SLOTS), i, bf16), inner, none) for i in range(count)], axis=0
    )


def weights_of(limit, t, rows, species, mix):
    part = pl.ds(t * LANES, LANES)
    lane = lax.broadcasted_iota(jnp.int32, (COLS, LANES), 1)
    valid = (lane + t * LANES) < limit
    kind = species[rows, part]
    found = []
    for k in range(SPECIES):
        w = jnp.where(kind == k, 1.0, 0.0) + mix[k, rows, part].astype(f32)
        found.append(jnp.where(valid, w, 0.0).astype(bf16).astype(f32))
    return found


def limits_of(counts, first):
    rows = lax.broadcasted_iota(jnp.int32, (COLS, LANES), 0)
    limit = jnp.zeros((COLS, LANES), jnp.int32)
    for i in range(COLS):
        limit = jnp.where(rows == i, counts[first + i], limit)
    return limit


def deposit_kernel(counts_far, cells_far, species_far, mix_far, own_far, sent_far,
                   counts, cells, species, mix, own, sent, w_s, d_s, sems, out_sems, count_sem):

    def fetches(r):
        rows = pl.ds(pl.multiple_of(r * COLS, COLS), COLS)
        return (
            pltpu.make_async_copy(cells_far.at[rows], cells.at[rows], sems.at[0, r]),
            pltpu.make_async_copy(species_far.at[rows], species.at[rows], sems.at[1, r]),
            pltpu.make_async_copy(mix_far.at[:, rows], mix.at[:, rows], sems.at[2, r]),
        )

    def results(r):
        part = pl.ds(2 * r, 2)
        return [
            pltpu.make_async_copy(near.at[:, :, part], far.at[:, :, part], out_sems.at[i, r])
            for i, (near, far) in enumerate(((sent, sent_far), (own, own_far)))
        ]

    count_copy = pltpu.make_async_copy(counts_far, counts, count_sem)
    count_copy.start()
    for r in range(ROWS):
        for copy in fetches(r):
            copy.start()
    zero = jnp.zeros((COLS, LANES), f32)
    for t in range(4):
        for k in (6, 7):
            w_s[t, k * WIDE:k * WIDE + COLS] = zero
            w_s[t, (8 + k) * WIDE:(8 + k) * WIDE + COLS] = zero

    count_copy.wait()

    def one_row(r, carry):
        for copy in fetches(r):
            copy.wait()
        first = pl.multiple_of(r * COLS, COLS)
        rows = pl.ds(first, COLS)
        limit = limits_of(counts, first)
        for t in range(4):
            upper = (cells[rows, pl.ds(t * LANES, LANES)] & 1) == 1
            for k, w in enumerate(weights_of(limit, t, rows, species, mix)):
                w_s[t, k * WIDE:k * WIDE + COLS] = jnp.where(upper, 0.0, w)
                w_s[t, (8 + k) * WIDE:(8 + k) * WIDE + COLS] = jnp.where(upper, w, 0.0)
        for b in range(COLS):
            inner, outer = digits_of(cells[pl.ds(first + b, 1), :])
            second = outer > 7.5
            table = table_of(inner, jnp.where(second, outer - 8.0, outer), 8)
            w = jnp.concatenate([w_s[t, pl.ds(b, 16, stride=WIDE)] for t in range(4)], axis=1).astype(bf16)
            none = jnp.zeros((16, SLOTS), bf16)
            halves = jnp.concatenate([jnp.where(second, none, w), jnp.where(second, w, none)], axis=0)
            dens = lax.dot_general(halves, table, (((1,), (1,)), ((), ())), preferred_element_type=f32)
            d_s[0, pl.ds(b, 16, stride=WIDE)] = dens[:16]
            d_s[1, pl.ds(b, 16, stride=WIDE)] = dens[16:]
        for z in range(2):
            for k in range(SPECIES):
                for h in range(2):
                    value = d_s[h, (z * 8 + k) * WIDE:(z * 8 + k) * WIDE + COLS]
                    own[z, k, 2 * r + h] = value
                    sent[z, k, 2 * r + h] = value.astype(bf16)
        for copy in results(r):
            copy.start()
        return carry

    lax.fori_loop(0, ROWS, one_row, 0)
    for r in range(ROWS):
        for copy in results(r):
            copy.wait()


VM = pltpu.MemorySpace.VMEM
SM = pltpu.MemorySpace.SMEM
FAR = pltpu.MemorySpace.HBM


def deposit(counts, cells, species, mix):
    half = (HALVES, COLS, LANES)
    return pl.pallas_call(
        deposit_kernel,
        name="deposit",
        in_specs=[pl.BlockSpec(memory_space=FAR)] * 4,
        out_specs=[pl.BlockSpec(memory_space=FAR)] * 2,
        scratch_shapes=[
            pltpu.SMEM((ROWS * COLS,), jnp.int32),
            pltpu.VMEM((ROWS * COLS, SLOTS), jnp.int32),
            pltpu.VMEM((ROWS * COLS, SLOTS), jnp.int32),
            pltpu.VMEM((SPECIES, ROWS * COLS, SLOTS), bf16),
            pltpu.VMEM((2, SPECIES) + half, f32),
            pltpu.VMEM((2, SPECIES) + half, bf16),
            pltpu.VMEM((4, 16 * WIDE, LANES), f32),
            pltpu.VMEM((2, 16 * WIDE, LANES), f32),
            pltpu.SemaphoreType.DMA((3, ROWS)),
            pltpu.SemaphoreType.DMA((2, ROWS)),
            pltpu.SemaphoreType.DMA,
        ],
        out_shape=[jax.ShapeDtypeStruct((2, SPECIES) + half, dtype) for dtype in (f32, bf16)],
        compiler_params=pltpu.CompilerParams(vmem_limit_bytes=LIMIT * MIB),
        cost_estimate=pl.CostEstimate(flops=10**9, bytes_accessed=5 * 10**6, transcendentals=0),
    )(*(pltpu.with_memory_space_constraint(v, FAR) for v in (counts, cells, species, mix)))


def mixing_kernel(counts, mix_matrix, species, mix, mixed):
    def one_row(r, carry):
        first = pl.multiple_of(r * COLS, COLS)
        rows = pl.ds(first, COLS)
        limit = limits_of(counts, first)
        for t in range(4):
            ws = weights_of(limit, t, rows, species, mix)
            for l in range(SPECIES):
                v = mix_matrix[l, 0] * ws[0]
                for k in range(1, SPECIES):
                    v = v + mix_matrix[l, k] * ws[k]
                mixed[l, rows, t * LANES:(t + 1) * LANES] = v
        return carry

    lax.fori_loop(0, ROWS, one_row, 0)


def mixing(counts, mix_matrix, species, mix):
    return pl.pallas_call(
        mixing_kernel,
        name="mixing",
        in_specs=[pl.BlockSpec(memory_space=SM)] * 2 + [pl.BlockSpec(memory_space=VM)] * 2,
        out_specs=pl.BlockSpec(memory_space=VM),
        out_shape=jax.ShapeDtypeStruct((SPECIES, ROWS * COLS, SLOTS), f32),
        compiler_params=pltpu.CompilerParams(vmem_limit_bytes=12 * MIB),
        cost_estimate=pl.CostEstimate(flops=10**9, bytes_accessed=4 * 10**6, transcendentals=0),
    )(counts, mix_matrix, species, mix)


def scaled_taps():
    smooth_scale, slope_scale = 1.6396387, 1.5596421
    smooth_taps = {0: T0, 1: T1, -1: T1, 2: T2, -2: T2}
    slope_taps = {1: 0.5 * (T0 - T2), 2: 0.5 * T1, 3: 0.5 * T2}
    slope_taps.update({-j: -v for j, v in slope_taps.items()})
    return (
        {j: smooth_scale * v for j, v in smooth_taps.items()},
        {j: slope_scale * v for j, v in slope_taps.items()},
        smooth_scale,
        slope_scale,
    )


SMOOTH, SLOPE, SMOOTH_SCALE, SLOPE_SCALE = scaled_taps()


def tap_matrices():
    lane = np.arange(LANES)
    x, y = lane // 16, lane % 16
    results = []
    for main, other, extent in ((y, x, 16), (x, y, 8)):
        source = np.concatenate([main, np.where(main < extent // 2, main + extent, main - extent)])
        same = np.concatenate([other, other])[:, None] == other[None, :]
        gap = source[:, None] - main[None, :]
        for taps in (SMOOTH, SLOPE):
            matrix = np.zeros((2 * LANES, LANES), np.float32)
            for j, value in taps.items():
                matrix += np.where(same & (gap == j), np.float32(value), np.float32(0))
            results.append(matrix)
    return jnp.asarray(np.concatenate(results, axis=1)).astype(bf16)


def split(v):
    top = v.astype(bf16)
    return top, (v - top.astype(f32)).astype(bf16)


def smooth_kernel(planes, even_ref, taps, *refs):
    flat = planes == FLAT
    if flat:
        own, near_a, near_b, ready, partial, x_s, y_s, w_s, g_s = refs
    else:
        partial, far_a, far_b, ready, x_s, y_s, w_s, g_s = refs
    outs = (0, 1, 2, 3) if flat else (4, 5)
    rows_of, count = ROWS_OF[planes]
    k = pl.program_id(0)
    lane = lax.broadcasted_iota(jnp.int32, (COLS, LANES), 1)
    col = lane & 15
    lower = lane.astype(f32).astype(bf16) < 64
    cu = 1.0 / (SMOOTH_SCALE * SLOPE_SCALE)
    cz = 0.5 / (SMOOTH_SCALE * SMOOTH_SCALE)
    even = jnp.full((COLS, LANES), even_ref[0], jnp.int32) == 1
    for h in range(HALVES):
        def sides(a, b):
            a, b = a.astype(f32), b.astype(f32)
            return jnp.where(even, b, a), jnp.where(even, a, b)

        if flat:
            a, r0 = sides(near_a[0, 0, h], near_b[0, 0, h])
            b, r1 = sides(near_a[1, 0, h], near_b[1, 0, h])
            o0 = own[0, 0, h]
            o1 = own[1, 0, h]
            u0 = T2 * (a + r0) + T1 * (b + o1) + T0 * o0
            u1 = T2 * (b + r1) + T1 * (o0 + r0) + T0 * o1
            partial[0, 0, h] = cz * (u1 - (T2 * o1 + T1 * (a + o0) + T0 * b))
            partial[1, 0, h] = cz * ((T2 * o0 + T1 * (o1 + r1) + T0 * r0) - u0)
            values = (cu * u0, cu * u1)
        else:
            l2, r2 = sides(far_a[0, h], far_b[0, h])
            values = (partial[0, 0, h] - (cz * T2) * l2, partial[1, 0, h] + (cz * T2) * r2)
        for i, v in enumerate(values):
            around = jnp.where(col < 8, pltpu.roll(v, COLS - 1, 0), pltpu.roll(v, 1, 0))
            for part, value in ((0, v), (1, around)):
                for level, piece in enumerate(split(value)):
                    x_s[level, i, h * COLS:(h + 1) * COLS, part * LANES:(part + 1) * LANES] = piece
    for i, plane in enumerate(planes):
        table = taps[:, :2 * LANES] if plane < 2 else taps[:, :LANES]
        out = jnp.dot(x_s[0, i], table, preferred_element_type=f32) + jnp.dot(
            x_s[1, i], table, preferred_element_type=f32
        )
        if plane < 2:
            y_s[outs.index(plane)] = out[:, :LANES]
            y_s[outs.index(2 + plane)] = out[:, LANES:]
        else:
            y_s[outs.index(2 + plane)] = out
    for i, p in enumerate(outs):
        pieces = [split(y_s[i, h * COLS:(h + 1) * COLS]) for h in range(HALVES)]
        for h in range(HALVES):
            rows = slice(h * COLS, (h + 1) * COLS)
            for level in range(2):
                w_s[level, i, rows, :LANES] = pieces[h][level]
                w_s[level, i, rows, LANES:] = jnp.where(
                    lower, pieces[(h + 1) % HALVES][level], pieces[(h - 1) % HALVES][level]
                )
        table = taps[:, 3 * LANES:] if p < 2 else taps[:, 2 * LANES:3 * LANES]
        out = jnp.dot(w_s[0, i], table, preferred_element_type=f32) + jnp.dot(
            w_s[1, i], table, preferred_element_type=f32
        )
        for h in range(HALVES):
            g_s[h, pl.ds((k * rows_of + i) * WIDE, COLS)] = out[h * COLS:(h + 1) * COLS]

    if count > rows_of * SPECIES:
        @pl.when(k == 0)
        def _():
            g_s[:, rows_of * SPECIES * WIDE:] = jnp.zeros(
                (HALVES, (count - rows_of * SPECIES) * WIDE, LANES), f32
            )

    @pl.when(k == SPECIES - 1)
    def _():
        def one_row(r, carry):
            for q in range(COLS):
                for h in range(2):
                    value = g_s[2 * r + h, pl.ds(q, count, stride=WIDE)]
                    top = value.astype(bf16).astype(f32)
                    ready[r * COLS + q, :, h * LANES:(h + 1) * LANES] = jnp.concatenate(
                        [top, value - top], axis=0
                    ).astype(bf16)
            return carry

        lax.fori_loop(0, ROWS, one_row, 0)


FLAT = (0, 1)
SLOPES = (2, 3)
ROWS_OF = {FLAT: (4, 24), SLOPES: (2, 16)}


def smooth(planes, even, taps, *planes_in):
    _, count = ROWS_OF[planes]
    half = (HALVES, COLS, LANES)
    outs = 4 if planes == FLAT else 2
    two = pl.BlockSpec((2, 1) + half, lambda k: (0, k, 0, 0, 0))
    one = pl.BlockSpec((1,) + half, lambda k: (k, 0, 0, 0))
    ready_spec = pl.BlockSpec((ROWS * COLS, 2 * count, 2 * LANES), lambda k: (0, 0, 0))
    ready_shape = jax.ShapeDtypeStruct((ROWS * COLS, 2 * count, 2 * LANES), bf16)
    partial_shape = jax.ShapeDtypeStruct((2, SPECIES) + half, f32)
    return pl.pallas_call(
        functools.partial(smooth_kernel, planes),
        name="smooth",
        grid=(SPECIES,),
        in_specs=[
            pl.BlockSpec(memory_space=SM),
            pl.BlockSpec((2 * LANES, 4 * LANES), lambda k: (0, 0)),
        ]
        + ([two, two, two] if planes == FLAT else [two, one, one]),
        out_specs=[ready_spec, two] if planes == FLAT else ready_spec,
        out_shape=[ready_shape, partial_shape] if planes == FLAT else ready_shape,
        scratch_shapes=[
            pltpu.VMEM((2, len(planes), HALVES * COLS, 2 * LANES), bf16),
            pltpu.VMEM((outs, HALVES * COLS, LANES), f32),
            pltpu.VMEM((2, outs, HALVES * COLS, 2 * LANES), bf16),
            pltpu.VMEM((HALVES, count * WIDE, LANES), f32),
        ],
        compiler_params=pltpu.CompilerParams(vmem_limit_bytes=24 * MIB),
        cost_estimate=pl.CostEstimate(flops=10**9, bytes_accessed=4 * 10**6, transcendentals=0),
    )(even, taps, *planes_in)


def row_of(k, p):
    return k * 4 + p if p < 4 else 24 + k * 2 + p - 4


def pick_kernel(cells, flat, slopes, mixed, forces_far, got_s, forces, sems):
    def result(i):
        rows = pl.ds(pl.multiple_of(i * 4 * GROUP, 4 * GROUP), 4 * GROUP)
        return pltpu.make_async_copy(forces.at[:, rows], forces_far.at[:, rows], sems.at[i])

    def one_group(g, slot):
        first = pl.multiple_of(g * GROUP, GROUP)
        for b in range(GROUP):
            d = first + b
            table = table_of(*digits_of(cells[pl.ds(d, 1), :]), 16)
            rows = jnp.concatenate([flat[d], slopes[d]], axis=0)
            got = jnp.dot(rows, table, preferred_element_type=f32)
            got = jnp.concatenate([got[:24] + got[24:48], got[48:64] + got[64:]], axis=0)
            for t in range(4):
                got_s[slot, t, pl.ds(b, 40, stride=SLOT)] = got[:, t * LANES:(t + 1) * LANES]
        for t in range(4):
            lanes = slice(t * LANES, (t + 1) * LANES)
            upper = (cells[pl.ds(first, GROUP), lanes] & 1) == 1
            vs = [mixed[k, pl.ds(first, GROUP), lanes] for k in range(SPECIES)]
            for a in range(3):
                total = None
                for k in range(SPECIES):
                    low, high = (
                        got_s[slot, t, pl.ds(row_of(k, 2 * a + z) * SLOT, GROUP)] for z in range(2)
                    )
                    value = jnp.where(upper, high, low)
                    total = vs[k] * value if total is None else total + vs[k] * value
                forces[a, pl.ds(first, GROUP), lanes] = total

    def four_groups(i, carry):
        for j in range(4):
            one_group(4 * i + j, j)
        result(i).start()
        return carry

    lax.fori_loop(0, ROWS * COLS // GROUP // 4, four_groups, 0)
    for i in range(ROWS * COLS // GROUP // 4):
        result(i).wait()


def pick(cells, ready, mixed):
    return pl.pallas_call(
        pick_kernel,
        name="pick",
        in_specs=[pl.BlockSpec(memory_space=VM)] * 4,
        out_specs=pl.BlockSpec(memory_space=FAR),
        out_shape=jax.ShapeDtypeStruct((3, ROWS * COLS, SLOTS), f32),
        scratch_shapes=[
            pltpu.VMEM((4, 4, 40 * SLOT, LANES), f32),
            pltpu.VMEM((3, ROWS * COLS, SLOTS), f32),
            pltpu.SemaphoreType.DMA((ROWS * COLS // GROUP // 4,)),
        ],
        compiler_params=pltpu.CompilerParams(vmem_limit_bytes=24 * MIB),
        cost_estimate=pl.CostEstimate(flops=6 * 10**9, bytes_accessed=10**7, transcendentals=0),
    )(cells, *ready, mixed)


def body(send_cells, send_species, send_mix, send_counts, chi):
    axes = ("row", "col")
    count = lax.axis_size("row") * lax.axis_size("col")
    swap_a = [(i, i ^ 1) for i in range(count)]
    swap_b = [(i, (i + (1 if i % 2 else -1)) % count) for i in range(count)]
    odd = lax.axis_index("col") % 2
    even = (1 - odd).reshape(1)
    chis = 0.5 * (chi + chi.T) * (1.0 - jnp.eye(SPECIES, dtype=f32))
    mix_matrix = -0.5 * (chis + 1.0)
    cells, species, mix, counts = send_cells[0], send_species[0], send_mix[0], send_counts[0]
    own, sent = deposit(counts, cells, species, mix)
    own = pltpu.with_memory_space_constraint(own, FAR)
    taps = tap_matrices()

    def swap(value, pairs):
        return lax.ppermute(value, axes, pairs)

    near_a = swap(sent, swap_a)
    near_b = swap(sent, swap_b)
    far_a = swap(lax.dynamic_index_in_dim(near_b, 1 - odd, 0, False), swap_a)
    far_b = swap(lax.dynamic_index_in_dim(near_a, odd, 0, False), swap_b)
    flat, partial = smooth(FLAT, even, taps, own, near_a, near_b)
    slopes = smooth(SLOPES, even, taps, partial, far_a, far_b)
    mixed = mixing(counts, mix_matrix, species, mix)
    return pick(cells, (flat, slopes), mixed)[None]


def solution(mesh):
    return jax.shard_map(
        body,
        mesh=mesh,
        in_specs=(
            P(("row", "col"), None, None),
            P(("row", "col"), None, None),
            P(("row", "col"), None, None, None),
            P(("row", "col"), None),
            P(),
        ),
        out_specs=P(("row", "col"), None, None, None),
        check_vma=False,
    )
```
